512 devices in a mesh: exp: 32 (over x_lo, z, core), ccd: 16 (over x_hi, y).
Axes of the slice: x: 4 (x_hi: 2, x_lo: 2; x = x_hi * 2 + x_lo), y: 8, z: 8, core: 2. Of those that a mesh axis runs over, the one named last changes fastest.
Arguments:
- pixels: bfloat16 [32, 16000, 4, 128], P('exp', 'ccd'), may hold values from -24 to 24
- psf_proj: bfloat16 [32, 100, 2160], P('ccd'), may hold values from -0.5 to 0.5
- resolution: float32 [800, 11, 512], P('ccd', None, 'exp'), may hold values from 0.02 to 0.16
- basis: float32 [10, 528], replicated, may hold values from -4 to 4
- sky_fibres: int32 [96], replicated, may hold values from 0 to 799, as said below
- fibre_slot: int32 [800], P('ccd'), may hold values from 0 to 799, as said below
- band_shift: int32 [800], P('ccd'), may hold values from -3 to 3
Outputs:
- sky_subtracted: float32 [32, 800, 512], P(None, 'ccd', 'exp')
- noise_rms: float32 [800, 512], P('ccd', 'exp')
The draws below stay inside these ranges and needn't reach their ends.
Inputs may be any that keep to these rules, and one draw needn't show every extreme that they name: `sky_fibres`: 96 distinct fibre numbers, listed group by group: entries g * 6 to (g + 1) * 6 - 1 are fibres of the group g of 50 consecutive fibres. `fibre_slot`: for each group g of 50 consecutive fibres, a permutation of the slots g * 50 to (g + 1) * 50 - 1.
All inputs are finite; a program needn't handle non-finite values.
Results may differ from the reference program's by a relative error of at most 0.00095.
Values may be sent and summed in bfloat16 or wider, within the bound.
No kernel may reach another device: no remote copies, remote signals or barrier semaphores. Data moves between devices by JAX's collectives and lax.ppermute only.
A program may use at most 64 MiB of HBM per device.

```python
import jax
import jax.numpy as jnp
from jax import lax

FIBBLK = 25
BPIX = 500
MARG = 20
ROWS = 4
COMP = 10
BAND = 11
SHIFT = 3
WAVE = 512
EXPOS = 32
NBLK = 32
COLS = 16000
FIB = 800
FC = 50
GROUPS = 128
SPAN = 540
EXT = 528
SKYC = 6
SKY = 96


def sky_parts(key):
    inner = jax.random.fold_in(key, 17)
    first, second = jax.random.split(inner)
    spectra = jnp.clip(jax.random.normal(first, (COMP, EXT), jnp.float32), -4.0, 4.0)
    weights = jnp.clip(0.6 * jax.random.normal(second, (EXPOS, COMP), jnp.float32), -1.8, 1.8)
    return (spectra, weights)


def draw_basis(key, part):
    return sky_parts(key)[0]


def draw_pixels(key, part):
    spectra, weights = sky_parts(key)
    centre = spectra[:, SHIFT + BAND // 2:SHIFT + BAND // 2 + WAVE]
    glow = jnp.sum(weights[:, :, None] * centre[None, :, :], axis=1)
    glow = glow.reshape(EXPOS, ROWS, GROUPS)[:, None, :, :]
    noise = jnp.clip(jax.random.normal(jax.random.fold_in(key, 29), (EXPOS, COLS, ROWS, GROUPS), jnp.float32), -5.0, 5.0)
    return jnp.clip(noise + glow, -24.0, 24.0).astype(jnp.bfloat16)


def draw_psf_proj(key, part):
    inner = jax.random.fold_in(key, 41)
    spread = jnp.clip(jax.random.normal(inner, (NBLK, FIBBLK * ROWS, SPAN * ROWS), jnp.float32), -5.0, 5.0)
    spread = spread / float(SPAN * ROWS) ** 0.5
    out_row = jnp.arange(FIBBLK * ROWS, dtype=jnp.int32) % ROWS
    in_row = jnp.arange(SPAN * ROWS, dtype=jnp.int32) % ROWS
    level = jnp.where(out_row[:, None] == in_row[None, :], 1.0 / SPAN, 0.0).astype(jnp.float32)
    return (spread + level[None, :, :]).astype(jnp.bfloat16)


def draw_sky_fibres(key, part):
    inner = jax.random.fold_in(key, 53)
    count = FIB // FC
    keys = jax.random.split(inner, count)
    orders = jax.vmap(lambda single: jax.random.permutation(single, FC)[:SKYC])(keys).astype(jnp.int32)
    starts = (jnp.arange(count, dtype=jnp.int32) * FC)[:, None]
    return (orders + starts).reshape(SKY)


def draw_fibre_slot(key, part):
    inner = jax.random.fold_in(key, 67)
    count = FIB // FC
    keys = jax.random.split(inner, count)
    orders = jax.vmap(lambda single: jax.random.permutation(single, FC))(keys).astype(jnp.int32)
    starts = (jnp.arange(count, dtype=jnp.int32) * FC)[:, None]
    return (orders + starts).reshape(FIB)


def set_ends(entries, rng, low, top_value):
    longest = entries.shape.index(max(entries.shape))
    spots = []
    for shift in (0, 1):
        where = [jax.random.randint(jax.random.fold_in(rng, axis), (), 0, length) for axis, length in enumerate(entries.shape)]
        where[longest] = (where[longest] + shift) % entries.shape[longest]
        spots.append(tuple(where))
    return entries.at[spots[0]].set(low).at[spots[1]].set(top_value)


def shard_levels(rng, shape, cuts, least, high):
    level, own = 1.0, jax.random.fold_in(rng, 6)
    for axis_at, parts in cuts:
        steps = jnp.exp(jax.random.uniform(jax.random.fold_in(own, axis_at), (parts,), jnp.float32, least / len(cuts), high / len(cuts)))
        level = level * jnp.repeat(steps, shape[axis_at] // parts).reshape([-1 if axis == axis_at else 1 for axis in range(len(shape))])
    return level


def setup_inputs(seed: int = 0) -> dict:
    key_of = jax.random.split(jax.random.key(seed), 8)
    pixels = draw_pixels(jax.random.fold_in(key_of[7], 71), 0)
    psf_proj = draw_psf_proj(jax.random.fold_in(key_of[7], 71), 0)
    resolution = jnp.clip(0.02 + 0.14 * jax.random.uniform(key_of[2], (FIB, BAND, WAVE), jnp.float32) ** shard_levels(key_of[2], (FIB, BAND, WAVE), ((0, 16), (2, 32)), -0.2, 0.2), 0.02, 0.16)
    basis = draw_basis(jax.random.fold_in(key_of[7], 71), 0)
    sky_fibres = draw_sky_fibres(jax.random.fold_in(key_of[7], 71), 0)
    fibre_slot = draw_fibre_slot(jax.random.fold_in(key_of[7], 71), 0)
    band_shift = set_ends(jax.random.randint(key_of[6], (FIB,), 0 - SHIFT, SHIFT + 1), jax.random.fold_in(key_of[6], 1), 0 - SHIFT, SHIFT).astype(jnp.int32)
    return dict(pixels=pixels, psf_proj=psf_proj, resolution=resolution, basis=basis, sky_fibres=sky_fibres, fibre_slot=fibre_slot, band_shift=band_shift)


def band_model(pieces, spectra, shifts, first):
    length = pieces.shape[2]

    def window_of(shift):
        return lax.dynamic_slice(spectra, (jnp.int32(0), (first + shift + SHIFT).astype(jnp.int32)), (spectra.shape[0], length + BAND - 1))
    windows = jax.vmap(window_of)(shifts)
    total = jnp.zeros((pieces.shape[0], spectra.shape[0], length), jnp.float32)
    for offset in range(BAND):
        total = total + pieces[:, offset, None, :] * windows[:, :, offset:offset + length]
    return total

def solve_small(gram, target):
    factor = jnp.linalg.cholesky(gram)
    return jax.scipy.linalg.cho_solve((factor, True), target[..., None])[..., 0]

def reference(pixels, psf_proj, resolution, basis, sky_fibres, fibre_slot, band_shift):
    exposures = pixels.shape[0]
    padded = jnp.pad(pixels, ((0, 0), (MARG, MARG), (0, 0), (0, 0)))
    proj_square = jnp.square(psf_proj.astype(jnp.float32)).astype(jnp.bfloat16)
    proj_square = lax.optimization_barrier(proj_square)

    def extract(block):
        window = lax.dynamic_slice_in_dim(padded, block * BPIX, SPAN, 1).astype(jnp.float32)
        pixvar = (0.25 + jnp.square(window)).astype(jnp.bfloat16)
        pixvar = lax.optimization_barrier(pixvar).astype(jnp.float32)
        window = window.reshape(exposures, SPAN * ROWS, GROUPS)
        pixvar = pixvar.reshape(exposures, SPAN * ROWS, GROUPS)
        weights = lax.dynamic_index_in_dim(psf_proj, block, 0, keepdims=False).astype(jnp.float32)
        squares = lax.dynamic_index_in_dim(proj_square, block, 0, keepdims=False).astype(jnp.float32)
        flux_block = jnp.einsum('oi,eig->eog', weights, window)
        var_block = jnp.einsum('oi,eig->eog', squares, pixvar)
        return (flux_block, var_block)
    flux_blocks, var_blocks = lax.map(extract, jnp.arange(NBLK, dtype=jnp.int32))

    def arrange(blocks):
        ordered = blocks.reshape(NBLK, exposures, FIBBLK, ROWS, GROUPS).transpose(1, 0, 2, 3, 4)
        return ordered.reshape(exposures, FIB, WAVE)[:, fibre_slot, :]
    flux = arrange(flux_blocks)
    variance = arrange(var_blocks)
    model = band_model(resolution, basis, band_shift, 0)
    skymask = jnp.any(jnp.arange(FIB, dtype=jnp.int32)[:, None] == sky_fibres[None, :], axis=1).astype(jnp.float32)
    highest = lax.Precision.HIGHEST

    def normal_eqs(pair):
        flux_one, var_one = pair
        weight = skymask[:, None] / var_one
        weighted = model * weight[:, None, :]
        gram = jnp.einsum('fkw,flw->kl', weighted, model, precision=highest)
        target = jnp.einsum('fkw,fw->k', weighted, flux_one, precision=highest)
        return (gram, target)
    grams, targets = lax.map(normal_eqs, (flux, variance))
    coeffs = solve_small(grams, targets)

    def subtract(pair):
        flux_one, coeff_one = pair
        return flux_one - jnp.einsum('k,fkw->fw', coeff_one, model, precision=highest)
    sky_subtracted = lax.map(subtract, (flux, coeffs))
    centred = sky_subtracted - lax.optimization_barrier(jnp.mean(sky_subtracted, axis=0))
    noise_rms = jnp.sqrt(lax.optimization_barrier(jnp.mean(jnp.square(centred), axis=0)) + 1e-06)
    return (sky_subtracted, noise_rms)
```

```python
import jax
import jax.numpy as jnp
from jax import lax
from jax.experimental import pallas as pl
from jax.experimental.pallas import tpu as pltpu
from jax.sharding import PartitionSpec as P

BPIX = 500
MARG = 20
ROWS = 4
COMP = 10
BAND = 11
SHIFT = 3
FIBBLK = 25
FC = 50
SPAN = 540
SKYC = 6
EXPOS = 32
CHUNK = 16
GROUPS = 128
LANES = 128
HALF = 64
SUB = 8
TAPS = BAND + 2 * SHIFT
EDGE = MARG * ROWS
DEPTH = SPAN * ROWS
LOCAL = 2 * BPIX * ROWS


f32 = jnp.float32
highest = lax.Precision.HIGHEST


def lanes_of(shape=(SUB, LANES), dim=1):
    return lax.broadcasted_iota(jnp.int32, shape, dim)


def sky_index(lane):
    within = lane & (HALF - 1)
    fibre = jnp.zeros_like(within)
    for i in range(1, SKYC):
        fibre = fibre + jnp.where(within >= i * COMP, 1, 0)
    comp = within - fibre * COMP
    valid = within < SKYC * COMP
    return fibre, comp, valid


def pick(x, idx):
    return jnp.take_along_axis(x, idx, axis=1, mode="promise_in_bounds")


def by_sky(fibre, values):
    out = jnp.zeros_like(fibre)
    for i, value in enumerate(values):
        out = jnp.where(fibre == i, value, out)
    return out


def doubled(row_ref, scratch):
    scratch[...] = jnp.zeros((SUB, LANES), jnp.int32)
    row = row_ref[...]
    scratch[0:1, 0:FC] = row
    scratch[0:1, HALF : HALF + FC] = row
    return jnp.broadcast_to(scratch[0:1, :], (SUB, LANES))


def model_kernel(pos_ref, sky_ref, res_ref, basis_ref, shift_ref, send_ref, model_ref, res_s, basis_s, row_s, turned_s):
    exp_at = pos_ref[0]
    ccd_at = pos_ref[1]
    lane = lanes_of()
    shift = doubled(shift_ref, row_s) + SHIFT
    res_s[...] = jnp.zeros((BAND, SUB, LANES), f32)
    for d in range(BAND):
        res_s[d, :, 0:FC] = res_ref[d, 0:SUB, :]
        res_s[d, :, HALF : HALF + FC] = res_ref[d, SUB:CHUNK, :]
    bands = [res_s[d] for d in range(BAND)]
    masks = [shift == s for s in range(2 * SHIFT + 1)]
    basis_s[...] = jnp.zeros((16, 640), f32)
    basis_s[0:COMP, 0:528] = basis_ref[...]
    tile = exp_at // 8
    offset = CHUNK * (exp_at % 8)
    near = basis_s[:, pl.ds(pl.multiple_of(tile * LANES, LANES), LANES)]
    far = basis_s[:, pl.ds(pl.multiple_of(tile * LANES + LANES, LANES), LANES)]
    turn = (LANES - offset) % LANES
    wide = lanes_of((16, LANES))
    window = jnp.where(wide < LANES - offset, pltpu.roll(near, turn, 1), pltpu.roll(far, turn, 1))
    turned = jnp.transpose(jnp.concatenate([window, jnp.zeros((LANES - 16, LANES), f32)], axis=0))
    turned_s[...] = turned[0:32]
    totals = [jnp.zeros((SUB, LANES), f32) for _ in range(COMP)]
    for t in range(TAPS):
        tap = jnp.zeros((SUB, LANES), f32)
        for s in range(2 * SHIFT + 1):
            if 0 <= t - s < BAND:
                tap = jnp.where(masks[s], bands[t - s], tap)
        upper = turned_s[t : t + SUB, :]
        lower = turned_s[t + SUB : t + 2 * SUB, :]
        both = jnp.where(lane < HALF, upper, pltpu.roll(lower, HALF, 1))
        for k in range(COMP):
            totals[k] = totals[k] + tap * pick(both, (lane & HALF) + k)
    for k in range(COMP):
        model_ref[k] = totals[k]
    fibre, comp, valid = sky_index(lane)
    sky = by_sky(fibre, [sky_ref[ccd_at * SKYC + i] - ccd_at * FC for i in range(SKYC)])
    source = (lane & HALF) + sky
    out = jnp.zeros((SUB, LANES), f32)
    for k in range(COMP):
        out = jnp.where((comp == k) & valid, pick(totals[k], source), out)
    send_ref[...] = jnp.broadcast_to(out[None], (EXPOS, SUB, LANES))


def extract_kernel(pos_ref, sky_ref, slots_ref, pix_ref, before_ref, after_ref, psf_ref, slot_ref, flux_ref, weight_ref, skyflux_ref, pix_s, var_s, pad_s, flux_s, vari_s, row_s):
    ccd_at = pos_ref[1]
    base = ccd_at * FC
    lane = lanes_of()
    pix_s[0:EDGE, :] = before_ref[...]
    pix_s[EDGE : EDGE + LOCAL, :] = pix_ref[...]
    pix_s[EDGE + LOCAL : 2 * EDGE + LOCAL, :] = after_ref[...]
    var_s[...] = (0.25 + jnp.square(pix_s[...].astype(f32))).astype(jnp.bfloat16)
    pad_s[...] = jnp.zeros((LANES, LANES), f32)
    for b in range(2):
        lower = b * BPIX * ROWS
        psf = psf_ref[b]
        pad_s[0:100, :] = jnp.dot(psf, pix_s[lower : lower + DEPTH, :], preferred_element_type=f32)
        flux_s[b] = jnp.transpose(pad_s[...])
        square = jnp.square(psf.astype(f32)).astype(jnp.bfloat16)
        pad_s[0:100, :] = jnp.dot(square, var_s[lower : lower + DEPTH, :], preferred_element_type=f32)
        vari_s[b] = jnp.transpose(pad_s[...])
    slot = doubled(slot_ref, row_s)
    used = (lane & (HALF - 1)) < FC
    slot = jnp.where(used, slot - base, 0)
    second = slot >= FIBBLK
    place = jnp.where(second, slot - FIBBLK, slot) * ROWS
    fibre, _, valid = sky_index(lane)
    local = [sky_ref[ccd_at * SKYC + i] - base for i in range(SKYC)]
    sky = (lane & HALF) + by_sky(fibre, local)
    sky_slot = by_sky(fibre, [slots_ref[f] - base for f in local])
    sky_second = sky_slot >= FIBBLK
    sky_place = jnp.where(sky_second, sky_slot - FIBBLK, sky_slot) * ROWS

    def gathered(ref, row, spot, late):
        upper = jnp.where(late, pick(ref[1, row : row + SUB, :], spot), pick(ref[0, row : row + SUB, :], spot))
        row = row + SUB
        lower = jnp.where(late, pick(ref[1, row : row + SUB, :], spot), pick(ref[0, row : row + SUB, :], spot))
        return jnp.where(lane < HALF, upper, lower)

    for r in range(ROWS):
        for m in range(GROUPS // CHUNK):
            flux = jnp.where(used, gathered(flux_s, m * CHUNK, place + r, second), 0.0)
            flux_ref[r * 8 + m] = flux
            skyflux_ref[r * 8 + m] = jnp.where(valid, pick(flux, sky), 0.0)
            vari = gathered(vari_s, m * CHUNK, sky_place + r, sky_second)
            weight_ref[r * 8 + m] = jnp.where(valid, 1.0 / vari, 0.0)


def gram_kernel(model_ref, weight_ref, flux_ref, out_ref):
    model = model_ref[...].reshape(EXPOS * SUB, LANES)
    weighted = model * weight_ref[...].reshape(EXPOS * SUB, LANES)
    target = jnp.sum(weighted * flux_ref[...].reshape(EXPOS * SUB, LANES), axis=0, keepdims=True)
    square = lax.dot_general(weighted, model, (((0,), (0,)), ((), ())), precision=highest, preferred_element_type=f32)
    shape = (LANES, LANES)
    fibre_r, comp_r, valid_r = sky_index(lanes_of(shape, 0))
    row, col = lanes_of(shape, 0), lanes_of(shape, 1)
    fibre_c, comp_c, valid_c = sky_index(col)
    same = (fibre_r == fibre_c) & ((row & HALF) == (col & HALF)) & valid_r & valid_c
    square = jnp.where(same, square, 0.0)
    select = jnp.where((row == comp_c) & valid_c, 1.0, 0.0)
    half = jnp.dot(select[0:16], square, precision=highest, preferred_element_type=f32)
    half = jnp.where(row[0:16] == COMP, target, half)
    full = lax.dot_general(half, select, (((1,), (1,)), ((), ())), precision=highest, preferred_element_type=f32)
    tile = full[0:SUB] + pltpu.roll(full[SUB : 2 * SUB], HALF, 1)
    out_ref[...] = jnp.broadcast_to(tile[None], out_ref.shape)


def solve_kernel(parts_ref, flux_ref, out_ref):
    total = jnp.sum(parts_ref[...], axis=0)
    system = jnp.concatenate([total, pltpu.roll(total, HALF, 1)], axis=0)
    col = lanes_of((16, LANES))
    row = lanes_of((16, LANES), 0)
    system = jnp.where((col < COMP) & (row <= COMP), system, 0.0)
    for k in range(COMP):
        column = pick(system, jnp.full((16, LANES), k, jnp.int32))
        line = system[k : k + 1, :]
        pivot = column[k : k + 1, :]
        unit = jnp.where(col[0:1] == k, 1.0, 0.0)
        system = system - column * ((line - unit) / pivot)
    coeffs = jnp.broadcast_to(system[COMP : COMP + 1, :], (SUB, LANES))
    coeffs = pltpu.roll(coeffs, FC, 1)
    lane = lanes_of()
    here = (lane >= FC) & (lane < FC + COMP)
    for e in range(EXPOS):
        out_ref[e] = jnp.where(here, coeffs, flux_ref[e])


def subtract_kernel(flux_ref, model_ref, out_ref, noise_ref, left_s):
    models = [model_ref[k] for k in range(COMP)]
    spots = [jnp.full((SUB, LANES), FC + k, jnp.int32) for k in range(COMP)]
    total = jnp.zeros((SUB, LANES), f32)
    for e in range(EXPOS):
        left = flux_ref[e]
        sky = pick(left, spots[0]) * models[0]
        for k in range(1, COMP):
            sky = sky + pick(left, spots[k]) * models[k]
        left = left - sky
        left_s[e] = left
        total = total + left
        out_ref[e, 0:SUB, :] = left[:, 0:FC]
        out_ref[e, SUB:CHUNK, :] = pltpu.roll(left, HALF, 1)[:, 0:FC]
    mean = total * (1.0 / EXPOS)
    spread = jnp.zeros((SUB, LANES), f32)
    for e in range(EXPOS):
        spread = spread + jnp.square(left_s[e] - mean)
    noise = jnp.sqrt(spread * (1.0 / EXPOS) + 1e-06)
    noise_ref[0:SUB, :] = noise[:, 0:FC]
    noise_ref[SUB:CHUNK, :] = pltpu.roll(noise, HALF, 1)[:, 0:FC]


VMEM = pl.BlockSpec(memory_space=pltpu.VMEM)
SMEM = pl.BlockSpec(memory_space=pltpu.SMEM)
TILES = jax.ShapeDtypeStruct((EXPOS, SUB, LANES), f32)
PARAMS = pltpu.CompilerParams(vmem_limit_bytes=40 * 1024 * 1024)


def local_model(pos, sky_fibres, resolution, basis, band_shift):
    return pl.pallas_call(
        model_kernel,
        out_shape=(TILES, jax.ShapeDtypeStruct((COMP, SUB, LANES), f32)),
        in_specs=[SMEM, SMEM, VMEM, VMEM, VMEM],
        out_specs=(VMEM, VMEM),
        scratch_shapes=[
            pltpu.VMEM((BAND, SUB, LANES), f32),
            pltpu.VMEM((16, 640), f32),
            pltpu.VMEM((SUB, LANES), jnp.int32),
            pltpu.VMEM((32, LANES), f32),
        ],
        compiler_params=PARAMS,
        name="model",
    )(pos, sky_fibres, resolution.transpose(1, 2, 0), basis, band_shift.reshape(1, FC))


def extract(pos, sky_fibres, fibre_slot, pixels, before, after, psf):
    return pl.pallas_call(
        extract_kernel,
        out_shape=(TILES, TILES, TILES),
        in_specs=[SMEM, SMEM, SMEM, VMEM, VMEM, VMEM, VMEM, VMEM],
        out_specs=(VMEM, VMEM, VMEM),
        scratch_shapes=[
            pltpu.VMEM((2 * EDGE + LOCAL, LANES), jnp.bfloat16),
            pltpu.VMEM((2 * EDGE + LOCAL, LANES), jnp.bfloat16),
            pltpu.VMEM((LANES, LANES), f32),
            pltpu.VMEM((2, LANES, LANES), f32),
            pltpu.VMEM((2, LANES, LANES), f32),
            pltpu.VMEM((SUB, LANES), jnp.int32),
        ],
        compiler_params=PARAMS,
        name="extract",
    )(pos, sky_fibres, fibre_slot, pixels, before, after, psf, fibre_slot.reshape(1, FC))


def gram_parts(model, weight, flux, copies):
    return pl.pallas_call(
        gram_kernel,
        out_shape=jax.ShapeDtypeStruct((copies, SUB, LANES), f32),
        in_specs=[VMEM, VMEM, VMEM],
        out_specs=VMEM,
        compiler_params=PARAMS,
        name="gram",
    )(model, weight, flux)


def solve(parts, flux):
    return pl.pallas_call(
        solve_kernel, out_shape=TILES, in_specs=[VMEM, VMEM], out_specs=VMEM, compiler_params=PARAMS, name="solve"
    )(parts, flux)


def subtract(flux, model):
    return pl.pallas_call(
        subtract_kernel,
        out_shape=(jax.ShapeDtypeStruct((EXPOS, CHUNK, FC), f32), jax.ShapeDtypeStruct((CHUNK, FC), f32)),
        in_specs=[VMEM, VMEM],
        out_specs=(VMEM, VMEM),
        scratch_shapes=[pltpu.VMEM((EXPOS, SUB, LANES), f32)],
        compiler_params=PARAMS,
        name="subtract",
    )(flux, model)


def shards(pixels, psf_proj, resolution, basis, sky_fibres, fibre_slot, band_shift):
    size = lax.axis_size("ccd")
    rows = pixels.reshape(LOCAL, GROUPS)
    up = [(i, i + 1) for i in range(size - 1)]
    down = [(j, i) for i, j in up]
    before = lax.ppermute(rows[LOCAL - EDGE :], "ccd", up)
    after = lax.ppermute(rows[:EDGE], "ccd", down)
    pos = jnp.stack([lax.axis_index("exp"), lax.axis_index("ccd")]).astype(jnp.int32)
    send, model = local_model(pos, sky_fibres, resolution, basis, band_shift)
    sky_model = lax.all_to_all(send, "exp", split_axis=0, concat_axis=0, tiled=True)
    flux, weight, sky_flux = extract(pos, sky_fibres, fibre_slot, rows, before, after, psf_proj)
    parts = gram_parts(sky_model, weight, sky_flux, size)
    parts = lax.all_to_all(parts, "ccd", split_axis=0, concat_axis=0, tiled=True)
    flux = solve(parts, flux)
    flux = lax.all_to_all(flux, "exp", split_axis=0, concat_axis=0, tiled=True)
    sky_subtracted, noise_rms = subtract(flux, model)
    return (sky_subtracted.transpose(0, 2, 1), noise_rms.transpose(1, 0))


def solution(mesh):
    in_specs = (
        P("exp", "ccd", None, None),
        P("ccd", None, None),
        P("ccd", None, "exp"),
        P(),
        P(),
        P("ccd"),
        P("ccd"),
    )
    out_specs = (P(None, "ccd", "exp"), P("ccd", "exp"))
    return jax.shard_map(shards, mesh=mesh, in_specs=in_specs, out_specs=out_specs, check_vma=False)
```

```python
import jax
import jax.numpy as jnp
from jax import lax
from jax.experimental import pallas as pl
from jax.experimental.pallas import tpu as pltpu
from jax.sharding import PartitionSpec as P

BPIX = 500
MARG = 20
ROWS = 4
COMP = 10
BAND = 11
SHIFT = 3
FIBBLK = 25
FC = 50
SPAN = 540
SKYC = 6
EXPOS = 32
PIECE = 8
CHUNK = 16
GROUPS = 128
LANES = 128
HALF = 64
SUB = 8
TAPS = BAND + 2 * SHIFT
EDGE = MARG * ROWS
DEPTH = SPAN * ROWS
LOCAL = 2 * BPIX * ROWS


f32 = jnp.float32
highest = lax.Precision.HIGHEST


def lanes_of(shape=(SUB, LANES), dim=1):
    return lax.broadcasted_iota(jnp.int32, shape, dim)


def sky_index(lane):
    within = lane & (HALF - 1)
    fibre = jnp.zeros_like(within)
    for i in range(1, SKYC):
        fibre = fibre + jnp.where(within >= i * COMP, 1, 0)
    comp = within - fibre * COMP
    valid = within < SKYC * COMP
    return fibre, comp, valid


def pick(x, idx):
    return jnp.take_along_axis(x, idx, axis=1, mode="promise_in_bounds")


def doubled(row, scratch):
    scratch[...] = jnp.zeros((SUB, LANES), jnp.int32)
    scratch[0:1, 0:FC] = row
    scratch[0:1, HALF : HALF + FC] = row
    return jnp.broadcast_to(scratch[0:1, :], (SUB, LANES))


def sky_lanes(row, scratch, ccd_at, fibre):
    scratch[...] = jnp.zeros((SUB, LANES), jnp.int32)
    scratch[0:1, 0 : row.shape[1]] = row
    listed = jnp.broadcast_to(scratch[0:1, :], (SUB, LANES))
    return (lanes_of() & HALF) + pick(listed, fibre + ccd_at * SKYC) - ccd_at * FC


def banded(res_ref, res_s):
    res_s[...] = jnp.zeros((BAND, SUB, LANES), f32)
    for d in range(BAND):
        res_s[d, :, 0:FC] = res_ref[d, 0:SUB, :]
        res_s[d, :, HALF : HALF + FC] = res_ref[d, SUB:CHUNK, :]
    return [res_s[d] for d in range(BAND)]


def turned_basis(basis_ref, basis_s, turned_s, exp_at):
    basis_s[...] = jnp.zeros((16, 640), f32)
    basis_s[0:COMP, 0:528] = basis_ref[...]
    tile = exp_at // 8
    offset = CHUNK * (exp_at % 8)
    near = basis_s[:, pl.ds(pl.multiple_of(tile * LANES, LANES), LANES)]
    far = basis_s[:, pl.ds(pl.multiple_of(tile * LANES + LANES, LANES), LANES)]
    turn = (LANES - offset) % LANES
    wide = lanes_of((16, LANES))
    window = jnp.where(wide < LANES - offset, pltpu.roll(near, turn, 1), pltpu.roll(far, turn, 1))
    turned_s[...] = jnp.transpose(jnp.concatenate([window, jnp.zeros((LANES - 16, LANES), f32)], axis=0))[0:32]


def tap_of(t, bands, masks):
    tap = jnp.zeros((SUB, LANES), f32)
    for s in range(2 * SHIFT + 1):
        if 0 <= t - s < BAND:
            tap = jnp.where(masks[s], bands[t - s], tap)
    return tap


def basis_at(t, turned_s):
    upper = turned_s[t : t + SUB, :]
    lower = turned_s[t + SUB : t + 2 * SUB, :]
    return jnp.where(lanes_of() < HALF, upper, pltpu.roll(lower, HALF, 1))


def model_copies(res_h, basis_h, shift_h, res_v, basis_v, shift_v, sems):
    copies = [
        pltpu.make_async_copy(source, target, sems.at[i])
        for i, (source, target) in enumerate(((res_h, res_v), (basis_h, basis_v), (shift_h, shift_v)))
    ]
    for copy in copies:
        copy.start()
    return copies


def sky_kernel(res_h, basis_h, shift_h, sky_h, pix_h, send_ref, first_ref, last_ref, res_v, basis_v, shift_v, sky_v, res_s, basis_s, row_s, turned_s, sems):
    exp_at = lax.axis_index("exp")
    ccd_at = lax.axis_index("ccd")
    edges = [
        pltpu.make_async_copy(pix_h.at[0:EDGE, :], first_ref, sems.at[4]),
        pltpu.make_async_copy(pix_h.at[LOCAL - EDGE : LOCAL, :], last_ref, sems.at[5]),
    ]
    for edge in edges:
        edge.start()
    copies = model_copies(res_h, basis_h, shift_h, res_v, basis_v, shift_v, sems)
    listed = pltpu.make_async_copy(sky_h, sky_v, sems.at[3])
    listed.start()
    listed.wait()
    for copy in copies:
        copy.wait()
    lane = lanes_of()
    fibre, comp, valid = sky_index(lane)
    sky = sky_lanes(sky_v[...], row_s, ccd_at, fibre)
    shift = pick(doubled(shift_v[...], row_s), sky) + SHIFT
    masks = [shift == s for s in range(2 * SHIFT + 1)]
    bands = [pick(band, sky) for band in banded(res_v, res_s)]
    turned_basis(basis_v, basis_s, turned_s, exp_at)
    total = jnp.zeros((SUB, LANES), f32)
    for t in range(TAPS):
        total = total + tap_of(t, bands, masks) * pick(basis_at(t, turned_s), (lane & HALF) + comp)
    total = jnp.where(valid, total, 0.0)
    send_ref[...] = jnp.broadcast_to(total[None], (EXPOS, SUB, LANES))
    for edge in edges:
        edge.wait()


def model_kernel(res_h, basis_h, shift_h, model_ref, res_v, basis_v, shift_v, res_s, basis_s, row_s, turned_s, sems):
    exp_at = lax.axis_index("exp")
    for copy in model_copies(res_h, basis_h, shift_h, res_v, basis_v, shift_v, sems):
        copy.wait()
    lane = lanes_of()
    shift = doubled(shift_v[...], row_s) + SHIFT
    masks = [shift == s for s in range(2 * SHIFT + 1)]
    bands = banded(res_v, res_s)
    turned_basis(basis_v, basis_s, turned_s, exp_at)
    totals = [jnp.zeros((SUB, LANES), f32) for _ in range(COMP)]
    for t in range(TAPS):
        tap = tap_of(t, bands, masks)
        both = basis_at(t, turned_s)
        for k in range(COMP):
            totals[k] = totals[k] + tap * pick(both, (lane & HALF) + k)
    for k in range(COMP):
        model_ref[k] = totals[k]


def extract_kernel(sky_h, slot_h, pix_ref, before_ref, after_ref, psf_ref, flux_ref, weight_ref, skyflux_ref, sky_v, slot_v, pix_s, var_s, pad_s, flux_s, vari_s, row_s, sems):
    ccd_at = lax.axis_index("ccd")
    base = ccd_at * FC
    lane = lanes_of()
    listed = pltpu.make_async_copy(sky_h, sky_v, sems.at[0])
    slotted = pltpu.make_async_copy(slot_h, slot_v, sems.at[1])
    listed.start()
    slotted.start()
    pix_s[0:EDGE, :] = before_ref[...]
    pix_s[EDGE : EDGE + LOCAL, :] = pix_ref[...]
    pix_s[EDGE + LOCAL : 2 * EDGE + LOCAL, :] = after_ref[...]
    var_s[...] = (0.25 + jnp.square(pix_s[...].astype(f32))).astype(jnp.bfloat16)
    pad_s[...] = jnp.zeros((LANES, LANES), f32)
    for b in range(2):
        lower = b * BPIX * ROWS
        psf = psf_ref[b]
        pad_s[0:100, :] = jnp.dot(psf, pix_s[lower : lower + DEPTH, :], preferred_element_type=f32)
        flux_s[b] = jnp.transpose(pad_s[...])
        square = jnp.square(psf.astype(f32)).astype(jnp.bfloat16)
        pad_s[0:100, :] = jnp.dot(square, var_s[lower : lower + DEPTH, :], preferred_element_type=f32)
        vari_s[b] = jnp.transpose(pad_s[...])
    listed.wait()
    slotted.wait()
    fibre, _, valid = sky_index(lane)
    sky = sky_lanes(sky_v[...], row_s, ccd_at, fibre)
    slot = doubled(slot_v[...], row_s)
    used = (lane & (HALF - 1)) < FC
    slot = jnp.where(used, slot - base, 0)
    second = slot >= FIBBLK
    place = jnp.where(second, slot - FIBBLK, slot) * ROWS
    sky_slot = pick(slot, sky)
    sky_second = sky_slot >= FIBBLK
    sky_place = jnp.where(sky_second, sky_slot - FIBBLK, sky_slot) * ROWS

    def gathered(ref, row, spot, late):
        upper = jnp.where(late, pick(ref[1, row : row + SUB, :], spot), pick(ref[0, row : row + SUB, :], spot))
        row = row + SUB
        lower = jnp.where(late, pick(ref[1, row : row + SUB, :], spot), pick(ref[0, row : row + SUB, :], spot))
        return jnp.where(lane < HALF, upper, lower)

    for r in range(ROWS):
        for m in range(GROUPS // CHUNK):
            flux = jnp.where(used, gathered(flux_s, m * CHUNK, place + r, second), 0.0)
            flux_ref[r * 8 + m] = flux
            skyflux_ref[r * 8 + m] = jnp.where(valid, pick(flux, sky), 0.0)
            vari = gathered(vari_s, m * CHUNK, sky_place + r, sky_second)
            weight_ref[r * 8 + m] = jnp.where(valid, 1.0 / vari, 0.0)


def gram_kernel(model_ref, weight_ref, flux_ref, out_ref):
    model = model_ref[...].reshape(EXPOS * SUB, LANES)
    weighted = model * weight_ref[...].reshape(EXPOS * SUB, LANES)
    target = jnp.sum(weighted * flux_ref[...].reshape(EXPOS * SUB, LANES), axis=0, keepdims=True)
    square = lax.dot_general(weighted, model, (((0,), (0,)), ((), ())), precision=highest, preferred_element_type=f32)
    shape = (LANES, LANES)
    fibre_r, comp_r, valid_r = sky_index(lanes_of(shape, 0))
    row, col = lanes_of(shape, 0), lanes_of(shape, 1)
    fibre_c, comp_c, valid_c = sky_index(col)
    same = (fibre_r == fibre_c) & ((row & HALF) == (col & HALF)) & valid_r & valid_c
    square = jnp.where(same, square, 0.0)
    select = jnp.where((row == comp_c) & valid_c, 1.0, 0.0)
    half = jnp.dot(select[0:16], square, precision=highest, preferred_element_type=f32)
    half = jnp.where(row[0:16] == COMP, target, half)
    full = lax.dot_general(half, select, (((1,), (1,)), ((), ())), precision=highest, preferred_element_type=f32)
    tile = full[0:SUB] + pltpu.roll(full[SUB : 2 * SUB], HALF, 1)
    out_ref[...] = jnp.broadcast_to(tile[None], out_ref.shape)


def solve_kernel(parts_ref, flux_ref, out_ref):
    total = jnp.sum(parts_ref[...], axis=0)
    system = jnp.concatenate([total, pltpu.roll(total, HALF, 1)], axis=0)
    col = lanes_of((16, LANES))
    row = lanes_of((16, LANES), 0)
    system = jnp.where((col < COMP) & (row <= COMP), system, 0.0)
    for k in range(COMP):
        column = pick(system, jnp.full((16, LANES), k, jnp.int32))
        line = system[k : k + 1, :]
        pivot = column[k : k + 1, :]
        unit = jnp.where(col[0:1] == k, 1.0, 0.0)
        system = system - column * ((line - unit) / pivot)
    coeffs = jnp.broadcast_to(system[COMP : COMP + 1, :], (SUB, LANES))
    coeffs = pltpu.roll(coeffs, FC, 1)
    lane = lanes_of()
    here = (lane >= FC) & (lane < FC + COMP)
    for e in range(EXPOS):
        out_ref[e] = jnp.where(here, coeffs, flux_ref[e])


def subtract_kernel(flux_ref, model_ref, out_h, noise_ref, left_s, out_s, sems):
    models = [model_ref[k] for k in range(COMP)]
    spots = [jnp.full((SUB, LANES), FC + k, jnp.int32) for k in range(COMP)]
    total = jnp.zeros((SUB, LANES), f32)
    copies = []
    for e in range(EXPOS):
        left = flux_ref[e]
        sky = pick(left, spots[0]) * models[0]
        for k in range(1, COMP):
            sky = sky + pick(left, spots[k]) * models[k]
        left = left - sky
        left_s[e] = left
        total = total + left
        out_s[e, 0:SUB, :] = left[:, 0:FC]
        out_s[e, SUB:CHUNK, :] = pltpu.roll(left, HALF, 1)[:, 0:FC]
        if e % PIECE == PIECE - 1:
            at = pl.ds(e + 1 - PIECE, PIECE)
            copies.append(pltpu.make_async_copy(out_s.at[at], out_h.at[at], sems.at[e // PIECE]))
            copies[-1].start()
    mean = total * (1.0 / EXPOS)
    spread = jnp.zeros((SUB, LANES), f32)
    for e in range(EXPOS):
        spread = spread + jnp.square(left_s[e] - mean)
    noise = jnp.sqrt(spread * (1.0 / EXPOS) + 1e-06)
    noise_ref[0:SUB, :] = noise[:, 0:FC]
    noise_ref[SUB:CHUNK, :] = pltpu.roll(noise, HALF, 1)[:, 0:FC]
    for copy in copies:
        copy.wait()


VMEM = pl.BlockSpec(memory_space=pltpu.VMEM)
HBM = pl.BlockSpec(memory_space=pltpu.HBM)
TILES = jax.ShapeDtypeStruct((EXPOS, SUB, LANES), f32)
EDGES = jax.ShapeDtypeStruct((EDGE, GROUPS), jnp.bfloat16)
PARAMS = pltpu.CompilerParams(vmem_limit_bytes=40 * 1024 * 1024)
MODEL_INPUTS = [pltpu.VMEM((BAND, CHUNK, FC), f32), pltpu.VMEM((COMP, 528), f32), pltpu.VMEM((1, FC), jnp.int32)]
MODEL_SCRATCH = [
    pltpu.VMEM((BAND, SUB, LANES), f32),
    pltpu.VMEM((16, 640), f32),
    pltpu.VMEM((SUB, LANES), jnp.int32),
    pltpu.VMEM((32, LANES), f32),
]


def sky_model(resolution, basis, shift, sky, pixels):
    return pl.pallas_call(
        sky_kernel,
        out_shape=(TILES, EDGES, EDGES),
        in_specs=[HBM] * 5,
        out_specs=(VMEM, VMEM, VMEM),
        scratch_shapes=MODEL_INPUTS + [pltpu.VMEM((1, 96), jnp.int32)] + MODEL_SCRATCH + [pltpu.SemaphoreType.DMA((6,))],
        compiler_params=PARAMS,
        name="sky_model",
    )(*(pltpu.with_memory_space_constraint(v, pltpu.HBM) for v in (resolution, basis, shift, sky, pixels)))


def local_model(resolution, basis, shift):
    return pl.pallas_call(
        model_kernel,
        out_shape=jax.ShapeDtypeStruct((COMP, SUB, LANES), f32),
        in_specs=[HBM] * 3,
        out_specs=VMEM,
        scratch_shapes=MODEL_INPUTS + MODEL_SCRATCH + [pltpu.SemaphoreType.DMA((3,))],
        compiler_params=PARAMS,
        name="local_model",
    )(*(pltpu.with_memory_space_constraint(v, pltpu.HBM) for v in (resolution, basis, shift)))


def extract(sky, slot, pixels, before, after, psf):
    return pl.pallas_call(
        extract_kernel,
        out_shape=(TILES, TILES, TILES),
        in_specs=[HBM, HBM, VMEM, VMEM, VMEM, VMEM],
        out_specs=(VMEM, VMEM, VMEM),
        scratch_shapes=[
            pltpu.VMEM((1, 96), jnp.int32),
            pltpu.VMEM((1, FC), jnp.int32),
            pltpu.VMEM((2 * EDGE + LOCAL, LANES), jnp.bfloat16),
            pltpu.VMEM((2 * EDGE + LOCAL, LANES), jnp.bfloat16),
            pltpu.VMEM((LANES, LANES), f32),
            pltpu.VMEM((2, LANES, LANES), f32),
            pltpu.VMEM((2, LANES, LANES), f32),
            pltpu.VMEM((SUB, LANES), jnp.int32),
            pltpu.SemaphoreType.DMA((2,)),
        ],
        compiler_params=PARAMS,
        name="extract",
    )(*(pltpu.with_memory_space_constraint(v, pltpu.HBM) for v in (sky, slot)), pixels, before, after, psf)


def gram_parts(model, weight, flux, copies):
    return pl.pallas_call(
        gram_kernel,
        out_shape=jax.ShapeDtypeStruct((copies, SUB, LANES), f32),
        in_specs=[VMEM, VMEM, VMEM],
        out_specs=VMEM,
        compiler_params=PARAMS,
        name="gram",
    )(model, weight, flux)


def solve(parts, flux):
    return pl.pallas_call(
        solve_kernel, out_shape=TILES, in_specs=[VMEM, VMEM], out_specs=VMEM, compiler_params=PARAMS, name="solve"
    )(parts, flux)


def subtract(flux, model):
    return pl.pallas_call(
        subtract_kernel,
        out_shape=(jax.ShapeDtypeStruct((EXPOS, CHUNK, FC), f32), jax.ShapeDtypeStruct((CHUNK, FC), f32)),
        in_specs=[VMEM, VMEM],
        out_specs=(HBM, VMEM),
        scratch_shapes=[
            pltpu.VMEM((EXPOS, SUB, LANES), f32),
            pltpu.VMEM((EXPOS, CHUNK, FC), f32),
            pltpu.SemaphoreType.DMA((EXPOS // PIECE,)),
        ],
        compiler_params=PARAMS,
        name="subtract",
    )(flux, model)


def shards(pixels, psf_proj, resolution, basis, sky_fibres, fibre_slot, band_shift):
    size = lax.axis_size("ccd")
    rows = pixels.reshape(LOCAL, GROUPS)
    res = resolution.transpose(1, 2, 0)
    sky = sky_fibres.reshape(1, -1)
    slot = fibre_slot.reshape(1, FC)
    shift = band_shift.reshape(1, FC)
    up = [(i, i + 1) for i in range(size - 1)]
    down = [(j, i) for i, j in up]
    send, first, last = sky_model(res, basis, shift, sky, rows)
    before = lax.ppermute(last, "ccd", up)
    after = lax.ppermute(first, "ccd", down)
    model = lax.all_to_all(send, "exp", split_axis=0, concat_axis=0, tiled=True)
    flux, weight, sky_flux = extract(sky, slot, rows, before, after, psf_proj)
    parts = gram_parts(model, weight, sky_flux, size)
    res, parts = lax.optimization_barrier((res, parts))
    parts = lax.all_to_all(parts, "ccd", split_axis=0, concat_axis=0, tiled=True)
    model = local_model(res, basis, shift)
    flux = solve(parts, flux)
    flux = lax.all_to_all(flux, "exp", split_axis=0, concat_axis=0, tiled=True)
    sky_subtracted, noise_rms = subtract(flux, model)
    return (sky_subtracted.transpose(0, 2, 1), noise_rms.transpose(1, 0))


def solution(mesh):
    in_specs = (
        P("exp", "ccd", None, None),
        P("ccd", None, None),
        P("ccd", None, "exp"),
        P(),
        P(),
        P("ccd"),
        P("ccd"),
    )
    out_specs = (P(None, "ccd", "exp"), P("ccd", "exp"))
    return jax.shard_map(shards, mesh=mesh, in_specs=in_specs, out_specs=out_specs, check_vma=False)
```

```python
import jax
import jax.numpy as jnp
from jax import lax
from jax.experimental import pallas as pl
from jax.experimental.pallas import tpu as pltpu
from jax.sharding import PartitionSpec as P

BPIX = 500
MARG = 20
ROWS = 4
COMP = 10
BAND = 11
SHIFT = 3
FIBBLK = 25
FC = 50
SPAN = 540
SKYC = 6
EXPOS = 32
PIECE = 8
CHUNK = 16
GROUPS = 128
LANES = 128
HALF = 64
SUB = 8
TAPS = BAND + 2 * SHIFT
EDGE = MARG * ROWS
DEPTH = SPAN * ROWS
LOCAL = 2 * BPIX * ROWS


f32 = jnp.float32
highest = lax.Precision.HIGHEST


def lanes_of(shape=(SUB, LANES), dim=1):
    return lax.broadcasted_iota(jnp.int32, shape, dim)


def sky_index(lane):
    within = lane & (HALF - 1)
    fibre = jnp.zeros_like(within)
    for i in range(1, SKYC):
        fibre = fibre + jnp.where(within >= i * COMP, 1, 0)
    comp = within - fibre * COMP
    valid = within < SKYC * COMP
    return fibre, comp, valid


def pick(x, idx):
    return jnp.take_along_axis(x, idx, axis=1, mode="promise_in_bounds")


def doubled(row, scratch):
    scratch[...] = jnp.zeros((SUB, LANES), jnp.int32)
    scratch[0:1, 0:FC] = row
    scratch[0:1, HALF : HALF + FC] = row
    return jnp.broadcast_to(scratch[0:1, :], (SUB, LANES))


def sky_lanes(row, scratch, ccd_at, fibre):
    scratch[...] = jnp.zeros((SUB, LANES), jnp.int32)
    scratch[0:1, 0 : row.shape[1]] = row
    listed = jnp.broadcast_to(scratch[0:1, :], (SUB, LANES))
    return (lanes_of() & HALF) + pick(listed, fibre + ccd_at * SKYC) - ccd_at * FC


def banded(res_ref, res_s):
    res_s[...] = jnp.zeros((BAND, SUB, LANES), f32)
    for d in range(BAND):
        res_s[d, :, 0:FC] = res_ref[d, 0:SUB, :]
        res_s[d, :, HALF : HALF + FC] = res_ref[d, SUB:CHUNK, :]
    return [res_s[d] for d in range(BAND)]


def turned_basis(basis_ref, basis_s, turned_s, exp_at):
    basis_s[...] = jnp.zeros((16, 640), f32)
    basis_s[0:COMP, 0:528] = basis_ref[...]
    tile = exp_at // 8
    offset = CHUNK * (exp_at % 8)
    near = basis_s[:, pl.ds(pl.multiple_of(tile * LANES, LANES), LANES)]
    far = basis_s[:, pl.ds(pl.multiple_of(tile * LANES + LANES, LANES), LANES)]
    turn = (LANES - offset) % LANES
    wide = lanes_of((16, LANES))
    window = jnp.where(wide < LANES - offset, pltpu.roll(near, turn, 1), pltpu.roll(far, turn, 1))
    turned_s[...] = jnp.transpose(jnp.concatenate([window, jnp.zeros((LANES - 16, LANES), f32)], axis=0))[0:32]


def tap_of(t, bands, masks):
    tap = jnp.zeros((SUB, LANES), f32)
    for s in range(2 * SHIFT + 1):
        if 0 <= t - s < BAND:
            tap = jnp.where(masks[s], bands[t - s], tap)
    return tap


def basis_at(t, turned_s):
    upper = turned_s[t : t + SUB, :]
    lower = turned_s[t + SUB : t + 2 * SUB, :]
    return jnp.where(lanes_of() < HALF, upper, pltpu.roll(lower, HALF, 1))


def model_copies(res_h, basis_h, shift_h, res_v, basis_v, shift_v, sems):
    copies = [
        pltpu.make_async_copy(source, target, sems.at[i])
        for i, (source, target) in enumerate(((res_h, res_v), (basis_h, basis_v), (shift_h, shift_v)))
    ]
    for copy in copies:
        copy.start()
    return copies


def sky_kernel(res_h, basis_h, shift_h, sky_h, pix_h, send_ref, near_ref, far_ref, res_v, basis_v, shift_v, sky_v, res_s, basis_s, row_s, turned_s, sems):
    exp_at = lax.axis_index("exp")
    ccd_at = lax.axis_index("ccd")
    odd = ccd_at % 2
    at_near = pl.multiple_of(odd * (LOCAL - EDGE), EDGE)
    at_far = pl.multiple_of((1 - odd) * (LOCAL - EDGE), EDGE)
    edges = [
        pltpu.make_async_copy(pix_h.at[pl.ds(at_near, EDGE), :], near_ref, sems.at[4]),
        pltpu.make_async_copy(pix_h.at[pl.ds(at_far, EDGE), :], far_ref, sems.at[5]),
    ]
    for edge in edges:
        edge.start()
    copies = model_copies(res_h, basis_h, shift_h, res_v, basis_v, shift_v, sems)
    listed = pltpu.make_async_copy(sky_h, sky_v, sems.at[3])
    listed.start()
    listed.wait()
    for copy in copies:
        copy.wait()
    lane = lanes_of()
    fibre, comp, valid = sky_index(lane)
    sky = sky_lanes(sky_v[...], row_s, ccd_at, fibre)
    shift = pick(doubled(shift_v[...], row_s), sky) + SHIFT
    masks = [shift == s for s in range(2 * SHIFT + 1)]
    bands = [pick(band, sky) for band in banded(res_v, res_s)]
    turned_basis(basis_v, basis_s, turned_s, exp_at)
    total = jnp.zeros((SUB, LANES), f32)
    for t in range(TAPS):
        total = total + tap_of(t, bands, masks) * pick(basis_at(t, turned_s), (lane & HALF) + comp)
    total = jnp.where(valid, total, 0.0)
    send_ref[...] = jnp.broadcast_to(total[None], (EXPOS, SUB, LANES))
    for edge in edges:
        edge.wait()


def model_kernel(res_h, basis_h, shift_h, model_ref, res_v, basis_v, shift_v, res_s, basis_s, row_s, turned_s, sems):
    exp_at = lax.axis_index("exp")
    for copy in model_copies(res_h, basis_h, shift_h, res_v, basis_v, shift_v, sems):
        copy.wait()
    lane = lanes_of()
    shift = doubled(shift_v[...], row_s) + SHIFT
    masks = [shift == s for s in range(2 * SHIFT + 1)]
    bands = banded(res_v, res_s)
    turned_basis(basis_v, basis_s, turned_s, exp_at)
    totals = [jnp.zeros((SUB, LANES), f32) for _ in range(COMP)]
    for t in range(TAPS):
        tap = tap_of(t, bands, masks)
        both = basis_at(t, turned_s)
        for k in range(COMP):
            totals[k] = totals[k] + tap * pick(both, (lane & HALF) + k)
    for k in range(COMP):
        model_ref[k] = totals[k]


def extract_kernel(sky_h, slot_h, pix_ref, near_ref, far_ref, psf_ref, flux_ref, weight_ref, skyflux_ref, sky_v, slot_v, pix_s, var_s, pad_s, flux_s, vari_s, row_s, sems):
    ccd_at = lax.axis_index("ccd")
    base = ccd_at * FC
    lane = lanes_of()
    listed = pltpu.make_async_copy(sky_h, sky_v, sems.at[0])
    slotted = pltpu.make_async_copy(slot_h, slot_v, sems.at[1])
    listed.start()
    slotted.start()
    odd = ccd_at % 2
    pix_s[pl.ds(pl.multiple_of(odd * (EDGE + LOCAL), EDGE), EDGE), :] = near_ref[...]
    pix_s[EDGE : EDGE + LOCAL, :] = pix_ref[...]
    pix_s[pl.ds(pl.multiple_of((1 - odd) * (EDGE + LOCAL), EDGE), EDGE), :] = far_ref[...]
    var_s[...] = (0.25 + jnp.square(pix_s[...].astype(f32))).astype(jnp.bfloat16)
    pad_s[...] = jnp.zeros((LANES, LANES), f32)
    for b in range(2):
        lower = b * BPIX * ROWS
        psf = psf_ref[b]
        pad_s[0:100, :] = jnp.dot(psf, pix_s[lower : lower + DEPTH, :], preferred_element_type=f32)
        flux_s[b] = jnp.transpose(pad_s[...])
        square = jnp.square(psf.astype(f32)).astype(jnp.bfloat16)
        pad_s[0:100, :] = jnp.dot(square, var_s[lower : lower + DEPTH, :], preferred_element_type=f32)
        vari_s[b] = jnp.transpose(pad_s[...])
    listed.wait()
    slotted.wait()
    fibre, _, valid = sky_index(lane)
    sky = sky_lanes(sky_v[...], row_s, ccd_at, fibre)
    slot = doubled(slot_v[...], row_s)
    used = (lane & (HALF - 1)) < FC
    slot = jnp.where(used, slot - base, 0)
    second = slot >= FIBBLK
    place = jnp.where(second, slot - FIBBLK, slot) * ROWS
    sky_slot = pick(slot, sky)
    sky_second = sky_slot >= FIBBLK
    sky_place = jnp.where(sky_second, sky_slot - FIBBLK, sky_slot) * ROWS

    def gathered(ref, row, spot, late):
        upper = jnp.where(late, pick(ref[1, row : row + SUB, :], spot), pick(ref[0, row : row + SUB, :], spot))
        row = row + SUB
        lower = jnp.where(late, pick(ref[1, row : row + SUB, :], spot), pick(ref[0, row : row + SUB, :], spot))
        return jnp.where(lane < HALF, upper, lower)

    for r in range(ROWS):
        for m in range(GROUPS // CHUNK):
            flux = jnp.where(used, gathered(flux_s, m * CHUNK, place + r, second), 0.0)
            flux_ref[r * 8 + m] = flux
            skyflux_ref[r * 8 + m] = jnp.where(valid, pick(flux, sky), 0.0)
            vari = gathered(vari_s, m * CHUNK, sky_place + r, sky_second)
            weight_ref[r * 8 + m] = jnp.where(valid, 1.0 / vari, 0.0)


def gram_kernel(model_ref, weight_ref, flux_ref, out_ref):
    model = model_ref[...].reshape(EXPOS * SUB, LANES)
    weighted = model * weight_ref[...].reshape(EXPOS * SUB, LANES)
    target = jnp.sum(weighted * flux_ref[...].reshape(EXPOS * SUB, LANES), axis=0, keepdims=True)
    square = lax.dot_general(weighted, model, (((0,), (0,)), ((), ())), precision=highest, preferred_element_type=f32)
    shape = (LANES, LANES)
    fibre_r, comp_r, valid_r = sky_index(lanes_of(shape, 0))
    row, col = lanes_of(shape, 0), lanes_of(shape, 1)
    fibre_c, comp_c, valid_c = sky_index(col)
    same = (fibre_r == fibre_c) & ((row & HALF) == (col & HALF)) & valid_r & valid_c
    square = jnp.where(same, square, 0.0)
    select = jnp.where((row == comp_c) & valid_c, 1.0, 0.0)
    half = jnp.dot(select[0:16], square, precision=highest, preferred_element_type=f32)
    half = jnp.where(row[0:16] == COMP, target, half)
    full = lax.dot_general(half, select, (((1,), (1,)), ((), ())), precision=highest, preferred_element_type=f32)
    tile = full[0:SUB] + pltpu.roll(full[SUB : 2 * SUB], HALF, 1)
    out_ref[...] = jnp.broadcast_to(tile[None], out_ref.shape)


def solve_kernel(parts_ref, flux_ref, out_ref):
    total = jnp.sum(parts_ref[...], axis=0)
    system = jnp.concatenate([total, pltpu.roll(total, HALF, 1)], axis=0)
    col = lanes_of((16, LANES))
    row = lanes_of((16, LANES), 0)
    system = jnp.where((col < COMP) & (row <= COMP), system, 0.0)
    for k in range(COMP):
        column = pick(system, jnp.full((16, LANES), k, jnp.int32))
        line = system[k : k + 1, :]
        pivot = column[k : k + 1, :]
        unit = jnp.where(col[0:1] == k, 1.0, 0.0)
        system = system - column * ((line - unit) / pivot)
    coeffs = jnp.broadcast_to(system[COMP : COMP + 1, :], (SUB, LANES))
    coeffs = pltpu.roll(coeffs, FC, 1)
    lane = lanes_of()
    here = (lane >= FC) & (lane < FC + COMP)
    for e in range(EXPOS):
        out_ref[e] = jnp.where(here, coeffs, flux_ref[e])


def subtract_kernel(flux_ref, model_ref, out_h, noise_ref, left_s, out_s, sems):
    models = [model_ref[k] for k in range(COMP)]
    spots = [jnp.full((SUB, LANES), FC + k, jnp.int32) for k in range(COMP)]
    total = jnp.zeros((SUB, LANES), f32)
    copies = []
    for e in range(EXPOS):
        left = flux_ref[e]
        sky = pick(left, spots[0]) * models[0]
        for k in range(1, COMP):
            sky = sky + pick(left, spots[k]) * models[k]
        left = left - sky
        left_s[e] = left
        total = total + left
        out_s[e, 0:SUB, :] = left[:, 0:FC]
        out_s[e, SUB:CHUNK, :] = pltpu.roll(left, HALF, 1)[:, 0:FC]
        if e % PIECE == PIECE - 1:
            at = pl.ds(e + 1 - PIECE, PIECE)
            copies.append(pltpu.make_async_copy(out_s.at[at], out_h.at[at], sems.at[e // PIECE]))
            copies[-1].start()
    mean = total * (1.0 / EXPOS)
    spread = jnp.zeros((SUB, LANES), f32)
    for e in range(EXPOS):
        spread = spread + jnp.square(left_s[e] - mean)
    noise = jnp.sqrt(spread * (1.0 / EXPOS) + 1e-06)
    noise_ref[0:SUB, :] = noise[:, 0:FC]
    noise_ref[SUB:CHUNK, :] = pltpu.roll(noise, HALF, 1)[:, 0:FC]
    for copy in copies:
        copy.wait()


VMEM = pl.BlockSpec(memory_space=pltpu.VMEM)
HBM = pl.BlockSpec(memory_space=pltpu.HBM)
TILES = jax.ShapeDtypeStruct((EXPOS, SUB, LANES), f32)
EDGES = jax.ShapeDtypeStruct((EDGE, GROUPS), jnp.bfloat16)
PARAMS = pltpu.CompilerParams(vmem_limit_bytes=40 * 1024 * 1024)
MODEL_INPUTS = [pltpu.VMEM((BAND, CHUNK, FC), f32), pltpu.VMEM((COMP, 528), f32), pltpu.VMEM((1, FC), jnp.int32)]
MODEL_SCRATCH = [
    pltpu.VMEM((BAND, SUB, LANES), f32),
    pltpu.VMEM((16, 640), f32),
    pltpu.VMEM((SUB, LANES), jnp.int32),
    pltpu.VMEM((32, LANES), f32),
]


def sky_model(resolution, basis, shift, sky, pixels):
    return pl.pallas_call(
        sky_kernel,
        out_shape=(TILES, EDGES, EDGES),
        in_specs=[HBM] * 5,
        out_specs=(VMEM, VMEM, VMEM),
        scratch_shapes=MODEL_INPUTS + [pltpu.VMEM((1, 96), jnp.int32)] + MODEL_SCRATCH + [pltpu.SemaphoreType.DMA((6,))],
        compiler_params=PARAMS,
        name="sky_model",
    )(*(pltpu.with_memory_space_constraint(v, pltpu.HBM) for v in (resolution, basis, shift, sky, pixels)))


def local_model(resolution, basis, shift):
    return pl.pallas_call(
        model_kernel,
        out_shape=jax.ShapeDtypeStruct((COMP, SUB, LANES), f32),
        in_specs=[HBM] * 3,
        out_specs=VMEM,
        scratch_shapes=MODEL_INPUTS + MODEL_SCRATCH + [pltpu.SemaphoreType.DMA((3,))],
        compiler_params=PARAMS,
        name="local_model",
    )(*(pltpu.with_memory_space_constraint(v, pltpu.HBM) for v in (resolution, basis, shift)))


def extract(sky, slot, pixels, near, far, psf):
    return pl.pallas_call(
        extract_kernel,
        out_shape=(TILES, TILES, TILES),
        in_specs=[HBM, HBM, VMEM, VMEM, VMEM, VMEM],
        out_specs=(VMEM, VMEM, VMEM),
        scratch_shapes=[
            pltpu.VMEM((1, 96), jnp.int32),
            pltpu.VMEM((1, FC), jnp.int32),
            pltpu.VMEM((2 * EDGE + LOCAL, LANES), jnp.bfloat16),
            pltpu.VMEM((2 * EDGE + LOCAL, LANES), jnp.bfloat16),
            pltpu.VMEM((LANES, LANES), f32),
            pltpu.VMEM((2, LANES, LANES), f32),
            pltpu.VMEM((2, LANES, LANES), f32),
            pltpu.VMEM((SUB, LANES), jnp.int32),
            pltpu.SemaphoreType.DMA((2,)),
        ],
        compiler_params=PARAMS,
        name="extract",
    )(*(pltpu.with_memory_space_constraint(v, pltpu.HBM) for v in (sky, slot)), pixels, near, far, psf)


def gram_parts(model, weight, flux, copies):
    return pl.pallas_call(
        gram_kernel,
        out_shape=jax.ShapeDtypeStruct((copies, SUB, LANES), f32),
        in_specs=[VMEM, VMEM, VMEM],
        out_specs=VMEM,
        compiler_params=PARAMS,
        name="gram",
    )(model, weight, flux)


def solve(parts, flux):
    return pl.pallas_call(
        solve_kernel, out_shape=TILES, in_specs=[VMEM, VMEM], out_specs=VMEM, compiler_params=PARAMS, name="solve"
    )(parts, flux)


def subtract(flux, model):
    return pl.pallas_call(
        subtract_kernel,
        out_shape=(jax.ShapeDtypeStruct((EXPOS, CHUNK, FC), f32), jax.ShapeDtypeStruct((CHUNK, FC), f32)),
        in_specs=[VMEM, VMEM],
        out_specs=(HBM, VMEM),
        scratch_shapes=[
            pltpu.VMEM((EXPOS, SUB, LANES), f32),
            pltpu.VMEM((EXPOS, CHUNK, FC), f32),
            pltpu.SemaphoreType.DMA((EXPOS // PIECE,)),
        ],
        compiler_params=PARAMS,
        name="subtract",
    )(flux, model)


def shards(pixels, psf_proj, resolution, basis, sky_fibres, fibre_slot, band_shift):
    size = lax.axis_size("ccd")
    rows = pixels.reshape(LOCAL, GROUPS)
    res = resolution.transpose(1, 2, 0)
    sky = sky_fibres.reshape(1, -1)
    slot = fibre_slot.reshape(1, FC)
    shift = band_shift.reshape(1, FC)
    pairs = [[(i, i + 1) for i in range(start, size - 1, 2)] for start in (1, 0)]
    swaps = [[*pair, *((j, i) for i, j in pair)] for pair in pairs]
    send, near, far = sky_model(res, basis, shift, sky, rows)
    near = lax.ppermute(near, "ccd", swaps[0])
    far = lax.ppermute(far, "ccd", swaps[1])
    model = local_model(res, basis, shift)
    near, far, model = lax.optimization_barrier((near, far, model))
    sky_tiles = lax.all_to_all(send, "exp", split_axis=0, concat_axis=0, tiled=True)
    flux, weight, sky_flux = extract(sky, slot, rows, near, far, psf_proj)
    parts = gram_parts(sky_tiles, weight, sky_flux, size)
    parts = lax.all_to_all(parts, "ccd", split_axis=0, concat_axis=0, tiled=True)
    flux = solve(parts, flux)
    flux = lax.all_to_all(flux, "exp", split_axis=0, concat_axis=0, tiled=True)
    sky_subtracted, noise_rms = subtract(flux, model)
    return (sky_subtracted.transpose(0, 2, 1), noise_rms.transpose(1, 0))


def solution(mesh):
    in_specs = (
        P("exp", "ccd", None, None),
        P("ccd", None, None),
        P("ccd", None, "exp"),
        P(),
        P(),
        P("ccd"),
        P("ccd"),
    )
    out_specs = (P(None, "ccd", "exp"), P("ccd", "exp"))
    return jax.shard_map(shards, mesh=mesh, in_specs=in_specs, out_specs=out_specs, check_vma=False)
```

```python
import jax
import jax.numpy as jnp
from jax import lax
from jax.experimental import pallas as pl
from jax.experimental.pallas import tpu as pltpu
from jax.sharding import PartitionSpec as P

BPIX = 500
MARG = 20
ROWS = 4
COMP = 10
BAND = 11
SHIFT = 3
FIBBLK = 25
FC = 50
SPAN = 540
SKYC = 6
EXPOS = 32
PIECE = 8
CHUNK = 16
GROUPS = 128
LANES = 128
HALF = 64
SUB = 8
TAPS = BAND + 2 * SHIFT
EDGE = MARG * ROWS
DEPTH = SPAN * ROWS
LOCAL = 2 * BPIX * ROWS


f32 = jnp.float32
highest = lax.Precision.HIGHEST


def lanes_of(shape=(SUB, LANES), dim=1):
    return lax.broadcasted_iota(jnp.int32, shape, dim)


def sky_index(lane):
    within = lane & (HALF - 1)
    fibre = jnp.zeros_like(within)
    for i in range(1, SKYC):
        fibre = fibre + jnp.where(within >= i * COMP, 1, 0)
    comp = within - fibre * COMP
    valid = within < SKYC * COMP
    return fibre, comp, valid


def pick(x, idx):
    return jnp.take_along_axis(x, idx, axis=1, mode="promise_in_bounds")


def doubled(row, scratch):
    scratch[...] = jnp.zeros((SUB, LANES), jnp.int32)
    scratch[0:1, 0:FC] = row
    scratch[0:1, HALF : HALF + FC] = row
    return jnp.broadcast_to(scratch[0:1, :], (SUB, LANES))


def sky_lanes(row, scratch, ccd_at, fibre):
    scratch[...] = jnp.zeros((SUB, LANES), jnp.int32)
    scratch[0:1, 0 : row.shape[1]] = row
    listed = jnp.broadcast_to(scratch[0:1, :], (SUB, LANES))
    return (lanes_of() & HALF) + pick(listed, fibre + ccd_at * SKYC) - ccd_at * FC


def banded(res_ref, res_s):
    res_s[...] = jnp.zeros((BAND, SUB, LANES), f32)
    for d in range(BAND):
        res_s[d, :, 0:FC] = res_ref[d, 0:SUB, :]
        res_s[d, :, HALF : HALF + FC] = res_ref[d, SUB:CHUNK, :]
    return [res_s[d] for d in range(BAND)]


def turned_basis(basis_ref, basis_s, turned_s, exp_at):
    basis_s[...] = jnp.zeros((16, 640), f32)
    basis_s[0:COMP, 0:528] = basis_ref[...]
    tile = exp_at // 8
    offset = CHUNK * (exp_at % 8)
    near = basis_s[:, pl.ds(pl.multiple_of(tile * LANES, LANES), LANES)]
    far = basis_s[:, pl.ds(pl.multiple_of(tile * LANES + LANES, LANES), LANES)]
    turn = (LANES - offset) % LANES
    wide = lanes_of((16, LANES))
    window = jnp.where(wide < LANES - offset, pltpu.roll(near, turn, 1), pltpu.roll(far, turn, 1))
    turned_s[...] = jnp.transpose(jnp.concatenate([window, jnp.zeros((LANES - 16, LANES), f32)], axis=0))[0:32]


def tap_of(t, bands, masks):
    tap = jnp.zeros((SUB, LANES), f32)
    for s in range(2 * SHIFT + 1):
        if 0 <= t - s < BAND:
            tap = jnp.where(masks[s], bands[t - s], tap)
    return tap


def basis_at(t, turned_s):
    upper = turned_s[t : t + SUB, :]
    lower = turned_s[t + SUB : t + 2 * SUB, :]
    return jnp.where(lanes_of() < HALF, upper, pltpu.roll(lower, HALF, 1))


def model_copies(res_h, basis_h, shift_h, res_v, basis_v, shift_v, sems):
    copies = [
        pltpu.make_async_copy(source, target, sems.at[i])
        for i, (source, target) in enumerate(((res_h, res_v), (basis_h, basis_v), (shift_h, shift_v)))
    ]
    for copy in copies:
        copy.start()
    return copies


def sky_kernel(res_h, basis_h, shift_h, sky_h, pix_h, send_ref, near_ref, far_ref, res_v, basis_v, shift_v, sky_v, res_s, basis_s, row_s, turned_s, sems):
    exp_at = lax.axis_index("exp")
    ccd_at = lax.axis_index("ccd")
    odd = ccd_at % 2
    at_near = pl.multiple_of(odd * (LOCAL - EDGE), EDGE)
    at_far = pl.multiple_of((1 - odd) * (LOCAL - EDGE), EDGE)
    edges = [
        pltpu.make_async_copy(pix_h.at[pl.ds(at_near, EDGE), :], near_ref, sems.at[4]),
        pltpu.make_async_copy(pix_h.at[pl.ds(at_far, EDGE), :], far_ref, sems.at[5]),
    ]
    for edge in edges:
        edge.start()
    copies = model_copies(res_h, basis_h, shift_h, res_v, basis_v, shift_v, sems)
    listed = pltpu.make_async_copy(sky_h, sky_v, sems.at[3])
    listed.start()
    listed.wait()
    for copy in copies:
        copy.wait()
    lane = lanes_of()
    fibre, comp, valid = sky_index(lane)
    sky = sky_lanes(sky_v[...], row_s, ccd_at, fibre)
    shift = pick(doubled(shift_v[...], row_s), sky) + SHIFT
    masks = [shift == s for s in range(2 * SHIFT + 1)]
    bands = [pick(band, sky) for band in banded(res_v, res_s)]
    turned_basis(basis_v, basis_s, turned_s, exp_at)
    total = jnp.zeros((SUB, LANES), f32)
    for t in range(TAPS):
        total = total + tap_of(t, bands, masks) * pick(basis_at(t, turned_s), (lane & HALF) + comp)
    total = jnp.where(valid, total, 0.0)
    send_ref[...] = jnp.broadcast_to(total[None], (EXPOS, SUB, LANES))
    for edge in edges:
        edge.wait()


def model_kernel(res_h, basis_h, shift_h, model_ref, res_v, basis_v, shift_v, res_s, basis_s, row_s, turned_s, sems):
    exp_at = lax.axis_index("exp")
    for copy in model_copies(res_h, basis_h, shift_h, res_v, basis_v, shift_v, sems):
        copy.wait()
    lane = lanes_of()
    shift = doubled(shift_v[...], row_s) + SHIFT
    masks = [shift == s for s in range(2 * SHIFT + 1)]
    bands = banded(res_v, res_s)
    turned_basis(basis_v, basis_s, turned_s, exp_at)
    totals = [jnp.zeros((SUB, LANES), f32) for _ in range(COMP)]
    for t in range(TAPS):
        tap = tap_of(t, bands, masks)
        both = basis_at(t, turned_s)
        for k in range(COMP):
            totals[k] = totals[k] + tap * pick(both, (lane & HALF) + k)
    model_ref[...] = jnp.zeros((16, SUB * LANES), f32)
    for k in range(COMP):
        for j in range(SUB):
            model_ref[k : k + 1, j * LANES : (j + 1) * LANES] = totals[k][j : j + 1, :]


def extract_kernel(sky_h, slot_h, pix_ref, near_ref, far_ref, psf_ref, flux_ref, weight_ref, skyflux_ref, sky_v, slot_v, pix_s, var_s, pad_s, rows_s, flux_s, vari_s, row_s, sems):
    ccd_at = lax.axis_index("ccd")
    base = ccd_at * FC
    lane = lanes_of()
    listed = pltpu.make_async_copy(sky_h, sky_v, sems.at[0])
    slotted = pltpu.make_async_copy(slot_h, slot_v, sems.at[1])
    listed.start()
    slotted.start()
    odd = ccd_at % 2
    pix_s[pl.ds(pl.multiple_of(odd * (EDGE + LOCAL), EDGE), EDGE), :] = near_ref[...]
    pix_s[EDGE : EDGE + LOCAL, :] = pix_ref[...]
    pix_s[pl.ds(pl.multiple_of((1 - odd) * (EDGE + LOCAL), EDGE), EDGE), :] = far_ref[...]
    var_s[...] = (0.25 + jnp.square(pix_s[...].astype(f32))).astype(jnp.bfloat16)
    rows_s[...] = jnp.zeros((2, 2, LANES, LANES), f32)
    for b in range(2):
        lower = b * BPIX * ROWS
        psf = psf_ref[b]
        square = jnp.square(psf.astype(f32)).astype(jnp.bfloat16)
        for q, (weights, values) in enumerate(((psf, pix_s), (square, var_s))):
            pad_s[b, q] = jnp.dot(weights, values[lower : lower + DEPTH, :], preferred_element_type=f32)
            for r in range(ROWS):
                at = (r % 2) * HALF + b * 32
                rows_s[q, r // 2, at : at + FIBBLK, :] = pad_s[b, q, pl.ds(r, FIBBLK, stride=ROWS), :]
    for half in range(2):
        flux_s[half] = jnp.transpose(rows_s[0, half])
        vari_s[half] = jnp.transpose(rows_s[1, half])
    listed.wait()
    slotted.wait()
    fibre, _, valid = sky_index(lane)
    sky = sky_lanes(sky_v[...], row_s, ccd_at, fibre)
    slot = doubled(slot_v[...], row_s)
    used = (lane & (HALF - 1)) < FC
    slot = jnp.where(used, slot - base, 0)
    place = jnp.where(slot >= FIBBLK, slot + (32 - FIBBLK), slot)
    sky_place = pick(place, sky)

    def gathered(ref, row, spot):
        upper = pick(ref[row : row + SUB, :], spot)
        lower = pick(ref[row + SUB : row + 2 * SUB, :], spot)
        return jnp.where(lane < HALF, upper, lower)

    for r in range(ROWS):
        half, turn = r // 2, (r % 2) * HALF
        for m in range(GROUPS // CHUNK):
            flux = jnp.where(used, gathered(flux_s.at[half], m * CHUNK, place + turn), 0.0)
            flux_ref[r * 8 + m] = flux
            skyflux_ref[r * 8 + m] = jnp.where(valid, pick(flux, sky), 0.0)
            vari = gathered(vari_s.at[half], m * CHUNK, sky_place + turn)
            weight_ref[r * 8 + m] = jnp.where(valid, 1.0 / vari, 0.0)


def gram_kernel(model_ref, weight_ref, flux_ref, out_ref):
    model = model_ref[...].reshape(EXPOS * SUB, LANES)
    weighted = model * weight_ref[...].reshape(EXPOS * SUB, LANES)
    target = jnp.sum(weighted * flux_ref[...].reshape(EXPOS * SUB, LANES), axis=0, keepdims=True)
    square = lax.dot_general(weighted, model, (((0,), (0,)), ((), ())), precision=highest, preferred_element_type=f32)
    shape = (LANES, LANES)
    fibre_r, comp_r, valid_r = sky_index(lanes_of(shape, 0))
    row, col = lanes_of(shape, 0), lanes_of(shape, 1)
    fibre_c, comp_c, valid_c = sky_index(col)
    same = (fibre_r == fibre_c) & ((row & HALF) == (col & HALF)) & valid_r & valid_c
    square = jnp.where(same, square, 0.0)
    select = jnp.where((row == comp_c) & valid_c, 1.0, 0.0)
    half = jnp.dot(select[0:16], square, precision=highest, preferred_element_type=f32)
    half = jnp.where(row[0:16] == COMP, target, half)
    full = lax.dot_general(half, select, (((1,), (1,)), ((), ())), precision=highest, preferred_element_type=f32)
    tile = full[0:SUB] + pltpu.roll(full[SUB : 2 * SUB], HALF, 1)
    out_ref[...] = jnp.broadcast_to(tile[None], out_ref.shape)


def solve_kernel(parts_ref, flux_ref, out_ref):
    total = jnp.sum(parts_ref[...], axis=0)
    system = jnp.concatenate([total, pltpu.roll(total, HALF, 1)], axis=0)
    col = lanes_of((16, LANES))
    row = lanes_of((16, LANES), 0)
    system = jnp.where((col < COMP) & (row <= COMP), system, 0.0)
    for k in range(COMP):
        column = pick(system, jnp.full((16, LANES), k, jnp.int32))
        line = system[k : k + 1, :]
        pivot = column[k : k + 1, :]
        unit = jnp.where(col[0:1] == k, 1.0, 0.0)
        system = system - column * ((line - unit) / pivot)
    coeffs = jnp.broadcast_to(system[COMP : COMP + 1, :], (SUB, LANES))
    coeffs = pltpu.roll(coeffs, FC, 1)
    lane = lanes_of()
    here = (lane >= FC) & (lane < FC + COMP)
    for e in range(EXPOS):
        out_ref[e] = jnp.where(here, coeffs, flux_ref[e])


def subtract_kernel(flux_ref, model_ref, out_h, noise_ref, sky_s, left_s, out_s, sems):
    heads = flux_ref[pl.ds(0, EXPOS, stride=SUB), :]
    coeffs = pltpu.roll(heads, LANES - FC, 1)
    coeffs = jnp.where(lanes_of((EXPOS, LANES)) < COMP, coeffs, 0.0)[:, 0:16]
    sky = jnp.dot(coeffs, model_ref[...], precision=highest, preferred_element_type=f32)
    for j in range(SUB):
        sky_s[pl.ds(j, EXPOS, stride=SUB), :] = sky[:, j * LANES : (j + 1) * LANES]
    total = jnp.zeros((SUB, LANES), f32)
    copies = []
    for e in range(EXPOS):
        at = slice(e * SUB, (e + 1) * SUB)
        left = flux_ref[at, :] - sky_s[at, :]
        left_s[at, :] = left
        total = total + left
        out_s[e, 0:SUB, :] = left[:, 0:FC]
        out_s[e, SUB:CHUNK, :] = pltpu.roll(left, HALF, 1)[:, 0:FC]
        if e % PIECE == PIECE - 1:
            part = pl.ds(e + 1 - PIECE, PIECE)
            copies.append(pltpu.make_async_copy(out_s.at[part], out_h.at[part], sems.at[e // PIECE]))
            copies[-1].start()
    mean = total * (1.0 / EXPOS)
    spread = jnp.zeros((SUB, LANES), f32)
    for e in range(EXPOS):
        spread = spread + jnp.square(left_s[e * SUB : (e + 1) * SUB, :] - mean)
    noise = jnp.sqrt(spread * (1.0 / EXPOS) + 1e-06)
    noise_ref[0:SUB, :] = noise[:, 0:FC]
    noise_ref[SUB:CHUNK, :] = pltpu.roll(noise, HALF, 1)[:, 0:FC]
    for copy in copies:
        copy.wait()


VMEM = pl.BlockSpec(memory_space=pltpu.VMEM)
HBM = pl.BlockSpec(memory_space=pltpu.HBM)
TILES = jax.ShapeDtypeStruct((EXPOS, SUB, LANES), f32)
EDGES = jax.ShapeDtypeStruct((EDGE, GROUPS), jnp.bfloat16)
PARAMS = pltpu.CompilerParams(vmem_limit_bytes=40 * 1024 * 1024)
MODEL_INPUTS = [pltpu.VMEM((BAND, CHUNK, FC), f32), pltpu.VMEM((COMP, 528), f32), pltpu.VMEM((1, FC), jnp.int32)]
MODEL_SCRATCH = [
    pltpu.VMEM((BAND, SUB, LANES), f32),
    pltpu.VMEM((16, 640), f32),
    pltpu.VMEM((SUB, LANES), jnp.int32),
    pltpu.VMEM((32, LANES), f32),
]


def sky_model(resolution, basis, shift, sky, pixels):
    return pl.pallas_call(
        sky_kernel,
        out_shape=(TILES, EDGES, EDGES),
        in_specs=[HBM] * 5,
        out_specs=(VMEM, VMEM, VMEM),
        scratch_shapes=MODEL_INPUTS + [pltpu.VMEM((1, 96), jnp.int32)] + MODEL_SCRATCH + [pltpu.SemaphoreType.DMA((6,))],
        compiler_params=PARAMS,
        name="sky_model",
    )(*(pltpu.with_memory_space_constraint(v, pltpu.HBM) for v in (resolution, basis, shift, sky, pixels)))


def local_model(resolution, basis, shift):
    return pl.pallas_call(
        model_kernel,
        out_shape=jax.ShapeDtypeStruct((16, SUB * LANES), f32),
        in_specs=[HBM] * 3,
        out_specs=VMEM,
        scratch_shapes=MODEL_INPUTS + MODEL_SCRATCH + [pltpu.SemaphoreType.DMA((3,))],
        compiler_params=PARAMS,
        name="local_model",
    )(*(pltpu.with_memory_space_constraint(v, pltpu.HBM) for v in (resolution, basis, shift)))


def extract(sky, slot, pixels, near, far, psf):
    return pl.pallas_call(
        extract_kernel,
        out_shape=(TILES, TILES, TILES),
        in_specs=[HBM, HBM, VMEM, VMEM, VMEM, VMEM],
        out_specs=(VMEM, VMEM, VMEM),
        scratch_shapes=[
            pltpu.VMEM((1, 96), jnp.int32),
            pltpu.VMEM((1, FC), jnp.int32),
            pltpu.VMEM((2 * EDGE + LOCAL, LANES), jnp.bfloat16),
            pltpu.VMEM((2 * EDGE + LOCAL, LANES), jnp.bfloat16),
            pltpu.VMEM((2, 2, FIBBLK * ROWS, LANES), f32),
            pltpu.VMEM((2, 2, LANES, LANES), f32),
            pltpu.VMEM((2, LANES, LANES), f32),
            pltpu.VMEM((2, LANES, LANES), f32),
            pltpu.VMEM((SUB, LANES), jnp.int32),
            pltpu.SemaphoreType.DMA((2,)),
        ],
        compiler_params=PARAMS,
        cost_estimate=pl.CostEstimate(flops=2400000000, transcendentals=0, bytes_accessed=4000000),
        name="extract",
    )(*(pltpu.with_memory_space_constraint(v, pltpu.HBM) for v in (sky, slot)), pixels, near, far, psf)


def gram_parts(model, weight, flux, copies):
    return pl.pallas_call(
        gram_kernel,
        out_shape=jax.ShapeDtypeStruct((copies, SUB, LANES), f32),
        in_specs=[VMEM, VMEM, VMEM],
        out_specs=VMEM,
        compiler_params=PARAMS,
        name="gram",
    )(model, weight, flux)


def solve(parts, flux):
    return pl.pallas_call(
        solve_kernel, out_shape=TILES, in_specs=[VMEM, VMEM], out_specs=VMEM, compiler_params=PARAMS, name="solve"
    )(parts, flux)


def subtract(flux, model):
    return pl.pallas_call(
        subtract_kernel,
        out_shape=(jax.ShapeDtypeStruct((EXPOS, CHUNK, FC), f32), jax.ShapeDtypeStruct((CHUNK, FC), f32)),
        in_specs=[VMEM, VMEM],
        out_specs=(HBM, VMEM),
        scratch_shapes=[
            pltpu.VMEM((EXPOS * SUB, LANES), f32),
            pltpu.VMEM((EXPOS * SUB, LANES), f32),
            pltpu.VMEM((EXPOS, CHUNK, FC), f32),
            pltpu.SemaphoreType.DMA((EXPOS // PIECE,)),
        ],
        compiler_params=PARAMS,
        name="subtract",
    )(flux.reshape(EXPOS * SUB, LANES), model)


def shards(pixels, psf_proj, resolution, basis, sky_fibres, fibre_slot, band_shift):
    size = lax.axis_size("ccd")
    rows = pixels.reshape(LOCAL, GROUPS)
    res = resolution.transpose(1, 2, 0)
    sky = sky_fibres.reshape(1, -1)
    slot = fibre_slot.reshape(1, FC)
    shift = band_shift.reshape(1, FC)
    pairs = [[(i, i + 1) for i in range(start, size - 1, 2)] for start in (1, 0)]
    swaps = [[*pair, *((j, i) for i, j in pair)] for pair in pairs]
    send, near, far = sky_model(res, basis, shift, sky, rows)
    near = lax.ppermute(near, "ccd", swaps[0])
    near, far = lax.optimization_barrier((near, far))
    far = lax.ppermute(far, "ccd", swaps[1])
    model = local_model(res, basis, shift)
    near, far, model = lax.optimization_barrier((near, far, model))
    sky_tiles = lax.all_to_all(send, "exp", split_axis=0, concat_axis=0, tiled=True)
    flux, weight, sky_flux = extract(sky, slot, rows, near, far, psf_proj)
    parts = gram_parts(sky_tiles, weight, sky_flux, size)
    parts = lax.all_to_all(parts, "ccd", split_axis=0, concat_axis=0, tiled=True)
    flux = solve(parts, flux)
    flux = lax.all_to_all(flux, "exp", split_axis=0, concat_axis=0, tiled=True)
    sky_subtracted, noise_rms = subtract(flux, model)
    return (sky_subtracted.transpose(0, 2, 1), noise_rms.transpose(1, 0))


def solution(mesh):
    in_specs = (
        P("exp", "ccd", None, None),
        P("ccd", None, None),
        P("ccd", None, "exp"),
        P(),
        P(),
        P("ccd"),
        P("ccd"),
    )
    out_specs = (P(None, "ccd", "exp"), P("ccd", "exp"))
    return jax.shard_map(shards, mesh=mesh, in_specs=in_specs, out_specs=out_specs, check_vma=False)
```

```python
import jax
import jax.numpy as jnp
from jax import lax
from jax.experimental import pallas as pl
from jax.experimental.pallas import tpu as pltpu
from jax.sharding import PartitionSpec as P

BPIX = 500
MARG = 20
ROWS = 4
COMP = 10
BAND = 11
SHIFT = 3
FIBBLK = 25
FC = 50
SPAN = 540
SKYC = 6
EXPOS = 32
PIECE = 8
CHUNK = 16
GROUPS = 128
LANES = 128
HALF = 64
SUB = 8
TAPS = BAND + 2 * SHIFT
EDGE = MARG * ROWS
DEPTH = SPAN * ROWS
TAIL = 32
LOCAL = 2 * BPIX * ROWS


f32 = jnp.float32
highest = lax.Precision.HIGHEST


def lanes_of(shape=(SUB, LANES), dim=1):
    return lax.broadcasted_iota(jnp.int32, shape, dim)


def sky_index(lane):
    within = lane & (HALF - 1)
    fibre = jnp.zeros_like(within)
    for i in range(1, SKYC):
        fibre = fibre + jnp.where(within >= i * COMP, 1, 0)
    comp = within - fibre * COMP
    valid = within < SKYC * COMP
    return fibre, comp, valid


def pick(x, idx):
    return jnp.take_along_axis(x, idx, axis=1, mode="promise_in_bounds")


def doubled(row, scratch):
    scratch[...] = jnp.zeros((SUB, LANES), jnp.int32)
    scratch[0:1, 0:FC] = row
    scratch[0:1, HALF : HALF + FC] = row
    return jnp.broadcast_to(scratch[0:1, :], (SUB, LANES))


def sky_lanes(row, scratch, ccd_at, fibre):
    scratch[...] = jnp.zeros((SUB, LANES), jnp.int32)
    scratch[0:1, 0 : row.shape[1]] = row
    listed = jnp.broadcast_to(scratch[0:1, :], (SUB, LANES))
    return (lanes_of() & HALF) + pick(listed, fibre + ccd_at * SKYC) - ccd_at * FC


def banded(res_ref, res_s):
    res_s[...] = jnp.zeros((BAND, SUB, LANES), f32)
    for d in range(BAND):
        res_s[d, :, 0:FC] = res_ref[d, 0:SUB, :]
        res_s[d, :, HALF : HALF + FC] = res_ref[d, SUB:CHUNK, :]
    return [res_s[d] for d in range(BAND)]


def turned_basis(basis_ref, basis_s, turned_s, exp_at):
    basis_s[...] = jnp.zeros((16, 640), f32)
    basis_s[0:COMP, 0:528] = basis_ref[...]
    tile = exp_at // 8
    offset = CHUNK * (exp_at % 8)
    near = basis_s[:, pl.ds(pl.multiple_of(tile * LANES, LANES), LANES)]
    far = basis_s[:, pl.ds(pl.multiple_of(tile * LANES + LANES, LANES), LANES)]
    turn = (LANES - offset) % LANES
    wide = lanes_of((16, LANES))
    window = jnp.where(wide < LANES - offset, pltpu.roll(near, turn, 1), pltpu.roll(far, turn, 1))
    turned_s[...] = jnp.transpose(jnp.concatenate([window, jnp.zeros((LANES - 16, LANES), f32)], axis=0))[0:32]


def tap_of(t, bands, masks):
    tap = jnp.zeros((SUB, LANES), f32)
    for s in range(2 * SHIFT + 1):
        if 0 <= t - s < BAND:
            tap = jnp.where(masks[s], bands[t - s], tap)
    return tap


def basis_at(t, turned_s):
    upper = turned_s[t : t + SUB, :]
    lower = turned_s[t + SUB : t + 2 * SUB, :]
    return jnp.where(lanes_of() < HALF, upper, pltpu.roll(lower, HALF, 1))


def model_copies(res_h, basis_h, shift_h, res_v, basis_v, shift_v, sems):
    copies = [
        pltpu.make_async_copy(source, target, sems.at[i])
        for i, (source, target) in enumerate(((res_h, res_v), (basis_h, basis_v), (shift_h, shift_v)))
    ]
    for copy in copies:
        copy.start()
    return copies


def sky_kernel(res_h, basis_h, shift_h, sky_h, pix_h, send_ref, near_ref, far_ref, res_v, basis_v, shift_v, sky_v, res_s, basis_s, row_s, turned_s, sems):
    exp_at = lax.axis_index("exp")
    ccd_at = lax.axis_index("ccd")
    odd = ccd_at % 2
    at_near = pl.multiple_of(odd * (LOCAL - EDGE), EDGE)
    at_far = pl.multiple_of((1 - odd) * (LOCAL - EDGE), EDGE)
    edges = [
        pltpu.make_async_copy(pix_h.at[pl.ds(at_near, EDGE), :], near_ref, sems.at[4]),
        pltpu.make_async_copy(pix_h.at[pl.ds(at_far, EDGE), :], far_ref, sems.at[5]),
    ]
    for edge in edges:
        edge.start()
    copies = model_copies(res_h, basis_h, shift_h, res_v, basis_v, shift_v, sems)
    listed = pltpu.make_async_copy(sky_h, sky_v, sems.at[3])
    listed.start()
    listed.wait()
    for copy in copies:
        copy.wait()
    lane = lanes_of()
    fibre, comp, valid = sky_index(lane)
    sky = sky_lanes(sky_v[...], row_s, ccd_at, fibre)
    shift = pick(doubled(shift_v[...], row_s), sky) + SHIFT
    masks = [shift == s for s in range(2 * SHIFT + 1)]
    bands = [pick(band, sky) for band in banded(res_v, res_s)]
    turned_basis(basis_v, basis_s, turned_s, exp_at)
    total = jnp.zeros((SUB, LANES), f32)
    for t in range(TAPS):
        total = total + tap_of(t, bands, masks) * pick(basis_at(t, turned_s), (lane & HALF) + comp)
    total = jnp.where(valid, total, 0.0)
    send_ref[...] = jnp.broadcast_to(total[None], (EXPOS, SUB, LANES))
    for edge in edges:
        edge.wait()


def model_kernel(res_h, basis_h, shift_h, model_ref, res_v, basis_v, shift_v, res_s, basis_s, row_s, turned_s, sems):
    exp_at = lax.axis_index("exp")
    for copy in model_copies(res_h, basis_h, shift_h, res_v, basis_v, shift_v, sems):
        copy.wait()
    lane = lanes_of()
    shift = doubled(shift_v[...], row_s) + SHIFT
    masks = [shift == s for s in range(2 * SHIFT + 1)]
    bands = banded(res_v, res_s)
    turned_basis(basis_v, basis_s, turned_s, exp_at)
    totals = [jnp.zeros((SUB, LANES), f32) for _ in range(COMP)]
    for t in range(TAPS):
        tap = tap_of(t, bands, masks)
        both = basis_at(t, turned_s)
        for k in range(COMP):
            totals[k] = totals[k] + tap * pick(both, (lane & HALF) + k)
    model_ref[...] = jnp.zeros((16, SUB * LANES), f32)
    for k in range(COMP):
        for j in range(SUB):
            model_ref[k : k + 1, j * LANES : (j + 1) * LANES] = totals[k][j : j + 1, :]


def extract_kernel(pix_ref, near_ref, psf_ref, flux_ref, vari_ref, pix_s, var_s):
    odd = lax.axis_index("ccd") % 2
    far = pl.ds(pl.multiple_of((1 - odd) * (EDGE + LOCAL), EDGE), EDGE)
    pix_s[pl.ds(pl.multiple_of(odd * (EDGE + LOCAL), EDGE), EDGE), :] = near_ref[...]
    pix_s[EDGE : EDGE + LOCAL, :] = pix_ref[...]
    pix_s[far, :] = jnp.zeros((EDGE, LANES), jnp.bfloat16)
    var_s[...] = variance_of(pix_s[...])
    var_s[far, :] = jnp.zeros((EDGE, LANES), jnp.bfloat16)
    for b in range(2):
        lower = b * BPIX * ROWS
        psf = psf_ref[b]
        flux_ref[b] = jnp.dot(psf, pix_s[lower : lower + DEPTH, :], preferred_element_type=f32)
        vari_ref[b] = jnp.dot(squared(psf), var_s[lower : lower + DEPTH, :], preferred_element_type=f32)


def variance_of(x):
    return (0.25 + jnp.square(x.astype(f32))).astype(jnp.bfloat16)


def squared(x):
    return jnp.square(x.astype(f32)).astype(jnp.bfloat16)


def gram_kernel(sky_h, slot_h, far_ref, psf_ref, flux_in, vari_in, model_ref, flux_ref, out_ref, sky_v, slot_v, edge_s, extra_s, pad_s, rows_s, flux_s, vari_s, row_s, weighted_s, sems):
    ccd_at = lax.axis_index("ccd")
    base = ccd_at * FC
    odd = ccd_at % 2
    lane = lanes_of()
    listed = pltpu.make_async_copy(sky_h, sky_v, sems.at[0])
    slotted = pltpu.make_async_copy(slot_h, slot_v, sems.at[1])
    listed.start()
    slotted.start()
    rows_s[...] = jnp.zeros((2, 2, LANES, LANES), f32)
    edge_s[0, 0:TAIL, :] = jnp.zeros((TAIL, LANES), jnp.bfloat16)
    edge_s[1, 0:TAIL, :] = jnp.zeros((TAIL, LANES), jnp.bfloat16)
    edge_s[0, TAIL : TAIL + EDGE, :] = far_ref[...]
    edge_s[1, TAIL : TAIL + EDGE, :] = variance_of(far_ref[...])

    @pl.when(odd == 1)
    def first_block():
        psf = psf_ref[0, :, 0:EDGE]
        extra_s[0] = jnp.dot(psf, edge_s[0, TAIL : TAIL + EDGE, :], preferred_element_type=f32)
        extra_s[1] = jnp.dot(squared(psf), edge_s[1, TAIL : TAIL + EDGE, :], preferred_element_type=f32)

    @pl.when(odd == 0)
    def second_block():
        psf = psf_ref[1, :, DEPTH - EDGE - TAIL : DEPTH]
        extra_s[0] = jnp.dot(psf, edge_s[0], preferred_element_type=f32)
        extra_s[1] = jnp.dot(squared(psf), edge_s[1], preferred_element_type=f32)

    for b in range(2):
        for q, part in enumerate((flux_in, vari_in)):
            pad_s[b, q] = part[b] + jnp.where(odd == 1 - b, extra_s[q], 0.0)
            for r in range(ROWS):
                at = (r % 2) * HALF + b * 32
                rows_s[q, r // 2, at : at + FIBBLK, :] = pad_s[b, q, pl.ds(r, FIBBLK, stride=ROWS), :]
    for half in range(2):
        flux_s[half] = jnp.transpose(rows_s[0, half])
        vari_s[half] = jnp.transpose(rows_s[1, half])
    listed.wait()
    slotted.wait()
    fibre, _, valid = sky_index(lane)
    sky = sky_lanes(sky_v[...], row_s, ccd_at, fibre)
    slot = doubled(slot_v[...], row_s)
    used = (lane & (HALF - 1)) < FC
    slot = jnp.where(used, slot - base, 0)
    place = jnp.where(slot >= FIBBLK, slot + (32 - FIBBLK), slot)
    sky_place = pick(place, sky)

    def gathered(ref, row, spot):
        upper = pick(ref[row : row + SUB, :], spot)
        lower = pick(ref[row + SUB : row + 2 * SUB, :], spot)
        return jnp.where(lane < HALF, upper, lower)

    target = jnp.zeros((SUB, LANES), f32)
    for r in range(ROWS):
        half, turn = r // 2, (r % 2) * HALF
        for m in range(GROUPS // CHUNK):
            e = r * 8 + m
            flux = jnp.where(used, gathered(flux_s.at[half], m * CHUNK, place + turn), 0.0)
            flux_ref[e] = flux
            vari = gathered(vari_s.at[half], m * CHUNK, sky_place + turn)
            weighted = jnp.where(valid, model_ref[e] / vari, 0.0)
            weighted_s[e * SUB : (e + 1) * SUB, :] = weighted
            target = target + weighted * pick(flux, sky)
    target = jnp.sum(target, axis=0, keepdims=True)
    model = model_ref[...].reshape(EXPOS * SUB, LANES)
    square = lax.dot_general(weighted_s[...], model, (((0,), (0,)), ((), ())), precision=highest, preferred_element_type=f32)
    shape = (LANES, LANES)
    row, col = lanes_of(shape, 0), lanes_of(shape, 1)
    fibre_r, _, valid_r = sky_index(row)
    fibre_c, comp_c, valid_c = sky_index(col)
    same = (fibre_r == fibre_c) & ((row & HALF) == (col & HALF)) & valid_r & valid_c
    square = jnp.where(same, square, 0.0)
    select = jnp.where((row == comp_c) & valid_c, 1.0, 0.0)
    summed = jnp.dot(select[0:16], square, precision=highest, preferred_element_type=f32)
    summed = jnp.where(row[0:16] == COMP, target, summed)
    full = lax.dot_general(summed, select, (((1,), (1,)), ((), ())), precision=highest, preferred_element_type=f32)
    tile = full[0:SUB] + pltpu.roll(full[SUB : 2 * SUB], HALF, 1)
    out_ref[...] = jnp.broadcast_to(tile[None], out_ref.shape)


def solve_kernel(parts_ref, flux_ref, out_ref):
    total = jnp.sum(parts_ref[...], axis=0)
    system = jnp.concatenate([total, pltpu.roll(total, HALF, 1)], axis=0)
    col = lanes_of((16, LANES))
    row = lanes_of((16, LANES), 0)
    system = jnp.where((col < COMP) & (row <= COMP), system, 0.0)
    for k in range(0, COMP, 2):
        left = pick(system, jnp.full((16, LANES), k, jnp.int32))
        right = pick(system, jnp.full((16, LANES), k + 1, jnp.int32))
        upper = system[k : k + 1, :] - jnp.where(col[0:1] == k, 1.0, 0.0)
        lower = system[k + 1 : k + 2, :] - jnp.where(col[0:1] == k + 1, 1.0, 0.0)
        a, b = left[k : k + 1, :], right[k : k + 1, :]
        c, d = left[k + 1 : k + 2, :], right[k + 1 : k + 2, :]
        scale = 1.0 / (a * d - b * c)
        system = system - left * ((d * upper - b * lower) * scale) - right * ((a * lower - c * upper) * scale)
    coeffs = jnp.broadcast_to(system[COMP : COMP + 1, :], (SUB, LANES))
    coeffs = pltpu.roll(coeffs, FC, 1)
    lane = lanes_of()
    here = (lane >= FC) & (lane < FC + COMP)
    for e in range(EXPOS):
        out_ref[e] = jnp.where(here, coeffs, flux_ref[e])


def subtract_kernel(flux_ref, model_ref, out_h, noise_h, sky_s, left_s, out_s, noise_s, sems):
    heads = flux_ref[pl.ds(0, EXPOS, stride=SUB), :]
    coeffs = pltpu.roll(heads, LANES - FC, 1)
    coeffs = jnp.where(lanes_of((EXPOS, LANES)) < COMP, coeffs, 0.0)[:, 0:16]
    sky = jnp.dot(coeffs, model_ref[...], precision=highest, preferred_element_type=f32)
    for j in range(SUB):
        sky_s[pl.ds(j, EXPOS, stride=SUB), :] = sky[:, j * LANES : (j + 1) * LANES]
    total = jnp.zeros((SUB, LANES), f32)
    copies = []
    for e in range(EXPOS):
        at = slice(e * SUB, (e + 1) * SUB)
        left = flux_ref[at, :] - sky_s[at, :]
        left_s[at, :] = left
        total = total + left
        out_s[e, 0:SUB, :] = left[:, 0:FC]
        out_s[e, SUB:CHUNK, :] = pltpu.roll(left, HALF, 1)[:, 0:FC]
        if e % PIECE == PIECE - 1:
            part = pl.ds(e + 1 - PIECE, PIECE)
            copies.append(pltpu.make_async_copy(out_s.at[part], out_h.at[part], sems.at[e // PIECE]))
            copies[-1].start()
    mean = total * (1.0 / EXPOS)
    spread = jnp.zeros((SUB, LANES), f32)
    for e in range(EXPOS):
        spread = spread + jnp.square(left_s[e * SUB : (e + 1) * SUB, :] - mean)
    noise = jnp.sqrt(spread * (1.0 / EXPOS) + 1e-06)
    noise_s[0:SUB, :] = noise[:, 0:FC]
    noise_s[SUB:CHUNK, :] = pltpu.roll(noise, HALF, 1)[:, 0:FC]
    copies.append(pltpu.make_async_copy(noise_s, noise_h, sems.at[EXPOS // PIECE]))
    copies[-1].start()
    for copy in copies:
        copy.wait()


VMEM = pl.BlockSpec(memory_space=pltpu.VMEM)
HBM = pl.BlockSpec(memory_space=pltpu.HBM)
TILES = jax.ShapeDtypeStruct((EXPOS, SUB, LANES), f32)
EDGES = jax.ShapeDtypeStruct((EDGE, GROUPS), jnp.bfloat16)
PARAMS = pltpu.CompilerParams(vmem_limit_bytes=40 * 1024 * 1024)
MODEL_INPUTS = [pltpu.VMEM((BAND, CHUNK, FC), f32), pltpu.VMEM((COMP, 528), f32), pltpu.VMEM((1, FC), jnp.int32)]
MODEL_SCRATCH = [
    pltpu.VMEM((BAND, SUB, LANES), f32),
    pltpu.VMEM((16, 640), f32),
    pltpu.VMEM((SUB, LANES), jnp.int32),
    pltpu.VMEM((32, LANES), f32),
]


def sky_model(resolution, basis, shift, sky, pixels):
    return pl.pallas_call(
        sky_kernel,
        out_shape=(TILES, EDGES, EDGES),
        in_specs=[HBM] * 5,
        out_specs=(VMEM, VMEM, VMEM),
        scratch_shapes=MODEL_INPUTS + [pltpu.VMEM((1, 96), jnp.int32)] + MODEL_SCRATCH + [pltpu.SemaphoreType.DMA((6,))],
        compiler_params=PARAMS,
        name="sky_model",
    )(*(pltpu.with_memory_space_constraint(v, pltpu.HBM) for v in (resolution, basis, shift, sky, pixels)))


def local_model(resolution, basis, shift):
    return pl.pallas_call(
        model_kernel,
        out_shape=jax.ShapeDtypeStruct((16, SUB * LANES), f32),
        in_specs=[HBM] * 3,
        out_specs=VMEM,
        scratch_shapes=MODEL_INPUTS + MODEL_SCRATCH + [pltpu.SemaphoreType.DMA((3,))],
        compiler_params=PARAMS,
        name="local_model",
    )(*(pltpu.with_memory_space_constraint(v, pltpu.HBM) for v in (resolution, basis, shift)))


def extract(pixels, near, psf):
    part = jax.ShapeDtypeStruct((2, FIBBLK * ROWS, LANES), f32)
    return pl.pallas_call(
        extract_kernel,
        out_shape=(part, part),
        in_specs=[VMEM] * 3,
        out_specs=(VMEM, VMEM),
        scratch_shapes=[
            pltpu.VMEM((2 * EDGE + LOCAL, LANES), jnp.bfloat16),
            pltpu.VMEM((2 * EDGE + LOCAL, LANES), jnp.bfloat16),
        ],
        compiler_params=PARAMS,
        name="extract",
    )(pixels, near, psf)


def gram_parts(sky, slot, far, psf, flux, vari, model, copies):
    return pl.pallas_call(
        gram_kernel,
        out_shape=(TILES, jax.ShapeDtypeStruct((copies, SUB, LANES), f32)),
        in_specs=[HBM, HBM] + [VMEM] * 5,
        out_specs=(VMEM, VMEM),
        scratch_shapes=[
            pltpu.VMEM((1, 96), jnp.int32),
            pltpu.VMEM((1, FC), jnp.int32),
            pltpu.VMEM((2, TAIL + EDGE, LANES), jnp.bfloat16),
            pltpu.VMEM((2, FIBBLK * ROWS, LANES), f32),
            pltpu.VMEM((2, 2, FIBBLK * ROWS, LANES), f32),
            pltpu.VMEM((2, 2, LANES, LANES), f32),
            pltpu.VMEM((2, LANES, LANES), f32),
            pltpu.VMEM((2, LANES, LANES), f32),
            pltpu.VMEM((SUB, LANES), jnp.int32),
            pltpu.VMEM((EXPOS * SUB, LANES), f32),
            pltpu.SemaphoreType.DMA((2,)),
        ],
        compiler_params=PARAMS,
        name="gram",
    )(*(pltpu.with_memory_space_constraint(v, pltpu.HBM) for v in (sky, slot)), far, psf, flux, vari, model)


def solve(parts, flux):
    return pl.pallas_call(
        solve_kernel, out_shape=TILES, in_specs=[VMEM, VMEM], out_specs=VMEM, compiler_params=PARAMS, name="solve"
    )(parts, flux)


def subtract(flux, model):
    return pl.pallas_call(
        subtract_kernel,
        out_shape=(jax.ShapeDtypeStruct((EXPOS, CHUNK, FC), f32), jax.ShapeDtypeStruct((CHUNK, FC), f32)),
        in_specs=[VMEM, VMEM],
        out_specs=(HBM, HBM),
        scratch_shapes=[
            pltpu.VMEM((EXPOS * SUB, LANES), f32),
            pltpu.VMEM((EXPOS * SUB, LANES), f32),
            pltpu.VMEM((EXPOS, CHUNK, FC), f32),
            pltpu.VMEM((CHUNK, FC), f32),
            pltpu.SemaphoreType.DMA((EXPOS // PIECE + 1,)),
        ],
        compiler_params=PARAMS,
        name="subtract",
    )(flux.reshape(EXPOS * SUB, LANES), model)


def shards(pixels, psf_proj, resolution, basis, sky_fibres, fibre_slot, band_shift):
    size = lax.axis_size("ccd")
    rows = pixels.reshape(LOCAL, GROUPS)
    res = resolution.transpose(1, 2, 0)
    sky = sky_fibres.reshape(1, -1)
    slot = fibre_slot.reshape(1, FC)
    shift = band_shift.reshape(1, FC)
    pairs = [[(i, i + 1) for i in range(start, size - 1, 2)] for start in (1, 0)]
    swaps = [[*pair, *((j, i) for i, j in pair)] for pair in pairs]
    send, near, far = sky_model(res, basis, shift, sky, rows)
    near = lax.ppermute(near, "ccd", swaps[0])
    far = lax.ppermute(far, "ccd", swaps[1])
    model = local_model(res, basis, shift)
    part, vari = extract(rows, near, psf_proj)
    far, model, part, vari = lax.optimization_barrier((far, model, part, vari))
    sky_tiles = lax.all_to_all(send, "exp", split_axis=0, concat_axis=0, tiled=True)
    flux, parts = gram_parts(sky, slot, far, psf_proj, part, vari, sky_tiles, size)
    parts = lax.all_to_all(parts, "ccd", split_axis=0, concat_axis=0, tiled=True)
    flux = solve(parts, flux)
    flux = lax.all_to_all(flux, "exp", split_axis=0, concat_axis=0, tiled=True)
    sky_subtracted, noise_rms = subtract(flux, model)
    return (sky_subtracted.transpose(0, 2, 1), noise_rms.transpose(1, 0))


def solution(mesh):
    in_specs = (
        P("exp", "ccd", None, None),
        P("ccd", None, None),
        P("ccd", None, "exp"),
        P(),
        P(),
        P("ccd"),
        P("ccd"),
    )
    out_specs = (P(None, "ccd", "exp"), P("ccd", "exp"))
    return jax.shard_map(shards, mesh=mesh, in_specs=in_specs, out_specs=out_specs, check_vma=False)
```

```python
import jax
import jax.numpy as jnp
from jax import lax
from jax.experimental import pallas as pl
from jax.experimental.pallas import tpu as pltpu
from jax.sharding import PartitionSpec as P

BPIX = 500
MARG = 20
ROWS = 4
COMP = 10
BAND = 11
SHIFT = 3
FIBBLK = 25
FC = 50
SPAN = 540
SKYC = 6
EXPOS = 32
PIECE = 8
CHUNK = 16
GROUPS = 128
LANES = 128
HALF = 64
SUB = 8
TAPS = BAND + 2 * SHIFT
EDGE = MARG * ROWS
DEPTH = SPAN * ROWS
TAIL = 32
LOCAL = 2 * BPIX * ROWS


f32 = jnp.float32
highest = lax.Precision.HIGHEST


def lanes_of(shape=(SUB, LANES), dim=1):
    return lax.broadcasted_iota(jnp.int32, shape, dim)


def sky_index(lane):
    within = lane & (HALF - 1)
    fibre = jnp.zeros_like(within)
    for i in range(1, SKYC):
        fibre = fibre + jnp.where(within >= i * COMP, 1, 0)
    comp = within - fibre * COMP
    valid = within < SKYC * COMP
    return fibre, comp, valid


def pick(x, idx):
    return jnp.take_along_axis(x, idx, axis=1, mode="promise_in_bounds")


def doubled(row, scratch):
    scratch[...] = jnp.zeros((SUB, LANES), jnp.int32)
    scratch[0:1, 0:FC] = row
    scratch[0:1, HALF : HALF + FC] = row
    return jnp.broadcast_to(scratch[0:1, :], (SUB, LANES))


def sky_lanes(row, scratch, ccd_at, fibre):
    scratch[...] = jnp.zeros((SUB, LANES), jnp.int32)
    scratch[0:1, 0 : row.shape[1]] = row
    listed = jnp.broadcast_to(scratch[0:1, :], (SUB, LANES))
    return (lanes_of() & HALF) + pick(listed, fibre + ccd_at * SKYC) - ccd_at * FC


def banded(res_ref, res_s):
    res_s[...] = jnp.zeros((BAND, SUB, LANES), f32)
    for d in range(BAND):
        res_s[d, :, 0:FC] = res_ref[d, 0:SUB, :]
        res_s[d, :, HALF : HALF + FC] = res_ref[d, SUB:CHUNK, :]
    return [res_s[d] for d in range(BAND)]


def turned_basis(basis_ref, basis_s, turned_s, exp_at):
    basis_s[...] = jnp.zeros((16, 640), f32)
    basis_s[0:COMP, 0:528] = basis_ref[...]
    tile = exp_at // 8
    offset = CHUNK * (exp_at % 8)
    near = basis_s[:, pl.ds(pl.multiple_of(tile * LANES, LANES), LANES)]
    far = basis_s[:, pl.ds(pl.multiple_of(tile * LANES + LANES, LANES), LANES)]
    turn = (LANES - offset) % LANES
    wide = lanes_of((16, LANES))
    window = jnp.where(wide < LANES - offset, pltpu.roll(near, turn, 1), pltpu.roll(far, turn, 1))
    turned_s[...] = jnp.transpose(jnp.concatenate([window, jnp.zeros((LANES - 16, LANES), f32)], axis=0))[0:32]


def tap_of(t, bands, masks):
    tap = jnp.zeros((SUB, LANES), f32)
    for s in range(2 * SHIFT + 1):
        if 0 <= t - s < BAND:
            tap = jnp.where(masks[s], bands[t - s], tap)
    return tap


def basis_at(t, turned_s):
    upper = turned_s[t : t + SUB, :]
    lower = turned_s[t + SUB : t + 2 * SUB, :]
    return jnp.where(lanes_of() < HALF, upper, pltpu.roll(lower, HALF, 1))


def sky_kernel(res_h, basis_h, shift_h, sky_h, slot_h, pix_h, send_ref, near_ref, far_ref, bands_ref, turned_ref, table_ref, res_v, basis_v, shift_v, sky_v, slot_v, basis_s, row_s, sems):
    exp_at = lax.axis_index("exp")
    ccd_at = lax.axis_index("ccd")
    odd = ccd_at % 2
    at_near = pl.multiple_of(odd * (LOCAL - EDGE), EDGE)
    at_far = pl.multiple_of((1 - odd) * (LOCAL - EDGE), EDGE)
    copies = [
        pltpu.make_async_copy(source, target, sems.at[i])
        for i, (source, target) in enumerate(
            (
                (sky_h, sky_v),
                (shift_h, shift_v),
                (res_h, res_v),
                (basis_h, basis_v),
                (slot_h, slot_v),
                (pix_h.at[pl.ds(at_near, EDGE), :], near_ref),
                (pix_h.at[pl.ds(at_far, EDGE), :], far_ref),
            )
        )
    ]
    for copy in copies:
        copy.start()
    for copy in copies[:4]:
        copy.wait()
    lane = lanes_of()
    fibre, comp, valid = sky_index(lane)
    sky = sky_lanes(sky_v[...], row_s, ccd_at, fibre)
    shift = doubled(shift_v[...], row_s) + SHIFT
    table_ref[0] = sky
    table_ref[1] = shift
    shift = pick(shift, sky)
    masks = [shift == s for s in range(2 * SHIFT + 1)]
    bands = [pick(band, sky) for band in banded(res_v, bands_ref)]
    turned_basis(basis_v, basis_s, turned_ref, exp_at)
    total = jnp.zeros((SUB, LANES), f32)
    for t in range(TAPS):
        total = total + tap_of(t, bands, masks) * pick(basis_at(t, turned_ref), (lane & HALF) + comp)
    total = jnp.where(valid, total, 0.0)
    send_ref[...] = jnp.broadcast_to(total[None], (EXPOS, SUB, LANES))
    for copy in copies[4:]:
        copy.wait()
    table_ref[2] = doubled(slot_v[...], row_s)


def model_kernel(bands_ref, turned_ref, table_ref, model_ref, picks_ref, same_ref, select_ref):
    ccd_at = lax.axis_index("ccd")
    lane = lanes_of()
    sky, shift = table_ref[0], table_ref[1]
    masks = [shift == s for s in range(2 * SHIFT + 1)]
    bands = [bands_ref[d] for d in range(BAND)]
    totals = [jnp.zeros((SUB, LANES), f32) for _ in range(COMP)]
    for t in range(TAPS):
        tap = tap_of(t, bands, masks)
        both = basis_at(t, turned_ref)
        for k in range(COMP):
            totals[k] = totals[k] + tap * pick(both, (lane & HALF) + k)
    model_ref[...] = jnp.zeros((16, SUB * LANES), f32)
    for k in range(COMP):
        for j in range(SUB):
            model_ref[k : k + 1, j * LANES : (j + 1) * LANES] = totals[k][j : j + 1, :]
    slot = table_ref[2]
    slot = jnp.where((lane & (HALF - 1)) < FC, slot - ccd_at * FC, 0)
    place = jnp.where(slot >= FIBBLK, slot + (32 - FIBBLK), slot)
    picks_ref[0] = sky
    picks_ref[1] = place
    picks_ref[2] = pick(place, sky)
    shape = (LANES, LANES)
    row, col = lanes_of(shape, 0), lanes_of(shape, 1)
    fibre_r, _, valid_r = sky_index(row)
    fibre_c, comp_c, valid_c = sky_index(col)
    same = (fibre_r == fibre_c) & ((row & HALF) == (col & HALF)) & valid_r & valid_c
    same_ref[...] = jnp.where(same, 1.0, 0.0)
    select_ref[...] = jnp.where((row == comp_c) & valid_c, 1.0, 0.0)


def extract_kernel(pix_ref, near_ref, psf_ref, flux_ref, vari_ref, pix_s, var_s):
    odd = lax.axis_index("ccd") % 2
    far = pl.ds(pl.multiple_of((1 - odd) * (EDGE + LOCAL), EDGE), EDGE)
    pix_s[pl.ds(pl.multiple_of(odd * (EDGE + LOCAL), EDGE), EDGE), :] = near_ref[...]
    pix_s[EDGE : EDGE + LOCAL, :] = pix_ref[...]
    pix_s[far, :] = jnp.zeros((EDGE, LANES), jnp.bfloat16)
    var_s[...] = variance_of(pix_s[...])
    var_s[far, :] = jnp.zeros((EDGE, LANES), jnp.bfloat16)
    for b in range(2):
        lower = b * BPIX * ROWS
        psf = psf_ref[b]
        flux_ref[b] = jnp.dot(psf, pix_s[lower : lower + DEPTH, :], preferred_element_type=f32)
        vari_ref[b] = jnp.dot(squared(psf), var_s[lower : lower + DEPTH, :], preferred_element_type=f32)


def variance_of(x):
    return (0.25 + jnp.square(x.astype(f32))).astype(jnp.bfloat16)


def squared(x):
    return jnp.square(x.astype(f32)).astype(jnp.bfloat16)


def gram_kernel(picks_ref, same_ref, select_ref, far_ref, psf_ref, flux_in, vari_in, model_ref, flux_ref, out_ref, edge_s, extra_s, pad_s, rows_s, flux_s, vari_s, weighted_s):
    odd = lax.axis_index("ccd") % 2
    lane = lanes_of()
    rows_s[...] = jnp.zeros((2, 2, LANES, LANES), f32)
    edge_s[0, 0:TAIL, :] = jnp.zeros((TAIL, LANES), jnp.bfloat16)
    edge_s[1, 0:TAIL, :] = jnp.zeros((TAIL, LANES), jnp.bfloat16)
    edge_s[0, TAIL : TAIL + EDGE, :] = far_ref[...]
    edge_s[1, TAIL : TAIL + EDGE, :] = variance_of(far_ref[...])

    @pl.when(odd == 1)
    def first_block():
        psf = psf_ref[0, :, 0:EDGE]
        extra_s[0] = jnp.dot(psf, edge_s[0, TAIL : TAIL + EDGE, :], preferred_element_type=f32)
        extra_s[1] = jnp.dot(squared(psf), edge_s[1, TAIL : TAIL + EDGE, :], preferred_element_type=f32)

    @pl.when(odd == 0)
    def second_block():
        psf = psf_ref[1, :, DEPTH - EDGE - TAIL : DEPTH]
        extra_s[0] = jnp.dot(psf, edge_s[0], preferred_element_type=f32)
        extra_s[1] = jnp.dot(squared(psf), edge_s[1], preferred_element_type=f32)

    for b in range(2):
        for q, part in enumerate((flux_in, vari_in)):
            pad_s[b, q] = part[b] + jnp.where(odd == 1 - b, extra_s[q], 0.0)
            for r in range(ROWS):
                at = (r % 2) * HALF + b * 32
                rows_s[q, r // 2, at : at + FIBBLK, :] = pad_s[b, q, pl.ds(r, FIBBLK, stride=ROWS), :]
    for half in range(2):
        flux_s[half] = jnp.transpose(rows_s[0, half])
        vari_s[half] = jnp.transpose(rows_s[1, half])
    _, _, valid = sky_index(lane)
    used = (lane & (HALF - 1)) < FC
    sky, place, sky_place = picks_ref[0], picks_ref[1], picks_ref[2]

    def gathered(ref, row, spot):
        upper = pick(ref[row : row + SUB, :], spot)
        lower = pick(ref[row + SUB : row + 2 * SUB, :], spot)
        return jnp.where(lane < HALF, upper, lower)

    target = jnp.zeros((SUB, LANES), f32)
    for r in range(ROWS):
        half, turn = r // 2, (r % 2) * HALF
        for m in range(GROUPS // CHUNK):
            e = r * 8 + m
            flux = jnp.where(used, gathered(flux_s.at[half], m * CHUNK, place + turn), 0.0)
            flux_ref[e] = flux
            vari = gathered(vari_s.at[half], m * CHUNK, sky_place + turn)
            weighted = jnp.where(valid, model_ref[e] / vari, 0.0)
            weighted_s[e * SUB : (e + 1) * SUB, :] = weighted
            target = target + weighted * pick(flux, sky)
    target = jnp.sum(target, axis=0, keepdims=True)
    model = model_ref[...].reshape(EXPOS * SUB, LANES)
    square = lax.dot_general(weighted_s[...], model, (((0,), (0,)), ((), ())), precision=highest, preferred_element_type=f32)
    square = square * same_ref[...]
    select = select_ref[...]
    summed = jnp.dot(select[0:16], square, precision=highest, preferred_element_type=f32)
    summed = jnp.where(lanes_of((16, LANES), 0) == COMP, target, summed)
    full = lax.dot_general(summed, select, (((1,), (1,)), ((), ())), precision=highest, preferred_element_type=f32)
    tile = full[0:SUB] + pltpu.roll(full[SUB : 2 * SUB], HALF, 1)
    out_ref[...] = jnp.broadcast_to(tile[None], out_ref.shape)


def solve_kernel(parts_ref, flux_ref, out_ref):
    total = jnp.sum(parts_ref[...], axis=0)
    system = jnp.concatenate([total, pltpu.roll(total, HALF, 1)], axis=0)
    col = lanes_of((16, LANES))
    row = lanes_of((16, LANES), 0)
    system = jnp.where((col < COMP) & (row <= COMP), system, 0.0)
    for k in range(0, COMP, 2):
        left = pick(system, jnp.full((16, LANES), k, jnp.int32))
        right = pick(system, jnp.full((16, LANES), k + 1, jnp.int32))
        upper = system[k : k + 1, :] - jnp.where(col[0:1] == k, 1.0, 0.0)
        lower = system[k + 1 : k + 2, :] - jnp.where(col[0:1] == k + 1, 1.0, 0.0)
        a, b = left[k : k + 1, :], right[k : k + 1, :]
        c, d = left[k + 1 : k + 2, :], right[k + 1 : k + 2, :]
        scale = 1.0 / (a * d - b * c)
        system = system - left * ((d * upper - b * lower) * scale) - right * ((a * lower - c * upper) * scale)
    coeffs = jnp.broadcast_to(system[COMP : COMP + 1, :], (SUB, LANES))
    coeffs = pltpu.roll(coeffs, FC, 1)
    lane = lanes_of()
    here = (lane >= FC) & (lane < FC + COMP)
    for e in range(EXPOS):
        out_ref[e] = jnp.where(here, coeffs, flux_ref[e])


def subtract_kernel(flux_ref, model_ref, out_h, noise_h, sky_s, left_s, out_s, noise_s, sems):
    heads = flux_ref[pl.ds(0, EXPOS, stride=SUB), :]
    coeffs = pltpu.roll(heads, LANES - FC, 1)
    coeffs = jnp.where(lanes_of((EXPOS, LANES)) < COMP, coeffs, 0.0)[:, 0:16]
    sky = jnp.dot(coeffs, model_ref[...], precision=highest, preferred_element_type=f32)
    for j in range(SUB):
        sky_s[pl.ds(j, EXPOS, stride=SUB), :] = sky[:, j * LANES : (j + 1) * LANES]
    total = jnp.zeros((SUB, LANES), f32)
    copies = []
    for e in range(EXPOS):
        at = slice(e * SUB, (e + 1) * SUB)
        left = flux_ref[at, :] - sky_s[at, :]
        left_s[at, :] = left
        total = total + left
        out_s[e, 0:SUB, :] = left[:, 0:FC]
        out_s[e, SUB:CHUNK, :] = pltpu.roll(left, HALF, 1)[:, 0:FC]
        if e % PIECE == PIECE - 1:
            part = pl.ds(e + 1 - PIECE, PIECE)
            copies.append(pltpu.make_async_copy(out_s.at[part], out_h.at[part], sems.at[e // PIECE]))
            copies[-1].start()
    mean = total * (1.0 / EXPOS)
    spread = jnp.zeros((SUB, LANES), f32)
    for e in range(EXPOS):
        spread = spread + jnp.square(left_s[e * SUB : (e + 1) * SUB, :] - mean)
    noise = jnp.sqrt(spread * (1.0 / EXPOS) + 1e-06)
    noise_s[0:SUB, :] = noise[:, 0:FC]
    noise_s[SUB:CHUNK, :] = pltpu.roll(noise, HALF, 1)[:, 0:FC]
    copies.append(pltpu.make_async_copy(noise_s, noise_h, sems.at[EXPOS // PIECE]))
    copies[-1].start()
    for copy in copies:
        copy.wait()


VMEM = pl.BlockSpec(memory_space=pltpu.VMEM)
HBM = pl.BlockSpec(memory_space=pltpu.HBM)
TILES = jax.ShapeDtypeStruct((EXPOS, SUB, LANES), f32)
EDGES = jax.ShapeDtypeStruct((EDGE, GROUPS), jnp.bfloat16)
PARAMS = pltpu.CompilerParams(vmem_limit_bytes=40 * 1024 * 1024)
BANDS = jax.ShapeDtypeStruct((BAND, SUB, LANES), f32)
SQUARE = jax.ShapeDtypeStruct((LANES, LANES), f32)


def sky_model(*arrays):
    return pl.pallas_call(
        sky_kernel,
        out_shape=(
            TILES,
            EDGES,
            EDGES,
            BANDS,
            jax.ShapeDtypeStruct((32, LANES), f32),
            jax.ShapeDtypeStruct((3, SUB, LANES), jnp.int32),
        ),
        in_specs=[HBM] * 6,
        out_specs=(VMEM,) * 6,
        scratch_shapes=[
            pltpu.VMEM((BAND, CHUNK, FC), f32),
            pltpu.VMEM((COMP, 528), f32),
            pltpu.VMEM((1, FC), jnp.int32),
            pltpu.VMEM((1, 96), jnp.int32),
            pltpu.VMEM((1, FC), jnp.int32),
            pltpu.VMEM((16, 640), f32),
            pltpu.VMEM((SUB, LANES), jnp.int32),
            pltpu.SemaphoreType.DMA((7,)),
        ],
        compiler_params=PARAMS,
        name="sky_model",
    )(*(pltpu.with_memory_space_constraint(v, pltpu.HBM) for v in arrays))


def local_model(bands, turned, table):
    return pl.pallas_call(
        model_kernel,
        out_shape=(
            jax.ShapeDtypeStruct((16, SUB * LANES), f32),
            jax.ShapeDtypeStruct((3, SUB, LANES), jnp.int32),
            SQUARE,
            SQUARE,
        ),
        in_specs=[VMEM] * 3,
        out_specs=(VMEM,) * 4,
        compiler_params=PARAMS,
        name="local_model",
    )(bands, turned, table)


def extract(pixels, near, psf):
    part = jax.ShapeDtypeStruct((2, FIBBLK * ROWS, LANES), f32)
    return pl.pallas_call(
        extract_kernel,
        out_shape=(part, part),
        in_specs=[VMEM] * 3,
        out_specs=(VMEM, VMEM),
        scratch_shapes=[
            pltpu.VMEM((2 * EDGE + LOCAL, LANES), jnp.bfloat16),
            pltpu.VMEM((2 * EDGE + LOCAL, LANES), jnp.bfloat16),
        ],
        compiler_params=PARAMS,
        name="extract",
    )(pixels, near, psf)


def gram_parts(tables, far, psf, flux, vari, model, copies):
    return pl.pallas_call(
        gram_kernel,
        out_shape=(TILES, jax.ShapeDtypeStruct((copies, SUB, LANES), f32)),
        in_specs=[VMEM] * 8,
        out_specs=(VMEM, VMEM),
        scratch_shapes=[
            pltpu.VMEM((2, TAIL + EDGE, LANES), jnp.bfloat16),
            pltpu.VMEM((2, FIBBLK * ROWS, LANES), f32),
            pltpu.VMEM((2, 2, FIBBLK * ROWS, LANES), f32),
            pltpu.VMEM((2, 2, LANES, LANES), f32),
            pltpu.VMEM((2, LANES, LANES), f32),
            pltpu.VMEM((2, LANES, LANES), f32),
            pltpu.VMEM((EXPOS * SUB, LANES), f32),
        ],
        compiler_params=PARAMS,
        name="gram",
    )(*tables, far, psf, flux, vari, model)


def solve(parts, flux):
    return pl.pallas_call(
        solve_kernel, out_shape=TILES, in_specs=[VMEM, VMEM], out_specs=VMEM, compiler_params=PARAMS, name="solve"
    )(parts, flux)


def subtract(flux, model):
    return pl.pallas_call(
        subtract_kernel,
        out_shape=(jax.ShapeDtypeStruct((EXPOS, CHUNK, FC), f32), jax.ShapeDtypeStruct((CHUNK, FC), f32)),
        in_specs=[VMEM, VMEM],
        out_specs=(HBM, HBM),
        scratch_shapes=[
            pltpu.VMEM((EXPOS * SUB, LANES), f32),
            pltpu.VMEM((EXPOS * SUB, LANES), f32),
            pltpu.VMEM((EXPOS, CHUNK, FC), f32),
            pltpu.VMEM((CHUNK, FC), f32),
            pltpu.SemaphoreType.DMA((EXPOS // PIECE + 1,)),
        ],
        compiler_params=PARAMS,
        name="subtract",
    )(flux.reshape(EXPOS * SUB, LANES), model)


def shards(pixels, psf_proj, resolution, basis, sky_fibres, fibre_slot, band_shift):
    size = lax.axis_size("ccd")
    rows = pixels.reshape(LOCAL, GROUPS)
    res = resolution.transpose(1, 2, 0)
    sky = sky_fibres.reshape(1, -1)
    slot = fibre_slot.reshape(1, FC)
    shift = band_shift.reshape(1, FC)
    pairs = [[(i, i + 1) for i in range(start, size - 1, 2)] for start in (1, 0)]
    swaps = [[*pair, *((j, i) for i, j in pair)] for pair in pairs]
    send, near, far, *prepared = sky_model(res, basis, shift, sky, slot, rows)
    near = lax.ppermute(near, "ccd", swaps[0])
    far = lax.ppermute(far, "ccd", swaps[1])
    model, *tables = local_model(*prepared)
    part, vari = extract(rows, near, psf_proj)
    far, model, tables, part, vari = lax.optimization_barrier((far, model, tables, part, vari))
    sky_tiles = lax.all_to_all(send, "exp", split_axis=0, concat_axis=0, tiled=True)
    flux, parts = gram_parts(tables, far, psf_proj, part, vari, sky_tiles, size)
    parts = lax.all_to_all(parts, "ccd", split_axis=0, concat_axis=0, tiled=True)
    flux = solve(parts, flux)
    flux = lax.all_to_all(flux, "exp", split_axis=0, concat_axis=0, tiled=True)
    sky_subtracted, noise_rms = subtract(flux, model)
    return (sky_subtracted.transpose(0, 2, 1), noise_rms.transpose(1, 0))


def solution(mesh):
    in_specs = (
        P("exp", "ccd", None, None),
        P("ccd", None, None),
        P("ccd", None, "exp"),
        P(),
        P(),
        P("ccd"),
        P("ccd"),
    )
    out_specs = (P(None, "ccd", "exp"), P("ccd", "exp"))
    return jax.shard_map(shards, mesh=mesh, in_specs=in_specs, out_specs=out_specs, check_vma=False)
```

```python
import jax
import jax.numpy as jnp
from jax import lax
from jax.experimental import pallas as pl
from jax.experimental.pallas import tpu as pltpu
from jax.sharding import PartitionSpec as P

BPIX = 500
MARG = 20
ROWS = 4
COMP = 10
BAND = 11
SHIFT = 3
FIBBLK = 25
FC = 50
SPAN = 540
SKYC = 6
EXPOS = 32
PIECE = 16
CHUNK = 16
GROUPS = 128
LANES = 128
HALF = 64
SUB = 8
TAPS = BAND + 2 * SHIFT
EDGE = MARG * ROWS
DEPTH = SPAN * ROWS
TAIL = 32
LOCAL = 2 * BPIX * ROWS


f32 = jnp.float32
highest = lax.Precision.HIGHEST


def lanes_of(shape=(SUB, LANES), dim=1):
    return lax.broadcasted_iota(jnp.int32, shape, dim)


def sky_index(lane):
    within = lane & (HALF - 1)
    fibre = jnp.zeros_like(within)
    for i in range(1, SKYC):
        fibre = fibre + jnp.where(within >= i * COMP, 1, 0)
    comp = within - fibre * COMP
    valid = within < SKYC * COMP
    return fibre, comp, valid


def pick(x, idx):
    return jnp.take_along_axis(x, idx, axis=1, mode="promise_in_bounds")


def doubled(row, scratch):
    scratch[...] = jnp.zeros((SUB, LANES), jnp.int32)
    scratch[0:1, 0:FC] = row
    scratch[0:1, HALF : HALF + FC] = row
    return jnp.broadcast_to(scratch[0:1, :], (SUB, LANES))


def sky_lanes(row, scratch, ccd_at, fibre):
    scratch[...] = jnp.zeros((SUB, LANES), jnp.int32)
    scratch[0:1, 0 : row.shape[1]] = row
    listed = jnp.broadcast_to(scratch[0:1, :], (SUB, LANES))
    return (lanes_of() & HALF) + pick(listed, fibre + ccd_at * SKYC) - ccd_at * FC


def banded(res_ref, res_s):
    res_s[...] = jnp.zeros((BAND, SUB, LANES), f32)
    for d in range(BAND):
        res_s[d, :, 0:FC] = res_ref[d, 0:SUB, :]
        res_s[d, :, HALF : HALF + FC] = res_ref[d, SUB:CHUNK, :]
    return [res_s[d] for d in range(BAND)]


def turned_basis(basis_ref, basis_s, turned_s, exp_at):
    basis_s[...] = jnp.zeros((16, 640), f32)
    basis_s[0:COMP, 0:528] = basis_ref[...]
    tile = exp_at // 8
    offset = CHUNK * (exp_at % 8)
    near = basis_s[:, pl.ds(pl.multiple_of(tile * LANES, LANES), LANES)]
    far = basis_s[:, pl.ds(pl.multiple_of(tile * LANES + LANES, LANES), LANES)]
    turn = (LANES - offset) % LANES
    wide = lanes_of((16, LANES))
    window = jnp.where(wide < LANES - offset, pltpu.roll(near, turn, 1), pltpu.roll(far, turn, 1))
    turned_s[...] = jnp.transpose(jnp.concatenate([window, jnp.zeros((LANES - 16, LANES), f32)], axis=0))[0:32]


def tap_of(t, bands, masks):
    tap = jnp.zeros((SUB, LANES), f32)
    for s in range(2 * SHIFT + 1):
        if 0 <= t - s < BAND:
            tap = jnp.where(masks[s], bands[t - s], tap)
    return tap


def basis_at(t, turned_s):
    upper = turned_s[t : t + SUB, :]
    lower = turned_s[t + SUB : t + 2 * SUB, :]
    return jnp.where(lanes_of() < HALF, upper, pltpu.roll(lower, HALF, 1))


def sky_kernel(res_h, basis_h, shift_h, sky_h, slot_h, pix_h, send_ref, near_ref, far_ref, bands_ref, turned_ref, table_ref, res_v, basis_v, shift_v, sky_v, slot_v, basis_s, row_s, sems):
    exp_at = lax.axis_index("exp")
    ccd_at = lax.axis_index("ccd")
    odd = ccd_at % 2
    at_near = pl.multiple_of(odd * (LOCAL - EDGE), EDGE)
    at_far = pl.multiple_of((1 - odd) * (LOCAL - EDGE), EDGE)
    moves = {
        "res": (res_h, res_v),
        "basis": (basis_h, basis_v),
        "sky": (sky_h, sky_v),
        "shift": (shift_h, shift_v),
        "slot": (slot_h, slot_v),
        "near": (pix_h.at[pl.ds(at_near, EDGE), :], near_ref),
        "far": (pix_h.at[pl.ds(at_far, EDGE), :], far_ref),
    }
    copies = {name: pltpu.make_async_copy(*move, sems.at[i]) for i, (name, move) in enumerate(moves.items())}
    for copy in copies.values():
        copy.start()
    lane = lanes_of()
    fibre, comp, valid = sky_index(lane)
    copies["sky"].wait()
    copies["shift"].wait()
    copies["slot"].wait()
    sky = sky_lanes(sky_v[...], row_s, ccd_at, fibre)
    shift = doubled(shift_v[...], row_s) + SHIFT
    table_ref[0] = sky
    table_ref[1] = shift
    table_ref[2] = doubled(slot_v[...], row_s)
    shift = pick(shift, sky)
    masks = [shift == s for s in range(2 * SHIFT + 1)]
    copies["basis"].wait()
    turned_basis(basis_v, basis_s, turned_ref, exp_at)
    copies["res"].wait()
    bands = [pick(band, sky) for band in banded(res_v, bands_ref)]
    total = jnp.zeros((SUB, LANES), f32)
    for t in range(TAPS):
        total = total + tap_of(t, bands, masks) * pick(basis_at(t, turned_ref), (lane & HALF) + comp)
    total = jnp.where(valid, total, 0.0)
    send_ref[...] = jnp.broadcast_to(total[None], (EXPOS, SUB, LANES))
    copies["near"].wait()
    copies["far"].wait()


def model_kernel(bands_ref, turned_ref, table_ref, model_ref, picks_ref, same_ref, select_ref):
    ccd_at = lax.axis_index("ccd")
    lane = lanes_of()
    sky, shift = table_ref[0], table_ref[1]
    masks = [shift == s for s in range(2 * SHIFT + 1)]
    bands = [bands_ref[d] for d in range(BAND)]
    totals = [jnp.zeros((SUB, LANES), f32) for _ in range(COMP)]
    for t in range(TAPS):
        tap = tap_of(t, bands, masks)
        both = basis_at(t, turned_ref)
        for k in range(COMP):
            totals[k] = totals[k] + tap * pick(both, (lane & HALF) + k)
    model_ref[...] = jnp.zeros((16, SUB * LANES), f32)
    for k in range(COMP):
        for j in range(SUB):
            model_ref[k : k + 1, j * LANES : (j + 1) * LANES] = totals[k][j : j + 1, :]
    slot = table_ref[2]
    slot = jnp.where((lane & (HALF - 1)) < FC, slot - ccd_at * FC, 0)
    place = jnp.where(slot >= FIBBLK, slot + (32 - FIBBLK), slot)
    picks_ref[0] = sky
    picks_ref[1] = place
    picks_ref[2] = pick(place, sky)
    shape = (LANES, LANES)
    row, col = lanes_of(shape, 0), lanes_of(shape, 1)
    fibre_r, _, valid_r = sky_index(row)
    fibre_c, comp_c, valid_c = sky_index(col)
    same = (fibre_r == fibre_c) & ((row & HALF) == (col & HALF)) & valid_r & valid_c
    same_ref[...] = jnp.where(same, 1.0, 0.0)
    select_ref[...] = jnp.where((row == comp_c) & valid_c, 1.0, 0.0).astype(jnp.bfloat16)


def extract_kernel(pix_ref, near_ref, psf_ref, flux_ref, vari_ref, pix_s, var_s):
    odd = lax.axis_index("ccd") % 2
    far = pl.ds(pl.multiple_of((1 - odd) * (EDGE + LOCAL), EDGE), EDGE)
    pix_s[pl.ds(pl.multiple_of(odd * (EDGE + LOCAL), EDGE), EDGE), :] = near_ref[...]
    pix_s[EDGE : EDGE + LOCAL, :] = pix_ref[...]
    pix_s[far, :] = jnp.zeros((EDGE, LANES), jnp.bfloat16)
    var_s[...] = variance_of(pix_s[...])
    var_s[far, :] = jnp.zeros((EDGE, LANES), jnp.bfloat16)
    for b in range(2):
        lower = b * BPIX * ROWS
        psf = psf_ref[b]
        flux_ref[b] = jnp.dot(psf, pix_s[lower : lower + DEPTH, :], preferred_element_type=f32)
        vari_ref[b] = jnp.dot(squared(psf), var_s[lower : lower + DEPTH, :], preferred_element_type=f32)


def variance_of(x):
    return (0.25 + jnp.square(x.astype(f32))).astype(jnp.bfloat16)


def squared(x):
    return jnp.square(x.astype(f32)).astype(jnp.bfloat16)


def split(x):
    high = x.astype(jnp.bfloat16)
    rest = x - high.astype(f32)
    middle = rest.astype(jnp.bfloat16)
    return high, middle, (rest - middle.astype(f32)).astype(jnp.bfloat16)


def gram_kernel(picks_ref, same_ref, select_ref, far_ref, psf_ref, flux_in, vari_in, model_ref, flux_ref, out_ref, edge_s, extra_s, pad_s, rows_s, flux_s, vari_s, weighted_s):
    odd = lax.axis_index("ccd") % 2
    lane = lanes_of()
    rows_s[...] = jnp.zeros((2, 2, LANES, LANES), f32)
    edge_s[0, 0:TAIL, :] = jnp.zeros((TAIL, LANES), jnp.bfloat16)
    edge_s[1, 0:TAIL, :] = jnp.zeros((TAIL, LANES), jnp.bfloat16)
    edge_s[0, TAIL : TAIL + EDGE, :] = far_ref[...]
    edge_s[1, TAIL : TAIL + EDGE, :] = variance_of(far_ref[...])

    @pl.when(odd == 1)
    def first_block():
        psf = psf_ref[0, :, 0:EDGE]
        extra_s[0] = jnp.dot(psf, edge_s[0, TAIL : TAIL + EDGE, :], preferred_element_type=f32)
        extra_s[1] = jnp.dot(squared(psf), edge_s[1, TAIL : TAIL + EDGE, :], preferred_element_type=f32)

    @pl.when(odd == 0)
    def second_block():
        psf = psf_ref[1, :, DEPTH - EDGE - TAIL : DEPTH]
        extra_s[0] = jnp.dot(psf, edge_s[0], preferred_element_type=f32)
        extra_s[1] = jnp.dot(squared(psf), edge_s[1], preferred_element_type=f32)

    for b in range(2):
        for q, part in enumerate((flux_in, vari_in)):
            pad_s[b, q] = part[b] + jnp.where(odd == 1 - b, extra_s[q], 0.0)
            for r in range(ROWS):
                at = (r % 2) * HALF + b * 32
                rows_s[q, r // 2, at : at + FIBBLK, :] = pad_s[b, q, pl.ds(r, FIBBLK, stride=ROWS), :]
    for half in range(2):
        flux_s[half] = jnp.transpose(rows_s[0, half])
        vari_s[half] = jnp.transpose(rows_s[1, half])
    _, _, valid = sky_index(lane)
    used = (lane & (HALF - 1)) < FC
    sky, place, sky_place = picks_ref[0], picks_ref[1], picks_ref[2]

    def gathered(ref, row, spot):
        upper = pick(ref[row : row + SUB, :], spot)
        lower = pick(ref[row + SUB : row + 2 * SUB, :], spot)
        return jnp.where(lane < HALF, upper, lower)

    target = jnp.zeros((SUB, LANES), f32)
    for r in range(ROWS):
        half, turn = r // 2, (r % 2) * HALF
        for m in range(GROUPS // CHUNK):
            e = r * 8 + m
            flux = jnp.where(used, gathered(flux_s.at[half], m * CHUNK, place + turn), 0.0)
            flux_ref[e] = flux
            vari = gathered(vari_s.at[half], m * CHUNK, sky_place + turn)
            weighted = jnp.where(valid, model_ref[e] / vari, 0.0)
            weighted_s[e * SUB : (e + 1) * SUB, :] = weighted
            target = target + weighted * pick(flux, sky)
    target = jnp.sum(target, axis=0, keepdims=True)
    model = model_ref[...].reshape(EXPOS * SUB, LANES)
    square = lax.dot_general(weighted_s[...], model, (((0,), (0,)), ((), ())), precision=highest, preferred_element_type=f32)
    square = square * same_ref[...]
    select = select_ref[...]
    summed = sum(jnp.dot(select[0:16], piece, preferred_element_type=f32) for piece in split(square))
    summed = jnp.where(lanes_of((16, LANES), 0) == COMP, target, summed)
    turned = (((1,), (1,)), ((), ()))
    full = sum(lax.dot_general(piece, select, turned, preferred_element_type=f32) for piece in split(summed))
    tile = full[0:SUB] + pltpu.roll(full[SUB : 2 * SUB], HALF, 1)
    out_ref[...] = jnp.broadcast_to(tile[None], out_ref.shape)


def solve_kernel(parts_ref, flux_ref, out_ref):
    total = jnp.sum(parts_ref[...], axis=0)
    system = jnp.concatenate([total, pltpu.roll(total, HALF, 1)], axis=0)
    col = lanes_of((16, LANES))
    row = lanes_of((16, LANES), 0)
    system = jnp.where((col < COMP) & (row <= COMP), system, 0.0)
    for k in range(0, COMP, 2):
        left = pick(system, jnp.full((16, LANES), k, jnp.int32))
        right = pick(system, jnp.full((16, LANES), k + 1, jnp.int32))
        upper = system[k : k + 1, :] - jnp.where(col[0:1] == k, 1.0, 0.0)
        lower = system[k + 1 : k + 2, :] - jnp.where(col[0:1] == k + 1, 1.0, 0.0)
        a, b = left[k : k + 1, :], right[k : k + 1, :]
        c, d = left[k + 1 : k + 2, :], right[k + 1 : k + 2, :]
        scale = 1.0 / (a * d - b * c)
        system = system - left * ((d * upper - b * lower) * scale) - right * ((a * lower - c * upper) * scale)
    coeffs = jnp.broadcast_to(system[COMP : COMP + 1, :], (SUB, LANES))
    coeffs = pltpu.roll(coeffs, FC, 1)
    lane = lanes_of()
    here = (lane >= FC) & (lane < FC + COMP)
    for e in range(EXPOS):
        out_ref[e] = jnp.where(here, coeffs, flux_ref[e])


def subtract_kernel(flux_ref, model_ref, out_h, noise_h, sky_s, left_s, out_s, noise_s, sems):
    heads = flux_ref[pl.ds(0, EXPOS, stride=SUB), :]
    coeffs = pltpu.roll(heads, LANES - FC, 1)
    coeffs = jnp.where(lanes_of((EXPOS, LANES)) < COMP, coeffs, 0.0)[:, 0:16]
    sky = jnp.dot(coeffs, model_ref[...], precision=highest, preferred_element_type=f32)
    for j in range(SUB):
        sky_s[pl.ds(j, EXPOS, stride=SUB), :] = sky[:, j * LANES : (j + 1) * LANES]
    total = jnp.zeros((SUB, LANES), f32)
    copies = []
    for e in range(EXPOS):
        at = slice(e * SUB, (e + 1) * SUB)
        left = flux_ref[at, :] - sky_s[at, :]
        left_s[at, :] = left
        total = total + left
        out_s[e, 0:SUB, :] = left[:, 0:FC]
        out_s[e, SUB:CHUNK, :] = pltpu.roll(left, HALF, 1)[:, 0:FC]
        if e % PIECE == PIECE - 1:
            part = pl.ds(e + 1 - PIECE, PIECE)
            copies.append(pltpu.make_async_copy(out_s.at[part], out_h.at[part], sems.at[e // PIECE]))
            copies[-1].start()
    mean = total * (1.0 / EXPOS)
    spread = jnp.zeros((SUB, LANES), f32)
    for e in range(EXPOS):
        spread = spread + jnp.square(left_s[e * SUB : (e + 1) * SUB, :] - mean)
    noise = jnp.sqrt(spread * (1.0 / EXPOS) + 1e-06)
    noise_s[0:SUB, :] = noise[:, 0:FC]
    noise_s[SUB:CHUNK, :] = pltpu.roll(noise, HALF, 1)[:, 0:FC]
    copies.append(pltpu.make_async_copy(noise_s, noise_h, sems.at[EXPOS // PIECE]))
    copies[-1].start()
    for copy in copies:
        copy.wait()


VMEM = pl.BlockSpec(memory_space=pltpu.VMEM)
HBM = pl.BlockSpec(memory_space=pltpu.HBM)
TILES = jax.ShapeDtypeStruct((EXPOS, SUB, LANES), f32)
EDGES = jax.ShapeDtypeStruct((EDGE, GROUPS), jnp.bfloat16)
PARAMS = pltpu.CompilerParams(vmem_limit_bytes=40 * 1024 * 1024)
BANDS = jax.ShapeDtypeStruct((BAND, SUB, LANES), f32)


def sky_model(*arrays):
    return pl.pallas_call(
        sky_kernel,
        out_shape=(
            TILES,
            EDGES,
            EDGES,
            BANDS,
            jax.ShapeDtypeStruct((32, LANES), f32),
            jax.ShapeDtypeStruct((3, SUB, LANES), jnp.int32),
        ),
        in_specs=[HBM] * 6,
        out_specs=(VMEM,) * 6,
        scratch_shapes=[
            pltpu.VMEM((BAND, CHUNK, FC), f32),
            pltpu.VMEM((COMP, 528), f32),
            pltpu.VMEM((1, FC), jnp.int32),
            pltpu.VMEM((1, 96), jnp.int32),
            pltpu.VMEM((1, FC), jnp.int32),
            pltpu.VMEM((16, 640), f32),
            pltpu.VMEM((SUB, LANES), jnp.int32),
            pltpu.SemaphoreType.DMA((7,)),
        ],
        compiler_params=PARAMS,
        name="sky_model",
    )(*(pltpu.with_memory_space_constraint(v, pltpu.HBM) for v in arrays))


def local_model(bands, turned, table):
    return pl.pallas_call(
        model_kernel,
        out_shape=(
            jax.ShapeDtypeStruct((16, SUB * LANES), f32),
            jax.ShapeDtypeStruct((3, SUB, LANES), jnp.int32),
            jax.ShapeDtypeStruct((LANES, LANES), f32),
            jax.ShapeDtypeStruct((LANES, LANES), jnp.bfloat16),
        ),
        in_specs=[VMEM] * 3,
        out_specs=(VMEM,) * 4,
        compiler_params=PARAMS,
        name="local_model",
    )(bands, turned, table)


def extract(pixels, near, psf):
    part = jax.ShapeDtypeStruct((2, FIBBLK * ROWS, LANES), f32)
    return pl.pallas_call(
        extract_kernel,
        out_shape=(part, part),
        in_specs=[VMEM] * 3,
        out_specs=(VMEM, VMEM),
        scratch_shapes=[
            pltpu.VMEM((2 * EDGE + LOCAL, LANES), jnp.bfloat16),
            pltpu.VMEM((2 * EDGE + LOCAL, LANES), jnp.bfloat16),
        ],
        compiler_params=PARAMS,
        name="extract",
    )(pixels, near, psf)


def gram_parts(tables, far, psf, flux, vari, model, copies):
    return pl.pallas_call(
        gram_kernel,
        out_shape=(TILES, jax.ShapeDtypeStruct((copies, SUB, LANES), f32)),
        in_specs=[VMEM] * 8,
        out_specs=(VMEM, VMEM),
        scratch_shapes=[
            pltpu.VMEM((2, TAIL + EDGE, LANES), jnp.bfloat16),
            pltpu.VMEM((2, FIBBLK * ROWS, LANES), f32),
            pltpu.VMEM((2, 2, FIBBLK * ROWS, LANES), f32),
            pltpu.VMEM((2, 2, LANES, LANES), f32),
            pltpu.VMEM((2, LANES, LANES), f32),
            pltpu.VMEM((2, LANES, LANES), f32),
            pltpu.VMEM((EXPOS * SUB, LANES), f32),
        ],
        compiler_params=PARAMS,
        name="gram",
    )(*tables, far, psf, flux, vari, model)


def solve(parts, flux):
    return pl.pallas_call(
        solve_kernel, out_shape=TILES, in_specs=[VMEM, VMEM], out_specs=VMEM, compiler_params=PARAMS, name="solve"
    )(parts, flux)


def subtract(flux, model):
    return pl.pallas_call(
        subtract_kernel,
        out_shape=(jax.ShapeDtypeStruct((EXPOS, CHUNK, FC), f32), jax.ShapeDtypeStruct((CHUNK, FC), f32)),
        in_specs=[VMEM, VMEM],
        out_specs=(HBM, HBM),
        scratch_shapes=[
            pltpu.VMEM((EXPOS * SUB, LANES), f32),
            pltpu.VMEM((EXPOS * SUB, LANES), f32),
            pltpu.VMEM((EXPOS, CHUNK, FC), f32),
            pltpu.VMEM((CHUNK, FC), f32),
            pltpu.SemaphoreType.DMA((EXPOS // PIECE + 1,)),
        ],
        compiler_params=PARAMS,
        name="subtract",
    )(flux.reshape(EXPOS * SUB, LANES), model)


def shards(pixels, psf_proj, resolution, basis, sky_fibres, fibre_slot, band_shift):
    size = lax.axis_size("ccd")
    rows = pixels.reshape(LOCAL, GROUPS)
    res = resolution.transpose(1, 2, 0)
    sky = sky_fibres.reshape(1, -1)
    slot = fibre_slot.reshape(1, FC)
    shift = band_shift.reshape(1, FC)
    pairs = [[(i, i + 1) for i in range(start, size - 1, 2)] for start in (1, 0)]
    swaps = [[*pair, *((j, i) for i, j in pair)] for pair in pairs]
    send, near, far, *prepared = sky_model(res, basis, shift, sky, slot, rows)
    near = lax.ppermute(near, "ccd", swaps[0])
    far = lax.ppermute(far, "ccd", swaps[1])
    model, *tables = local_model(*prepared)
    part, vari = extract(rows, near, psf_proj)
    far, model, tables, part, vari = lax.optimization_barrier((far, model, tables, part, vari))
    sky_tiles = lax.all_to_all(send, "exp", split_axis=0, concat_axis=0, tiled=True)
    flux, parts = gram_parts(tables, far, psf_proj, part, vari, sky_tiles, size)
    parts = lax.all_to_all(parts, "ccd", split_axis=0, concat_axis=0, tiled=True)
    flux = solve(parts, flux)
    flux = lax.all_to_all(flux, "exp", split_axis=0, concat_axis=0, tiled=True)
    sky_subtracted, noise_rms = subtract(flux, model)
    return (sky_subtracted.transpose(0, 2, 1), noise_rms.transpose(1, 0))


def solution(mesh):
    in_specs = (
        P("exp", "ccd", None, None),
        P("ccd", None, None),
        P("ccd", None, "exp"),
        P(),
        P(),
        P("ccd"),
        P("ccd"),
    )
    out_specs = (P(None, "ccd", "exp"), P("ccd", "exp"))
    return jax.shard_map(shards, mesh=mesh, in_specs=in_specs, out_specs=out_specs, check_vma=False)
```

```python
import jax
import jax.numpy as jnp
from jax import lax
from jax.experimental import pallas as pl
from jax.experimental.pallas import tpu as pltpu
from jax.sharding import PartitionSpec as P

BPIX = 500
MARG = 20
ROWS = 4
COMP = 10
BAND = 11
SHIFT = 3
FIBBLK = 25
FC = 50
SPAN = 540
SKYC = 6
EXPOS = 32
PIECE = 16
CHUNK = 16
GROUPS = 128
LANES = 128
HALF = 64
SUB = 8
TAPS = BAND + 2 * SHIFT
EDGE = MARG * ROWS
DEPTH = SPAN * ROWS
TAIL = 32
LOCAL = 2 * BPIX * ROWS


f32 = jnp.float32
highest = lax.Precision.HIGHEST


def lanes_of(shape=(SUB, LANES), dim=1):
    return lax.broadcasted_iota(jnp.int32, shape, dim)


def sky_index(lane):
    within = lane & (HALF - 1)
    fibre = jnp.zeros_like(within)
    for i in range(1, SKYC):
        fibre = fibre + jnp.where(within >= i * COMP, 1, 0)
    comp = within - fibre * COMP
    valid = within < SKYC * COMP
    return fibre, comp, valid


def pick(x, idx):
    return jnp.take_along_axis(x, idx, axis=1, mode="promise_in_bounds")


def doubled(row, scratch):
    scratch[...] = jnp.zeros((SUB, LANES), jnp.int32)
    scratch[0:1, 0:FC] = row
    scratch[0:1, HALF : HALF + FC] = row
    return jnp.broadcast_to(scratch[0:1, :], (SUB, LANES))


def sky_lanes(row, scratch, ccd_at, fibre):
    scratch[...] = jnp.zeros((SUB, LANES), jnp.int32)
    scratch[0:1, 0 : row.shape[1]] = row
    listed = jnp.broadcast_to(scratch[0:1, :], (SUB, LANES))
    return (lanes_of() & HALF) + pick(listed, fibre + ccd_at * SKYC) - ccd_at * FC


def banded(res_ref, res_s):
    res_s[...] = jnp.zeros((BAND, SUB, LANES), f32)
    for d in range(BAND):
        res_s[d, :, 0:FC] = res_ref[d, 0:SUB, :]
        res_s[d, :, HALF : HALF + FC] = res_ref[d, SUB:CHUNK, :]
    return [res_s[d] for d in range(BAND)]


def turned_basis(basis_ref, basis_s, turned_s, exp_at):
    basis_s[...] = jnp.zeros((16, 640), f32)
    basis_s[0:COMP, 0:528] = basis_ref[...]
    tile = exp_at // 8
    offset = CHUNK * (exp_at % 8)
    near = basis_s[:, pl.ds(pl.multiple_of(tile * LANES, LANES), LANES)]
    far = basis_s[:, pl.ds(pl.multiple_of(tile * LANES + LANES, LANES), LANES)]
    turn = (LANES - offset) % LANES
    wide = lanes_of((16, LANES))
    window = jnp.where(wide < LANES - offset, pltpu.roll(near, turn, 1), pltpu.roll(far, turn, 1))
    turned_s[...] = jnp.transpose(jnp.concatenate([window, jnp.zeros((LANES - 16, LANES), f32)], axis=0))[0:32]


def tap_of(t, bands, masks):
    tap = jnp.zeros((SUB, LANES), f32)
    for s in range(2 * SHIFT + 1):
        if 0 <= t - s < BAND:
            tap = jnp.where(masks[s], bands[t - s], tap)
    return tap


def basis_at(t, turned_s):
    upper = turned_s[t : t + SUB, :]
    lower = turned_s[t + SUB : t + 2 * SUB, :]
    return jnp.where(lanes_of() < HALF, upper, pltpu.roll(lower, HALF, 1))


def sky_kernel(res_h, basis_h, shift_h, sky_h, slot_h, pix_h, send_ref, near_ref, far_ref, bands_ref, turned_ref, table_ref, res_v, basis_v, shift_v, sky_v, slot_v, basis_s, row_s, sems):
    exp_at = lax.axis_index("exp")
    ccd_at = lax.axis_index("ccd")
    odd = ccd_at % 2
    at_near = pl.multiple_of(odd * (LOCAL - EDGE), EDGE)
    at_far = pl.multiple_of((1 - odd) * (LOCAL - EDGE), EDGE)
    moves = {
        "res": (res_h, res_v),
        "basis": (basis_h, basis_v),
        "sky": (sky_h, sky_v),
        "shift": (shift_h, shift_v),
        "slot": (slot_h, slot_v),
        "near": (pix_h.at[pl.ds(at_near, EDGE), :], near_ref),
        "far": (pix_h.at[pl.ds(at_far, EDGE), :], far_ref),
    }
    copies = {name: pltpu.make_async_copy(*move, sems.at[i]) for i, (name, move) in enumerate(moves.items())}
    for copy in copies.values():
        copy.start()
    lane = lanes_of()
    fibre, comp, valid = sky_index(lane)
    copies["sky"].wait()
    copies["shift"].wait()
    copies["slot"].wait()
    sky = sky_lanes(sky_v[...], row_s, ccd_at, fibre)
    shift = doubled(shift_v[...], row_s) + SHIFT
    table_ref[0] = sky
    table_ref[1] = shift
    table_ref[2] = doubled(slot_v[...], row_s)
    shift = pick(shift, sky)
    masks = [shift == s for s in range(2 * SHIFT + 1)]
    copies["basis"].wait()
    turned_basis(basis_v, basis_s, turned_ref, exp_at)
    copies["res"].wait()
    bands = [pick(band, sky) for band in banded(res_v, bands_ref)]
    total = jnp.zeros((SUB, LANES), f32)
    for t in range(TAPS):
        total = total + tap_of(t, bands, masks) * pick(basis_at(t, turned_ref), (lane & HALF) + comp)
    total = jnp.where(valid, total, 0.0)
    send_ref[...] = jnp.broadcast_to(total[None], (EXPOS, SUB, LANES))
    copies["near"].wait()
    copies["far"].wait()


def model_kernel(bands_ref, turned_ref, table_ref, model_ref, picks_ref, same_ref, select_ref):
    ccd_at = lax.axis_index("ccd")
    lane = lanes_of()
    sky, shift = table_ref[0], table_ref[1]
    masks = [shift == s for s in range(2 * SHIFT + 1)]
    bands = [bands_ref[d] for d in range(BAND)]
    totals = [jnp.zeros((SUB, LANES), f32) for _ in range(COMP)]
    for t in range(TAPS):
        tap = tap_of(t, bands, masks)
        both = basis_at(t, turned_ref)
        for k in range(COMP):
            totals[k] = totals[k] + tap * pick(both, (lane & HALF) + k)
    model_ref[...] = jnp.zeros((16, SUB * LANES), f32)
    for k in range(COMP):
        for j in range(SUB):
            model_ref[k : k + 1, j * LANES : (j + 1) * LANES] = totals[k][j : j + 1, :]
    slot = table_ref[2]
    slot = jnp.where((lane & (HALF - 1)) < FC, slot - ccd_at * FC, 0)
    place = jnp.where(slot >= FIBBLK, slot + (32 - FIBBLK), slot)
    picks_ref[0] = sky
    picks_ref[1] = place
    picks_ref[2] = pick(place, sky)
    shape = (LANES, LANES)
    row, col = lanes_of(shape, 0), lanes_of(shape, 1)
    fibre_r, _, valid_r = sky_index(row)
    fibre_c, comp_c, valid_c = sky_index(col)
    same = (fibre_r == fibre_c) & ((row & HALF) == (col & HALF)) & valid_r & valid_c
    same_ref[...] = jnp.where(same, 1.0, 0.0)
    for at, first in enumerate((0, FC)):
        select_ref[at] = jnp.where((row == comp_c + first) & valid_c, 1.0, 0.0).astype(jnp.bfloat16)


def extract_kernel(pix_ref, near_ref, psf_ref, flux_ref, vari_ref, pix_s, var_s):
    odd = lax.axis_index("ccd") % 2
    far = pl.ds(pl.multiple_of((1 - odd) * (EDGE + LOCAL), EDGE), EDGE)
    pix_s[pl.ds(pl.multiple_of(odd * (EDGE + LOCAL), EDGE), EDGE), :] = near_ref[...]
    pix_s[EDGE : EDGE + LOCAL, :] = pix_ref[...]
    pix_s[far, :] = jnp.zeros((EDGE, LANES), jnp.bfloat16)
    var_s[...] = variance_of(pix_s[...])
    var_s[far, :] = jnp.zeros((EDGE, LANES), jnp.bfloat16)
    for b in range(2):
        lower = b * BPIX * ROWS
        psf = psf_ref[b]
        flux_ref[b] = jnp.dot(psf, pix_s[lower : lower + DEPTH, :], preferred_element_type=f32)
        vari_ref[b] = jnp.dot(squared(psf), var_s[lower : lower + DEPTH, :], preferred_element_type=f32)


def variance_of(x):
    return (0.25 + jnp.square(x.astype(f32))).astype(jnp.bfloat16)


def squared(x):
    return jnp.square(x.astype(f32)).astype(jnp.bfloat16)


def split(x):
    high = x.astype(jnp.bfloat16)
    rest = x - high.astype(f32)
    middle = rest.astype(jnp.bfloat16)
    return high, middle, (rest - middle.astype(f32)).astype(jnp.bfloat16)


def gram_kernel(picks_ref, same_ref, select_ref, far_ref, psf_ref, flux_in, vari_in, model_ref, flux_ref, out_ref, edge_s, extra_s, pad_s, rows_s, flux_s, vari_s, weighted_s):
    odd = lax.axis_index("ccd") % 2
    lane = lanes_of()
    rows_s[...] = jnp.zeros((2, 2, LANES, LANES), f32)
    edge_s[0, 0:TAIL, :] = jnp.zeros((TAIL, LANES), jnp.bfloat16)
    edge_s[1, 0:TAIL, :] = jnp.zeros((TAIL, LANES), jnp.bfloat16)
    edge_s[0, TAIL : TAIL + EDGE, :] = far_ref[...]
    edge_s[1, TAIL : TAIL + EDGE, :] = variance_of(far_ref[...])

    @pl.when(odd == 1)
    def first_block():
        psf = psf_ref[0, :, 0:EDGE]
        extra_s[0] = jnp.dot(psf, edge_s[0, TAIL : TAIL + EDGE, :], preferred_element_type=f32)
        extra_s[1] = jnp.dot(squared(psf), edge_s[1, TAIL : TAIL + EDGE, :], preferred_element_type=f32)

    @pl.when(odd == 0)
    def second_block():
        psf = psf_ref[1, :, DEPTH - EDGE - TAIL : DEPTH]
        extra_s[0] = jnp.dot(psf, edge_s[0], preferred_element_type=f32)
        extra_s[1] = jnp.dot(squared(psf), edge_s[1], preferred_element_type=f32)

    for b in range(2):
        for q, part in enumerate((flux_in, vari_in)):
            pad_s[b, q, 0 : FIBBLK * ROWS, :] = part[b] + jnp.where(odd == 1 - b, extra_s[q], 0.0)
            for r in range(ROWS):
                at = (r % 2) * HALF + b * 32
                rows_s[q, r // 2, at : at + FIBBLK, :] = pad_s[b, q, pl.ds(r, FIBBLK, stride=ROWS), :]
    for half in range(2):
        flux_s[half] = jnp.transpose(rows_s[0, half])
        vari_s[half] = jnp.transpose(rows_s[1, half])
    _, _, valid = sky_index(lane)
    used = (lane & (HALF - 1)) < FC
    sky, place, sky_place = picks_ref[0], picks_ref[1], picks_ref[2]

    def gathered(ref, row, spot):
        upper = pick(ref[row : row + SUB, :], spot)
        lower = pick(ref[row + SUB : row + 2 * SUB, :], spot)
        return jnp.where(lane < HALF, upper, lower)

    target = jnp.zeros((SUB, LANES), f32)
    for r in range(ROWS):
        half, turn = r // 2, (r % 2) * HALF
        for m in range(GROUPS // CHUNK):
            e = r * 8 + m
            flux = jnp.where(used, gathered(flux_s.at[half], m * CHUNK, place + turn), 0.0)
            flux_ref[e] = flux
            vari = gathered(vari_s.at[half], m * CHUNK, sky_place + turn)
            weighted = jnp.where(valid, model_ref[e] / vari, 0.0)
            weighted_s[e * SUB : (e + 1) * SUB, :] = weighted
            target = target + weighted * pick(flux, sky)
    target = jnp.sum(target, axis=0, keepdims=True)
    model = model_ref[...].reshape(EXPOS * SUB, LANES)
    square = lax.dot_general(model, weighted_s[...], (((0,), (0,)), ((), ())), precision=highest, preferred_element_type=f32)
    square = square * same_ref[...]
    select = select_ref[0]
    summed = sum(jnp.dot(select[0:16], piece, preferred_element_type=f32) for piece in split(square))
    summed = jnp.where(lanes_of((16, LANES), 0) == COMP, target, summed)
    turned = (((1,), (1,)), ((), ()))
    placed = select_ref[1]
    full = sum(lax.dot_general(piece, placed, turned, preferred_element_type=f32) for piece in split(summed))
    tile = full[0:SUB] + pltpu.roll(full[SUB : 2 * SUB], HALF, 1)
    out_ref[...] = jnp.broadcast_to(tile[None], out_ref.shape)


def solve_kernel(parts_ref, flux_ref, out_ref):
    total = jnp.sum(parts_ref[...], axis=0)
    system = jnp.concatenate([total, pltpu.roll(total, HALF, 1)], axis=0)
    col = lanes_of((16, LANES))
    row = lanes_of((16, LANES), 0)
    col = col - FC
    system = jnp.where((col >= 0) & (col < COMP) & (row <= COMP), system, 0.0)
    for k in range(0, COMP, 2):
        left = pick(system, jnp.full((16, LANES), FC + k, jnp.int32))
        right = pick(system, jnp.full((16, LANES), FC + k + 1, jnp.int32))
        upper = system[k : k + 1, :] - jnp.where(col[0:1] == k, 1.0, 0.0)
        lower = system[k + 1 : k + 2, :] - jnp.where(col[0:1] == k + 1, 1.0, 0.0)
        a, b = left[k : k + 1, :], right[k : k + 1, :]
        c, d = left[k + 1 : k + 2, :], right[k + 1 : k + 2, :]
        scale = 1.0 / (a * d - b * c)
        system = system - left * ((d * upper - b * lower) * scale) - right * ((a * lower - c * upper) * scale)
    coeffs = jnp.broadcast_to(system[COMP : COMP + 1, :], (SUB, LANES))
    lane = lanes_of()
    here = (lane >= FC) & (lane < FC + COMP)
    for e in range(EXPOS):
        out_ref[e] = jnp.where(here, coeffs, flux_ref[e])


def subtract_kernel(flux_ref, model_ref, out_h, noise_h, sky_s, left_s, out_s, noise_s, sems):
    heads = flux_ref[pl.ds(0, EXPOS, stride=SUB), :]
    coeffs = pltpu.roll(heads, LANES - FC, 1)
    coeffs = jnp.where(lanes_of((EXPOS, LANES)) < COMP, coeffs, 0.0)[:, 0:16]
    sky = jnp.dot(coeffs, model_ref[...], precision=highest, preferred_element_type=f32)
    for j in range(SUB):
        sky_s[pl.ds(j, EXPOS, stride=SUB), :] = sky[:, j * LANES : (j + 1) * LANES]
    total = jnp.zeros((SUB, LANES), f32)
    copies = []
    for e in range(EXPOS):
        at = slice(e * SUB, (e + 1) * SUB)
        left = flux_ref[at, :] - sky_s[at, :]
        left_s[at, :] = left
        total = total + left
        out_s[e, 0:SUB, :] = left[:, 0:FC]
        out_s[e, SUB:CHUNK, :] = pltpu.roll(left, HALF, 1)[:, 0:FC]
        if e % PIECE == PIECE - 1:
            part = pl.ds(e + 1 - PIECE, PIECE)
            copies.append(pltpu.make_async_copy(out_s.at[part], out_h.at[part], sems.at[e // PIECE]))
            copies[-1].start()
    mean = total * (1.0 / EXPOS)
    spread = jnp.zeros((SUB, LANES), f32)
    for e in range(EXPOS):
        spread = spread + jnp.square(left_s[e * SUB : (e + 1) * SUB, :] - mean)
    noise = jnp.sqrt(spread * (1.0 / EXPOS) + 1e-06)
    noise_s[0:SUB, :] = noise[:, 0:FC]
    noise_s[SUB:CHUNK, :] = pltpu.roll(noise, HALF, 1)[:, 0:FC]
    copies.append(pltpu.make_async_copy(noise_s, noise_h, sems.at[EXPOS // PIECE]))
    copies[-1].start()
    for copy in copies:
        copy.wait()


VMEM = pl.BlockSpec(memory_space=pltpu.VMEM)
HBM = pl.BlockSpec(memory_space=pltpu.HBM)
TILES = jax.ShapeDtypeStruct((EXPOS, SUB, LANES), f32)
EDGES = jax.ShapeDtypeStruct((EDGE, GROUPS), jnp.bfloat16)
PARAMS = pltpu.CompilerParams(vmem_limit_bytes=40 * 1024 * 1024)
BANDS = jax.ShapeDtypeStruct((BAND, SUB, LANES), f32)


def sky_model(*arrays):
    return pl.pallas_call(
        sky_kernel,
        out_shape=(
            TILES,
            EDGES,
            EDGES,
            BANDS,
            jax.ShapeDtypeStruct((32, LANES), f32),
            jax.ShapeDtypeStruct((3, SUB, LANES), jnp.int32),
        ),
        in_specs=[HBM] * 6,
        out_specs=(VMEM,) * 6,
        scratch_shapes=[
            pltpu.VMEM((BAND, CHUNK, FC), f32),
            pltpu.VMEM((COMP, 528), f32),
            pltpu.VMEM((1, FC), jnp.int32),
            pltpu.VMEM((1, 96), jnp.int32),
            pltpu.VMEM((1, FC), jnp.int32),
            pltpu.VMEM((16, 640), f32),
            pltpu.VMEM((SUB, LANES), jnp.int32),
            pltpu.SemaphoreType.DMA((7,)),
        ],
        compiler_params=PARAMS,
        name="sky_model",
    )(*(pltpu.with_memory_space_constraint(v, pltpu.HBM) for v in arrays))


def local_model(bands, turned, table):
    return pl.pallas_call(
        model_kernel,
        out_shape=(
            jax.ShapeDtypeStruct((16, SUB * LANES), f32),
            jax.ShapeDtypeStruct((3, SUB, LANES), jnp.int32),
            jax.ShapeDtypeStruct((LANES, LANES), f32),
            jax.ShapeDtypeStruct((2, LANES, LANES), jnp.bfloat16),
        ),
        in_specs=[VMEM] * 3,
        out_specs=(VMEM,) * 4,
        compiler_params=PARAMS,
        name="local_model",
    )(bands, turned, table)


def extract(pixels, near, psf):
    part = jax.ShapeDtypeStruct((2, FIBBLK * ROWS, LANES), f32)
    return pl.pallas_call(
        extract_kernel,
        out_shape=(part, part),
        in_specs=[VMEM] * 3,
        out_specs=(VMEM, VMEM),
        scratch_shapes=[
            pltpu.VMEM((2 * EDGE + LOCAL, LANES), jnp.bfloat16),
            pltpu.VMEM((2 * EDGE + LOCAL, LANES), jnp.bfloat16),
        ],
        compiler_params=PARAMS,
        name="extract",
    )(pixels, near, psf)


def gram_parts(tables, far, psf, flux, vari, model, copies):
    return pl.pallas_call(
        gram_kernel,
        out_shape=(TILES, jax.ShapeDtypeStruct((copies, SUB, LANES), f32)),
        in_specs=[VMEM] * 8,
        out_specs=(VMEM, VMEM),
        scratch_shapes=[
            pltpu.VMEM((2, TAIL + EDGE, LANES), jnp.bfloat16),
            pltpu.VMEM((2, FIBBLK * ROWS, LANES), f32),
            pltpu.VMEM((2, 2, LANES, LANES), f32),
            pltpu.VMEM((2, 2, LANES, LANES), f32),
            pltpu.VMEM((2, LANES, LANES), f32),
            pltpu.VMEM((2, LANES, LANES), f32),
            pltpu.VMEM((EXPOS * SUB, LANES), f32),
        ],
        compiler_params=PARAMS,
        name="gram",
    )(*tables, far, psf, flux, vari, model)


def solve(parts, flux):
    return pl.pallas_call(
        solve_kernel, out_shape=TILES, in_specs=[VMEM, VMEM], out_specs=VMEM, compiler_params=PARAMS, name="solve"
    )(parts, flux)


def subtract(flux, model):
    return pl.pallas_call(
        subtract_kernel,
        out_shape=(jax.ShapeDtypeStruct((EXPOS, CHUNK, FC), f32), jax.ShapeDtypeStruct((CHUNK, FC), f32)),
        in_specs=[VMEM, VMEM],
        out_specs=(HBM, HBM),
        scratch_shapes=[
            pltpu.VMEM((EXPOS * SUB, LANES), f32),
            pltpu.VMEM((EXPOS * SUB, LANES), f32),
            pltpu.VMEM((EXPOS, CHUNK, FC), f32),
            pltpu.VMEM((CHUNK, FC), f32),
            pltpu.SemaphoreType.DMA((EXPOS // PIECE + 1,)),
        ],
        compiler_params=PARAMS,
        name="subtract",
    )(flux.reshape(EXPOS * SUB, LANES), model)


def shards(pixels, psf_proj, resolution, basis, sky_fibres, fibre_slot, band_shift):
    size = lax.axis_size("ccd")
    rows = pixels.reshape(LOCAL, GROUPS)
    res = resolution.transpose(1, 2, 0)
    sky = sky_fibres.reshape(1, -1)
    slot = fibre_slot.reshape(1, FC)
    shift = band_shift.reshape(1, FC)
    pairs = [[(i, i + 1) for i in range(start, size - 1, 2)] for start in (1, 0)]
    swaps = [[*pair, *((j, i) for i, j in pair)] for pair in pairs]
    send, near, far, *prepared = sky_model(res, basis, shift, sky, slot, rows)
    near = lax.ppermute(near, "ccd", swaps[0])
    far = lax.ppermute(far, "ccd", swaps[1])
    model, *tables = local_model(*prepared)
    part, vari = extract(rows, near, psf_proj)
    far, model, tables, part, vari = lax.optimization_barrier((far, model, tables, part, vari))
    sky_tiles = lax.all_to_all(send, "exp", split_axis=0, concat_axis=0, tiled=True)
    flux, parts = gram_parts(tables, far, psf_proj, part, vari, sky_tiles, size)
    parts = lax.all_to_all(parts, "ccd", split_axis=0, concat_axis=0, tiled=True)
    flux = solve(parts, flux)
    flux = lax.all_to_all(flux, "exp", split_axis=0, concat_axis=0, tiled=True)
    sky_subtracted, noise_rms = subtract(flux, model)
    return (sky_subtracted.transpose(0, 2, 1), noise_rms.transpose(1, 0))


def solution(mesh):
    in_specs = (
        P("exp", "ccd", None, None),
        P("ccd", None, None),
        P("ccd", None, "exp"),
        P(),
        P(),
        P("ccd"),
        P("ccd"),
    )
    out_specs = (P(None, "ccd", "exp"), P("ccd", "exp"))
    return jax.shard_map(shards, mesh=mesh, in_specs=in_specs, out_specs=out_specs, check_vma=False)
```

```python
import jax
import jax.numpy as jnp
from jax import lax
from jax.experimental import pallas as pl
from jax.experimental.pallas import tpu as pltpu
from jax.sharding import PartitionSpec as P

BPIX = 500
MARG = 20
ROWS = 4
COMP = 10
BAND = 11
SHIFT = 3
FIBBLK = 25
FC = 50
SPAN = 540
SKYC = 6
EXPOS = 32
PIECE = 16
CHUNK = 16
GROUPS = 128
LANES = 128
HALF = 64
SUB = 8
TAPS = BAND + 2 * SHIFT
EDGE = MARG * ROWS
DEPTH = SPAN * ROWS
TAIL = 32
LOCAL = 2 * BPIX * ROWS


f32 = jnp.float32
highest = lax.Precision.HIGHEST


def lanes_of(shape=(SUB, LANES), dim=1):
    return lax.broadcasted_iota(jnp.int32, shape, dim)


def sky_index(lane):
    within = lane & (HALF - 1)
    fibre = jnp.zeros_like(within)
    for i in range(1, SKYC):
        fibre = fibre + jnp.where(within >= i * COMP, 1, 0)
    comp = within - fibre * COMP
    valid = within < SKYC * COMP
    return fibre, comp, valid


def pick(x, idx):
    return jnp.take_along_axis(x, idx, axis=1, mode="promise_in_bounds")


def doubled(row, scratch):
    scratch[...] = jnp.zeros((SUB, LANES), jnp.int32)
    scratch[0:1, 0:FC] = row
    scratch[0:1, HALF : HALF + FC] = row
    return jnp.broadcast_to(scratch[0:1, :], (SUB, LANES))


def sky_lanes(row, scratch, ccd_at, fibre):
    scratch[...] = jnp.zeros((SUB, LANES), jnp.int32)
    scratch[0:1, 0 : row.shape[1]] = row
    listed = jnp.broadcast_to(scratch[0:1, :], (SUB, LANES))
    return (lanes_of() & HALF) + pick(listed, fibre + ccd_at * SKYC) - ccd_at * FC


def banded(res_ref, res_s):
    res_s[...] = jnp.zeros((BAND, SUB, LANES), f32)
    for d in range(BAND):
        res_s[d, :, 0:FC] = res_ref[d, 0:SUB, :]
        res_s[d, :, HALF : HALF + FC] = res_ref[d, SUB:CHUNK, :]
    return [res_s[d] for d in range(BAND)]


def turned_basis(basis_ref, basis_s, turned_s, exp_at):
    basis_s[...] = jnp.zeros((16, 640), f32)
    basis_s[0:COMP, 0:528] = basis_ref[...]
    tile = exp_at // 8
    offset = CHUNK * (exp_at % 8)
    near = basis_s[:, pl.ds(pl.multiple_of(tile * LANES, LANES), LANES)]
    far = basis_s[:, pl.ds(pl.multiple_of(tile * LANES + LANES, LANES), LANES)]
    turn = (LANES - offset) % LANES
    wide = lanes_of((16, LANES))
    window = jnp.where(wide < LANES - offset, pltpu.roll(near, turn, 1), pltpu.roll(far, turn, 1))
    turned_s[...] = jnp.transpose(jnp.concatenate([window, jnp.zeros((LANES - 16, LANES), f32)], axis=0))[0:32]


def tap_of(t, bands, masks):
    tap = jnp.zeros((SUB, LANES), f32)
    for s in range(2 * SHIFT + 1):
        if 0 <= t - s < BAND:
            tap = jnp.where(masks[s], bands[t - s], tap)
    return tap


def basis_at(t, turned_s):
    upper = turned_s[t : t + SUB, :]
    lower = turned_s[t + SUB : t + 2 * SUB, :]
    return jnp.where(lanes_of() < HALF, upper, pltpu.roll(lower, HALF, 1))


def sky_kernel(res_h, basis_h, shift_h, sky_h, slot_h, pix_h, send_h, near_ref, far_ref, bands_ref, turned_ref, table_ref, res_v, basis_v, shift_v, sky_v, slot_v, send_s, basis_s, row_s, sems):
    exp_at = lax.axis_index("exp")
    ccd_at = lax.axis_index("ccd")
    odd = ccd_at % 2
    at_near = pl.multiple_of(odd * (LOCAL - EDGE), EDGE)
    at_far = pl.multiple_of((1 - odd) * (LOCAL - EDGE), EDGE)
    moves = {
        "res": (res_h, res_v),
        "basis": (basis_h, basis_v),
        "sky": (sky_h, sky_v),
        "shift": (shift_h, shift_v),
        "slot": (slot_h, slot_v),
        "near": (pix_h.at[pl.ds(at_near, EDGE), :], near_ref),
        "far": (pix_h.at[pl.ds(at_far, EDGE), :], far_ref),
    }
    copies = {name: pltpu.make_async_copy(*move, sems.at[i]) for i, (name, move) in enumerate(moves.items())}
    for copy in copies.values():
        copy.start()
    lane = lanes_of()
    fibre, comp, valid = sky_index(lane)
    copies["sky"].wait()
    copies["shift"].wait()
    sky = sky_lanes(sky_v[...], row_s, ccd_at, fibre)
    shift = doubled(shift_v[...], row_s) + SHIFT
    table_ref[0] = sky
    table_ref[1] = shift
    shift = pick(shift, sky)
    masks = [shift == s for s in range(2 * SHIFT + 1)]
    copies["basis"].wait()
    turned_basis(basis_v, basis_s, turned_ref, exp_at)
    copies["res"].wait()
    bands = [pick(band, sky) for band in banded(res_v, bands_ref)]
    total = jnp.zeros((SUB, LANES), f32)
    for t in range(TAPS):
        total = total + tap_of(t, bands, masks) * pick(basis_at(t, turned_ref), (lane & HALF) + comp)
    total = jnp.where(valid, total, 0.0)
    send_s[...] = jnp.broadcast_to(total[None], (EXPOS, SUB, LANES))
    sent = pltpu.make_async_copy(send_s, send_h, sems.at[len(moves)])
    sent.start()
    copies["slot"].wait()
    table_ref[2] = doubled(slot_v[...], row_s)
    copies["near"].wait()
    copies["far"].wait()
    sent.wait()


def model_kernel(bands_ref, turned_ref, table_ref, model_ref, picks_ref, same_ref, select_ref):
    ccd_at = lax.axis_index("ccd")
    lane = lanes_of()
    sky, shift = table_ref[0], table_ref[1]
    masks = [shift == s for s in range(2 * SHIFT + 1)]
    bands = [bands_ref[d] for d in range(BAND)]
    totals = [jnp.zeros((SUB, LANES), f32) for _ in range(COMP)]
    for t in range(TAPS):
        tap = tap_of(t, bands, masks)
        both = basis_at(t, turned_ref)
        for k in range(COMP):
            totals[k] = totals[k] + tap * pick(both, (lane & HALF) + k)
    model_ref[...] = jnp.zeros((16, SUB * LANES), f32)
    for k in range(COMP):
        for j in range(SUB):
            model_ref[k : k + 1, j * LANES : (j + 1) * LANES] = totals[k][j : j + 1, :]
    slot = table_ref[2]
    slot = jnp.where((lane & (HALF - 1)) < FC, slot - ccd_at * FC, 0)
    place = jnp.where(slot >= FIBBLK, slot + (32 - FIBBLK), slot)
    picks_ref[0] = sky
    picks_ref[1] = place
    picks_ref[2] = pick(place, sky)
    shape = (LANES, LANES)
    row, col = lanes_of(shape, 0), lanes_of(shape, 1)
    fibre_r, _, valid_r = sky_index(row)
    fibre_c, comp_c, valid_c = sky_index(col)
    same = (fibre_r == fibre_c) & ((row & HALF) == (col & HALF)) & valid_r & valid_c
    same_ref[...] = jnp.where(same, 1.0, 0.0)
    for at, first in enumerate((0, FC)):
        select_ref[at] = jnp.where((row == comp_c + first) & valid_c, 1.0, 0.0).astype(jnp.bfloat16)


def extract_kernel(pix_ref, near_ref, psf_ref, flux_ref, vari_ref, pix_s, var_s):
    odd = lax.axis_index("ccd") % 2
    far = pl.ds(pl.multiple_of((1 - odd) * (EDGE + LOCAL), EDGE), EDGE)
    pix_s[pl.ds(pl.multiple_of(odd * (EDGE + LOCAL), EDGE), EDGE), :] = near_ref[...]
    pix_s[EDGE : EDGE + LOCAL, :] = pix_ref[...]
    pix_s[far, :] = jnp.zeros((EDGE, LANES), jnp.bfloat16)
    var_s[...] = variance_of(pix_s[...])
    var_s[far, :] = jnp.zeros((EDGE, LANES), jnp.bfloat16)
    for b in range(2):
        lower = b * BPIX * ROWS
        psf = psf_ref[b]
        flux_ref[b] = jnp.dot(psf, pix_s[lower : lower + DEPTH, :], preferred_element_type=f32)
        vari_ref[b] = jnp.dot(squared(psf), var_s[lower : lower + DEPTH, :], preferred_element_type=f32)


def variance_of(x):
    return (0.25 + jnp.square(x.astype(f32))).astype(jnp.bfloat16)


def squared(x):
    return jnp.square(x.astype(f32)).astype(jnp.bfloat16)


def split(x):
    high = x.astype(jnp.bfloat16)
    rest = x - high.astype(f32)
    middle = rest.astype(jnp.bfloat16)
    return high, middle, (rest - middle.astype(f32)).astype(jnp.bfloat16)


def gram_kernel(picks_ref, same_ref, select_ref, far_ref, psf_ref, flux_in, vari_in, model_ref, flux_ref, out_ref, edge_s, extra_s, pad_s, rows_s, flux_s, vari_s, weighted_s):
    odd = lax.axis_index("ccd") % 2
    lane = lanes_of()
    rows_s[...] = jnp.zeros((2, 2, LANES, LANES), f32)
    edge_s[0, 0:TAIL, :] = jnp.zeros((TAIL, LANES), jnp.bfloat16)
    edge_s[1, 0:TAIL, :] = jnp.zeros((TAIL, LANES), jnp.bfloat16)
    edge_s[0, TAIL : TAIL + EDGE, :] = far_ref[...]
    edge_s[1, TAIL : TAIL + EDGE, :] = variance_of(far_ref[...])

    @pl.when(odd == 1)
    def first_block():
        psf = psf_ref[0, :, 0:EDGE]
        extra_s[0] = jnp.dot(psf, edge_s[0, TAIL : TAIL + EDGE, :], preferred_element_type=f32)
        extra_s[1] = jnp.dot(squared(psf), edge_s[1, TAIL : TAIL + EDGE, :], preferred_element_type=f32)

    @pl.when(odd == 0)
    def second_block():
        psf = psf_ref[1, :, DEPTH - EDGE - TAIL : DEPTH]
        extra_s[0] = jnp.dot(psf, edge_s[0], preferred_element_type=f32)
        extra_s[1] = jnp.dot(squared(psf), edge_s[1], preferred_element_type=f32)

    for b in range(2):
        for q, part in enumerate((flux_in, vari_in)):
            pad_s[b, q, 0 : FIBBLK * ROWS, :] = part[b] + jnp.where(odd == 1 - b, extra_s[q], 0.0)
            for r in range(ROWS):
                at = (r % 2) * HALF + b * 32
                rows_s[q, r // 2, at : at + FIBBLK, :] = pad_s[b, q, pl.ds(r, FIBBLK, stride=ROWS), :]
    for half in range(2):
        flux_s[half] = jnp.transpose(rows_s[0, half])
        vari_s[half] = jnp.transpose(rows_s[1, half])
    _, _, valid = sky_index(lane)
    used = (lane & (HALF - 1)) < FC
    sky, place, sky_place = picks_ref[0], picks_ref[1], picks_ref[2]

    def gathered(ref, row, spot):
        upper = pick(ref[row : row + SUB, :], spot)
        lower = pick(ref[row + SUB : row + 2 * SUB, :], spot)
        return jnp.where(lane < HALF, upper, lower)

    target = jnp.zeros((SUB, LANES), f32)
    for r in range(ROWS):
        half, turn = r // 2, (r % 2) * HALF
        for m in range(GROUPS // CHUNK):
            e = r * 8 + m
            flux = jnp.where(used, gathered(flux_s.at[half], m * CHUNK, place + turn), 0.0)
            flux_ref[e] = flux
            vari = gathered(vari_s.at[half], m * CHUNK, sky_place + turn)
            weighted = jnp.where(valid, model_ref[e] / vari, 0.0)
            weighted_s[e * SUB : (e + 1) * SUB, :] = weighted
            target = target + weighted * pick(flux, sky)
    target = jnp.sum(target, axis=0, keepdims=True)
    model = model_ref[...].reshape(EXPOS * SUB, LANES)
    square = lax.dot_general(model, weighted_s[...], (((0,), (0,)), ((), ())), precision=highest, preferred_element_type=f32)
    square = square * same_ref[...]
    select = select_ref[0]
    summed = sum(jnp.dot(select[0:16], piece, preferred_element_type=f32) for piece in split(square))
    summed = jnp.where(lanes_of((16, LANES), 0) == COMP, target, summed)
    turned = (((1,), (1,)), ((), ()))
    placed = select_ref[1]
    full = sum(lax.dot_general(piece, placed, turned, preferred_element_type=f32) for piece in split(summed))
    tile = full[0:SUB] + pltpu.roll(full[SUB : 2 * SUB], HALF, 1)
    out_ref[...] = jnp.broadcast_to(tile[None], out_ref.shape)


def solve_kernel(parts_ref, flux_ref, out_ref):
    total = jnp.sum(parts_ref[...], axis=0)
    system = jnp.concatenate([total, pltpu.roll(total, HALF, 1)], axis=0)
    col = lanes_of((16, LANES))
    row = lanes_of((16, LANES), 0)
    col = col - FC
    system = jnp.where((col >= 0) & (col < COMP) & (row <= COMP), system, 0.0)
    for k in range(0, COMP, 2):
        left = pick(system, jnp.full((16, LANES), FC + k, jnp.int32))
        right = pick(system, jnp.full((16, LANES), FC + k + 1, jnp.int32))
        upper = system[k : k + 1, :] - jnp.where(col[0:1] == k, 1.0, 0.0)
        lower = system[k + 1 : k + 2, :] - jnp.where(col[0:1] == k + 1, 1.0, 0.0)
        a, b = left[k : k + 1, :], right[k : k + 1, :]
        c, d = left[k + 1 : k + 2, :], right[k + 1 : k + 2, :]
        scale = 1.0 / (a * d - b * c)
        system = system - left * ((d * upper - b * lower) * scale) - right * ((a * lower - c * upper) * scale)
    coeffs = jnp.broadcast_to(system[COMP : COMP + 1, :], (SUB, LANES))
    lane = lanes_of()
    here = (lane >= FC) & (lane < FC + COMP)
    for e in range(EXPOS):
        out_ref[e] = jnp.where(here, coeffs, flux_ref[e])


def subtract_kernel(flux_ref, model_ref, out_h, noise_h, sky_s, left_s, out_s, noise_s, sems):
    heads = flux_ref[pl.ds(0, EXPOS, stride=SUB), :]
    coeffs = pltpu.roll(heads, LANES - FC, 1)
    coeffs = jnp.where(lanes_of((EXPOS, LANES)) < COMP, coeffs, 0.0)[:, 0:16]
    sky = jnp.dot(coeffs, model_ref[...], precision=highest, preferred_element_type=f32)
    for j in range(SUB):
        sky_s[pl.ds(j, EXPOS, stride=SUB), :] = sky[:, j * LANES : (j + 1) * LANES]
    total = jnp.zeros((SUB, LANES), f32)
    copies = []
    for e in range(EXPOS):
        at = slice(e * SUB, (e + 1) * SUB)
        left = flux_ref[at, :] - sky_s[at, :]
        left_s[at, :] = left
        total = total + left
        out_s[e, 0:SUB, :] = left[:, 0:FC]
        out_s[e, SUB:CHUNK, :] = pltpu.roll(left, HALF, 1)[:, 0:FC]
        if e % PIECE == PIECE - 1:
            part = pl.ds(e + 1 - PIECE, PIECE)
            copies.append(pltpu.make_async_copy(out_s.at[part], out_h.at[part], sems.at[e // PIECE]))
            copies[-1].start()
    mean = total * (1.0 / EXPOS)
    spread = jnp.zeros((SUB, LANES), f32)
    for e in range(EXPOS):
        spread = spread + jnp.square(left_s[e * SUB : (e + 1) * SUB, :] - mean)
    noise = jnp.sqrt(spread * (1.0 / EXPOS) + 1e-06)
    noise_s[0:SUB, :] = noise[:, 0:FC]
    noise_s[SUB:CHUNK, :] = pltpu.roll(noise, HALF, 1)[:, 0:FC]
    copies.append(pltpu.make_async_copy(noise_s, noise_h, sems.at[EXPOS // PIECE]))
    copies[-1].start()
    for copy in copies:
        copy.wait()


VMEM = pl.BlockSpec(memory_space=pltpu.VMEM)
HBM = pl.BlockSpec(memory_space=pltpu.HBM)
TILES = jax.ShapeDtypeStruct((EXPOS, SUB, LANES), f32)
EDGES = jax.ShapeDtypeStruct((EDGE, GROUPS), jnp.bfloat16)
PARAMS = pltpu.CompilerParams(vmem_limit_bytes=40 * 1024 * 1024)
BANDS = jax.ShapeDtypeStruct((BAND, SUB, LANES), f32)


def sky_model(*arrays):
    return pl.pallas_call(
        sky_kernel,
        out_shape=(
            TILES,
            EDGES,
            EDGES,
            BANDS,
            jax.ShapeDtypeStruct((32, LANES), f32),
            jax.ShapeDtypeStruct((3, SUB, LANES), jnp.int32),
        ),
        in_specs=[HBM] * 6,
        out_specs=(HBM,) + (VMEM,) * 5,
        scratch_shapes=[
            pltpu.VMEM((BAND, CHUNK, FC), f32),
            pltpu.VMEM((COMP, 528), f32),
            pltpu.VMEM((1, FC), jnp.int32),
            pltpu.VMEM((1, 96), jnp.int32),
            pltpu.VMEM((1, FC), jnp.int32),
            pltpu.VMEM((EXPOS, SUB, LANES), f32),
            pltpu.VMEM((16, 640), f32),
            pltpu.VMEM((SUB, LANES), jnp.int32),
            pltpu.SemaphoreType.DMA((8,)),
        ],
        compiler_params=PARAMS,
        name="sky_model",
    )(*(pltpu.with_memory_space_constraint(v, pltpu.HBM) for v in arrays))


def local_model(bands, turned, table):
    return pl.pallas_call(
        model_kernel,
        out_shape=(
            jax.ShapeDtypeStruct((16, SUB * LANES), f32),
            jax.ShapeDtypeStruct((3, SUB, LANES), jnp.int32),
            jax.ShapeDtypeStruct((LANES, LANES), f32),
            jax.ShapeDtypeStruct((2, LANES, LANES), jnp.bfloat16),
        ),
        in_specs=[VMEM] * 3,
        out_specs=(VMEM,) * 4,
        compiler_params=PARAMS,
        name="local_model",
    )(bands, turned, table)


def extract(pixels, near, psf):
    part = jax.ShapeDtypeStruct((2, FIBBLK * ROWS, LANES), f32)
    return pl.pallas_call(
        extract_kernel,
        out_shape=(part, part),
        in_specs=[VMEM] * 3,
        out_specs=(VMEM, VMEM),
        scratch_shapes=[
            pltpu.VMEM((2 * EDGE + LOCAL, LANES), jnp.bfloat16),
            pltpu.VMEM((2 * EDGE + LOCAL, LANES), jnp.bfloat16),
        ],
        compiler_params=PARAMS,
        name="extract",
    )(pixels, near, psf)


def gram_parts(tables, far, psf, flux, vari, model, copies):
    return pl.pallas_call(
        gram_kernel,
        out_shape=(TILES, jax.ShapeDtypeStruct((copies, SUB, LANES), f32)),
        in_specs=[VMEM] * 8,
        out_specs=(VMEM, VMEM),
        scratch_shapes=[
            pltpu.VMEM((2, TAIL + EDGE, LANES), jnp.bfloat16),
            pltpu.VMEM((2, FIBBLK * ROWS, LANES), f32),
            pltpu.VMEM((2, 2, LANES, LANES), f32),
            pltpu.VMEM((2, 2, LANES, LANES), f32),
            pltpu.VMEM((2, LANES, LANES), f32),
            pltpu.VMEM((2, LANES, LANES), f32),
            pltpu.VMEM((EXPOS * SUB, LANES), f32),
        ],
        compiler_params=PARAMS,
        name="gram",
    )(*tables, far, psf, flux, vari, model)


def solve(parts, flux):
    return pl.pallas_call(
        solve_kernel, out_shape=TILES, in_specs=[VMEM, VMEM], out_specs=VMEM, compiler_params=PARAMS, name="solve"
    )(parts, flux)


def subtract(flux, model):
    return pl.pallas_call(
        subtract_kernel,
        out_shape=(jax.ShapeDtypeStruct((EXPOS, CHUNK, FC), f32), jax.ShapeDtypeStruct((CHUNK, FC), f32)),
        in_specs=[VMEM, VMEM],
        out_specs=(HBM, HBM),
        scratch_shapes=[
            pltpu.VMEM((EXPOS * SUB, LANES), f32),
            pltpu.VMEM((EXPOS * SUB, LANES), f32),
            pltpu.VMEM((EXPOS, CHUNK, FC), f32),
            pltpu.VMEM((CHUNK, FC), f32),
            pltpu.SemaphoreType.DMA((EXPOS // PIECE + 1,)),
        ],
        compiler_params=PARAMS,
        name="subtract",
    )(flux.reshape(EXPOS * SUB, LANES), model)


def shards(pixels, psf_proj, resolution, basis, sky_fibres, fibre_slot, band_shift):
    size = lax.axis_size("ccd")
    rows = pixels.reshape(LOCAL, GROUPS)
    res = resolution.transpose(1, 2, 0)
    sky = sky_fibres.reshape(1, -1)
    slot = fibre_slot.reshape(1, FC)
    shift = band_shift.reshape(1, FC)
    pairs = [[(i, i + 1) for i in range(start, size - 1, 2)] for start in (1, 0)]
    swaps = [[*pair, *((j, i) for i, j in pair)] for pair in pairs]
    send, near, far, *prepared = sky_model(res, basis, shift, sky, slot, rows)
    near = lax.ppermute(near, "ccd", swaps[0])
    far = lax.ppermute(far, "ccd", swaps[1])
    model, *tables = local_model(*prepared)
    part, vari = extract(rows, near, psf_proj)
    far, model, tables, part, vari = lax.optimization_barrier((far, model, tables, part, vari))
    sky_tiles = lax.all_to_all(send, "exp", split_axis=0, concat_axis=0, tiled=True)
    flux, parts = gram_parts(tables, far, psf_proj, part, vari, sky_tiles, size)
    parts = lax.all_to_all(parts, "ccd", split_axis=0, concat_axis=0, tiled=True)
    flux = solve(parts, flux)
    flux = lax.all_to_all(flux, "exp", split_axis=0, concat_axis=0, tiled=True)
    sky_subtracted, noise_rms = subtract(flux, model)
    return (sky_subtracted.transpose(0, 2, 1), noise_rms.transpose(1, 0))


def solution(mesh):
    in_specs = (
        P("exp", "ccd", None, None),
        P("ccd", None, None),
        P("ccd", None, "exp"),
        P(),
        P(),
        P("ccd"),
        P("ccd"),
    )
    out_specs = (P(None, "ccd", "exp"), P("ccd", "exp"))
    return jax.shard_map(shards, mesh=mesh, in_specs=in_specs, out_specs=out_specs, check_vma=False)
```

```python
import jax
import jax.numpy as jnp
from jax import lax
from jax.experimental import pallas as pl
from jax.experimental.pallas import tpu as pltpu
from jax.sharding import PartitionSpec as P

BPIX = 500
MARG = 20
ROWS = 4
COMP = 10
BAND = 11
SHIFT = 3
FIBBLK = 25
FC = 50
SPAN = 540
SKYC = 6
EXPOS = 32
PIECE = 16
CHUNK = 16
GROUPS = 128
LANES = 128
HALF = 64
SUB = 8
TAPS = BAND + 2 * SHIFT
EDGE = MARG * ROWS
DEPTH = SPAN * ROWS
TAIL = 32
LOCAL = 2 * BPIX * ROWS


f32 = jnp.float32
highest = lax.Precision.HIGHEST


def lanes_of(shape=(SUB, LANES), dim=1):
    return lax.broadcasted_iota(jnp.int32, shape, dim)


def sky_index(lane):
    within = lane & (HALF - 1)
    fibre = jnp.zeros_like(within)
    for i in range(1, SKYC):
        fibre = fibre + jnp.where(within >= i * COMP, 1, 0)
    comp = within - fibre * COMP
    valid = within < SKYC * COMP
    return fibre, comp, valid


def pick(x, idx):
    return jnp.take_along_axis(x, idx, axis=1, mode="promise_in_bounds")


def doubled(row, scratch):
    scratch[...] = jnp.zeros((SUB, LANES), jnp.int32)
    scratch[0:1, 0:FC] = row
    scratch[0:1, HALF : HALF + FC] = row
    return jnp.broadcast_to(scratch[0:1, :], (SUB, LANES))


def sky_lanes(row, scratch, ccd_at, fibre):
    scratch[...] = jnp.zeros((SUB, LANES), jnp.int32)
    scratch[0:1, 0 : row.shape[1]] = row
    listed = jnp.broadcast_to(scratch[0:1, :], (SUB, LANES))
    return (lanes_of() & HALF) + pick(listed, fibre + ccd_at * SKYC) - ccd_at * FC


def banded(res_ref, res_s):
    res_s[...] = jnp.zeros((BAND, SUB, LANES), f32)
    for d in range(BAND):
        res_s[d, :, 0:FC] = res_ref[d, 0:SUB, :]
        res_s[d, :, HALF : HALF + FC] = res_ref[d, SUB:CHUNK, :]
    return [res_s[d] for d in range(BAND)]


def turned_basis(basis_ref, basis_s, turned_s, exp_at):
    basis_s[...] = jnp.zeros((16, 640), f32)
    basis_s[0:COMP, 0:528] = basis_ref[...]
    tile = exp_at // 8
    offset = CHUNK * (exp_at % 8)
    near = basis_s[:, pl.ds(pl.multiple_of(tile * LANES, LANES), LANES)]
    far = basis_s[:, pl.ds(pl.multiple_of(tile * LANES + LANES, LANES), LANES)]
    turn = (LANES - offset) % LANES
    wide = lanes_of((16, LANES))
    window = jnp.where(wide < LANES - offset, pltpu.roll(near, turn, 1), pltpu.roll(far, turn, 1))
    turned_s[...] = jnp.transpose(jnp.concatenate([window, jnp.zeros((LANES - 16, LANES), f32)], axis=0))[0:32]


def tap_of(t, bands, masks):
    tap = jnp.zeros((SUB, LANES), f32)
    for s in range(2 * SHIFT + 1):
        if 0 <= t - s < BAND:
            tap = jnp.where(masks[s], bands[t - s], tap)
    return tap


def basis_at(t, turned_s):
    upper = turned_s[t : t + SUB, :]
    lower = turned_s[t + SUB : t + 2 * SUB, :]
    return jnp.where(lanes_of() < HALF, upper, pltpu.roll(lower, HALF, 1))


def sky_kernel(res_h, basis_h, shift_h, sky_h, slot_h, pix_h, send_h, near_ref, far_ref, bands_ref, turned_ref, table_ref, res_v, basis_v, shift_v, sky_v, slot_v, send_s, basis_s, row_s, sems):
    exp_at = lax.axis_index("exp")
    ccd_at = lax.axis_index("ccd")
    odd = ccd_at % 2
    at_near = pl.multiple_of(odd * (LOCAL - EDGE), EDGE)
    at_far = pl.multiple_of((1 - odd) * (LOCAL - EDGE), EDGE)
    moves = {
        "res": (res_h, res_v),
        "basis": (basis_h, basis_v),
        "sky": (sky_h, sky_v),
        "shift": (shift_h, shift_v),
        "slot": (slot_h, slot_v),
        "near": (pix_h.at[pl.ds(at_near, EDGE), :], near_ref),
        "far": (pix_h.at[pl.ds(at_far, EDGE), :], far_ref),
    }
    copies = {name: pltpu.make_async_copy(*move, sems.at[i]) for i, (name, move) in enumerate(moves.items())}
    for copy in copies.values():
        copy.start()
    lane = lanes_of()
    fibre, comp, valid = sky_index(lane)
    copies["sky"].wait()
    copies["shift"].wait()
    sky = sky_lanes(sky_v[...], row_s, ccd_at, fibre)
    shift = doubled(shift_v[...], row_s) + SHIFT
    table_ref[0] = sky
    table_ref[1] = shift
    shift = pick(shift, sky)
    masks = [shift == s for s in range(2 * SHIFT + 1)]
    copies["basis"].wait()
    turned_basis(basis_v, basis_s, turned_ref, exp_at)
    copies["res"].wait()
    bands = [pick(band, sky) for band in banded(res_v, bands_ref)]
    total = jnp.zeros((SUB, LANES), f32)
    for t in range(TAPS):
        total = total + tap_of(t, bands, masks) * pick(basis_at(t, turned_ref), (lane & HALF) + comp)
    total = jnp.where(valid, total, 0.0)
    send_s[...] = jnp.broadcast_to(total[None], (EXPOS, SUB, LANES))
    sent = pltpu.make_async_copy(send_s, send_h, sems.at[len(moves)])
    sent.start()
    copies["slot"].wait()
    table_ref[2] = doubled(slot_v[...], row_s)
    copies["near"].wait()
    copies["far"].wait()
    sent.wait()


def model_kernel(bands_ref, turned_ref, table_ref, model_ref, picks_ref, same_ref, select_ref):
    ccd_at = lax.axis_index("ccd")
    lane = lanes_of()
    sky, shift = table_ref[0], table_ref[1]
    masks = [shift == s for s in range(2 * SHIFT + 1)]
    bands = [bands_ref[d] for d in range(BAND)]
    totals = [jnp.zeros((SUB, LANES), f32) for _ in range(COMP)]
    for t in range(TAPS):
        tap = tap_of(t, bands, masks)
        both = basis_at(t, turned_ref)
        for k in range(COMP):
            totals[k] = totals[k] + tap * pick(both, (lane & HALF) + k)
    model_ref[...] = jnp.zeros((16, SUB * LANES), f32)
    for k in range(COMP):
        for j in range(SUB):
            model_ref[k : k + 1, j * LANES : (j + 1) * LANES] = totals[k][j : j + 1, :]
    slot = table_ref[2]
    slot = jnp.where((lane & (HALF - 1)) < FC, slot - ccd_at * FC, 0)
    place = jnp.where(slot >= FIBBLK, slot + (32 - FIBBLK), slot)
    picks_ref[0] = sky
    picks_ref[1] = place
    picks_ref[2] = pick(place, sky)
    shape = (LANES, LANES)
    row, col = lanes_of(shape, 0), lanes_of(shape, 1)
    fibre_r, _, valid_r = sky_index(row)
    fibre_c, comp_c, valid_c = sky_index(col)
    same = (fibre_r == fibre_c) & ((row & HALF) == (col & HALF)) & valid_r & valid_c
    same_ref[...] = jnp.where(same, 1.0, 0.0)
    for at, first in enumerate((0, FC)):
        select_ref[at] = jnp.where((row == comp_c + first) & valid_c, 1.0, 0.0).astype(jnp.bfloat16)


def extract_kernel(pix_ref, near_ref, psf_ref, flux_ref, vari_ref, pix_s, var_s):
    odd = lax.axis_index("ccd") % 2
    far = pl.ds(pl.multiple_of((1 - odd) * (EDGE + LOCAL), EDGE), EDGE)
    pix_s[pl.ds(pl.multiple_of(odd * (EDGE + LOCAL), EDGE), EDGE), :] = near_ref[...]
    pix_s[EDGE : EDGE + LOCAL, :] = pix_ref[...]
    pix_s[far, :] = jnp.zeros((EDGE, LANES), jnp.bfloat16)
    var_s[...] = variance_of(pix_s[...])
    var_s[far, :] = jnp.zeros((EDGE, LANES), jnp.bfloat16)
    for b in range(2):
        lower = b * BPIX * ROWS
        psf = psf_ref[b]
        flux_ref[b] = jnp.dot(psf, pix_s[lower : lower + DEPTH, :], preferred_element_type=f32)
        vari_ref[b] = jnp.dot(squared(psf), var_s[lower : lower + DEPTH, :], preferred_element_type=f32)


def variance_of(x):
    return (0.25 + jnp.square(x.astype(f32))).astype(jnp.bfloat16)


def squared(x):
    return jnp.square(x.astype(f32)).astype(jnp.bfloat16)


def split(x):
    high = x.astype(jnp.bfloat16)
    rest = x - high.astype(f32)
    middle = rest.astype(jnp.bfloat16)
    return high, middle, (rest - middle.astype(f32)).astype(jnp.bfloat16)


def gram_kernel(picks_ref, same_ref, select_ref, far_ref, psf_ref, flux_in, vari_in, model_ref, flux_ref, out_ref, edge_s, extra_s, pad_s, rows_s, flux_s, vari_s, weighted_s):
    odd = lax.axis_index("ccd") % 2
    lane = lanes_of()
    edge_s[0, 0:TAIL, :] = jnp.zeros((TAIL, LANES), jnp.bfloat16)
    edge_s[1, 0:TAIL, :] = jnp.zeros((TAIL, LANES), jnp.bfloat16)
    edge_s[0, TAIL : TAIL + EDGE, :] = far_ref[...]
    edge_s[1, TAIL : TAIL + EDGE, :] = variance_of(far_ref[...])

    @pl.when(odd == 1)
    def first_block():
        psf = psf_ref[0, :, 0:EDGE]
        extra_s[0] = jnp.dot(psf, edge_s[0, TAIL : TAIL + EDGE, :], preferred_element_type=f32)
        extra_s[1] = jnp.dot(squared(psf), edge_s[1, TAIL : TAIL + EDGE, :], preferred_element_type=f32)

    @pl.when(odd == 0)
    def second_block():
        psf = psf_ref[1, :, DEPTH - EDGE - TAIL : DEPTH]
        extra_s[0] = jnp.dot(psf, edge_s[0], preferred_element_type=f32)
        extra_s[1] = jnp.dot(squared(psf), edge_s[1], preferred_element_type=f32)

    for b in range(2):
        for q, part in enumerate((flux_in, vari_in)):
            pad_s[b, q, 0 : FIBBLK * ROWS, :] = part[b] + jnp.where(odd == 1 - b, extra_s[q], 0.0)
            for r in range(ROWS):
                at = (r % 2) * HALF + b * 32
                rows_s[q, r // 2, at : at + FIBBLK, :] = pad_s[b, q, pl.ds(r, FIBBLK, stride=ROWS), :]
    for half in range(2):
        flux_s[half] = jnp.transpose(rows_s[0, half])
        vari_s[half] = jnp.transpose(rows_s[1, half])
    _, _, valid = sky_index(lane)
    used = (lane & (HALF - 1)) < FC
    sky, place, sky_place = picks_ref[0], picks_ref[1], picks_ref[2]

    def gathered(ref, row, spot):
        upper = pick(ref[row : row + SUB, :], spot)
        lower = pick(ref[row + SUB : row + 2 * SUB, :], spot)
        return jnp.where(lane < HALF, upper, lower)

    target = jnp.zeros((SUB, LANES), f32)
    for r in range(ROWS):
        half, turn = r // 2, (r % 2) * HALF
        for m in range(GROUPS // CHUNK):
            e = r * 8 + m
            flux = jnp.where(used, gathered(flux_s.at[half], m * CHUNK, place + turn), 0.0)
            flux_ref[e] = flux
            vari = gathered(vari_s.at[half], m * CHUNK, sky_place + turn)
            weighted = jnp.where(valid, model_ref[e] / vari, 0.0)
            weighted_s[e * SUB : (e + 1) * SUB, :] = weighted
            target = target + weighted * pick(flux, sky)
    target = jnp.sum(target, axis=0, keepdims=True)
    model = model_ref[...].reshape(EXPOS * SUB, LANES)
    square = lax.dot_general(model, weighted_s[...], (((0,), (0,)), ((), ())), precision=highest, preferred_element_type=f32)
    square = square * same_ref[...]
    select = select_ref[0]
    summed = sum(jnp.dot(select[0:16], piece, preferred_element_type=f32) for piece in split(square))
    summed = jnp.where(lanes_of((16, LANES), 0) == COMP, target, summed)
    turned = (((1,), (1,)), ((), ()))
    placed = select_ref[1]
    full = sum(lax.dot_general(piece, placed, turned, preferred_element_type=f32) for piece in split(summed))
    tile = full[0:SUB] + pltpu.roll(full[SUB : 2 * SUB], HALF, 1)
    out_ref[...] = jnp.broadcast_to(tile[None], out_ref.shape)


def solve_kernel(parts_ref, flux_ref, out_ref):
    parts = [parts_ref[c] for c in range(parts_ref.shape[0])]
    while len(parts) > 1:
        parts = [sum(parts[c : c + 2]) for c in range(0, len(parts), 2)]
    total = parts[0]
    system = jnp.concatenate([total, pltpu.roll(total, HALF, 1)], axis=0)
    col = lanes_of((16, LANES))
    row = lanes_of((16, LANES), 0)
    col = col - FC
    system = jnp.where((col >= 0) & (col < COMP) & (row <= COMP), system, 0.0)
    for k in range(0, COMP, 2):
        left = pick(system, jnp.full((16, LANES), FC + k, jnp.int32))
        right = pick(system, jnp.full((16, LANES), FC + k + 1, jnp.int32))
        upper = system[k : k + 1, :] - jnp.where(col[0:1] == k, 1.0, 0.0)
        lower = system[k + 1 : k + 2, :] - jnp.where(col[0:1] == k + 1, 1.0, 0.0)
        a, b = left[k : k + 1, :], right[k : k + 1, :]
        c, d = left[k + 1 : k + 2, :], right[k + 1 : k + 2, :]
        scale = 1.0 / (a * d - b * c)
        system = system - left * ((d * upper - b * lower) * scale) - right * ((a * lower - c * upper) * scale)
    coeffs = jnp.broadcast_to(system[COMP : COMP + 1, :], (SUB, LANES))
    lane = lanes_of()
    here = (lane >= FC) & (lane < FC + COMP)
    for e in range(EXPOS):
        out_ref[e] = jnp.where(here, coeffs, flux_ref[e])


def subtract_kernel(flux_ref, model_ref, out_h, noise_h, sky_s, left_s, out_s, noise_s, sems):
    heads = flux_ref[pl.ds(0, EXPOS, stride=SUB), :]
    coeffs = pltpu.roll(heads, LANES - FC, 1)
    coeffs = jnp.where(lanes_of((EXPOS, LANES)) < COMP, coeffs, 0.0)[:, 0:16]
    sky = jnp.dot(coeffs, model_ref[...], precision=highest, preferred_element_type=f32)
    for j in range(SUB):
        sky_s[pl.ds(j, EXPOS, stride=SUB), :] = sky[:, j * LANES : (j + 1) * LANES]
    total = jnp.zeros((SUB, LANES), f32)
    copies = []
    for e in range(EXPOS):
        at = slice(e * SUB, (e + 1) * SUB)
        left = flux_ref[at, :] - sky_s[at, :]
        left_s[at, :] = left
        total = total + left
        out_s[e, 0:SUB, :] = left[:, 0:FC]
        out_s[e, SUB:CHUNK, :] = pltpu.roll(left, HALF, 1)[:, 0:FC]
        if e % PIECE == PIECE - 1:
            part = pl.ds(e + 1 - PIECE, PIECE)
            copies.append(pltpu.make_async_copy(out_s.at[part], out_h.at[part], sems.at[e // PIECE]))
            copies[-1].start()
    mean = total * (1.0 / EXPOS)
    spread = jnp.zeros((SUB, LANES), f32)
    for e in range(EXPOS):
        spread = spread + jnp.square(left_s[e * SUB : (e + 1) * SUB, :] - mean)
    noise = jnp.sqrt(spread * (1.0 / EXPOS) + 1e-06)
    noise_s[0:SUB, :] = noise[:, 0:FC]
    noise_s[SUB:CHUNK, :] = pltpu.roll(noise, HALF, 1)[:, 0:FC]
    copies.append(pltpu.make_async_copy(noise_s, noise_h, sems.at[EXPOS // PIECE]))
    copies[-1].start()
    for copy in copies:
        copy.wait()


VMEM = pl.BlockSpec(memory_space=pltpu.VMEM)
HBM = pl.BlockSpec(memory_space=pltpu.HBM)
TILES = jax.ShapeDtypeStruct((EXPOS, SUB, LANES), f32)
EDGES = jax.ShapeDtypeStruct((EDGE, GROUPS), jnp.bfloat16)
PARAMS = pltpu.CompilerParams(vmem_limit_bytes=40 * 1024 * 1024)
BANDS = jax.ShapeDtypeStruct((BAND, SUB, LANES), f32)


def sky_model(*arrays):
    return pl.pallas_call(
        sky_kernel,
        out_shape=(
            TILES,
            EDGES,
            EDGES,
            BANDS,
            jax.ShapeDtypeStruct((32, LANES), f32),
            jax.ShapeDtypeStruct((3, SUB, LANES), jnp.int32),
        ),
        in_specs=[HBM] * 6,
        out_specs=(HBM,) + (VMEM,) * 5,
        scratch_shapes=[
            pltpu.VMEM((BAND, CHUNK, FC), f32),
            pltpu.VMEM((COMP, 528), f32),
            pltpu.VMEM((1, FC), jnp.int32),
            pltpu.VMEM((1, 96), jnp.int32),
            pltpu.VMEM((1, FC), jnp.int32),
            pltpu.VMEM((EXPOS, SUB, LANES), f32),
            pltpu.VMEM((16, 640), f32),
            pltpu.VMEM((SUB, LANES), jnp.int32),
            pltpu.SemaphoreType.DMA((8,)),
        ],
        compiler_params=PARAMS,
        name="sky_model",
    )(*(pltpu.with_memory_space_constraint(v, pltpu.HBM) for v in arrays))


def local_model(bands, turned, table):
    return pl.pallas_call(
        model_kernel,
        out_shape=(
            jax.ShapeDtypeStruct((16, SUB * LANES), f32),
            jax.ShapeDtypeStruct((3, SUB, LANES), jnp.int32),
            jax.ShapeDtypeStruct((LANES, LANES), f32),
            jax.ShapeDtypeStruct((2, LANES, LANES), jnp.bfloat16),
        ),
        in_specs=[VMEM] * 3,
        out_specs=(VMEM,) * 4,
        compiler_params=PARAMS,
        name="local_model",
    )(bands, turned, table)


def extract(pixels, near, psf):
    part = jax.ShapeDtypeStruct((2, FIBBLK * ROWS, LANES), f32)
    return pl.pallas_call(
        extract_kernel,
        out_shape=(part, part),
        in_specs=[VMEM] * 3,
        out_specs=(VMEM, VMEM),
        scratch_shapes=[
            pltpu.VMEM((2 * EDGE + LOCAL, LANES), jnp.bfloat16),
            pltpu.VMEM((2 * EDGE + LOCAL, LANES), jnp.bfloat16),
        ],
        compiler_params=PARAMS,
        name="extract",
    )(pixels, near, psf)


def gram_parts(tables, far, psf, flux, vari, model, copies):
    return pl.pallas_call(
        gram_kernel,
        out_shape=(TILES, jax.ShapeDtypeStruct((copies, SUB, LANES), f32)),
        in_specs=[VMEM] * 8,
        out_specs=(VMEM, VMEM),
        scratch_shapes=[
            pltpu.VMEM((2, TAIL + EDGE, LANES), jnp.bfloat16),
            pltpu.VMEM((2, FIBBLK * ROWS, LANES), f32),
            pltpu.VMEM((2, 2, LANES, LANES), f32),
            pltpu.VMEM((2, 2, LANES, LANES), f32),
            pltpu.VMEM((2, LANES, LANES), f32),
            pltpu.VMEM((2, LANES, LANES), f32),
            pltpu.VMEM((EXPOS * SUB, LANES), f32),
        ],
        compiler_params=PARAMS,
        name="gram",
    )(*tables, far, psf, flux, vari, model)


def solve(parts, flux):
    return pl.pallas_call(
        solve_kernel, out_shape=TILES, in_specs=[VMEM, VMEM], out_specs=VMEM, compiler_params=PARAMS, name="solve"
    )(parts, flux)


def subtract(flux, model):
    return pl.pallas_call(
        subtract_kernel,
        out_shape=(jax.ShapeDtypeStruct((EXPOS, CHUNK, FC), f32), jax.ShapeDtypeStruct((CHUNK, FC), f32)),
        in_specs=[VMEM, VMEM],
        out_specs=(HBM, HBM),
        scratch_shapes=[
            pltpu.VMEM((EXPOS * SUB, LANES), f32),
            pltpu.VMEM((EXPOS * SUB, LANES), f32),
            pltpu.VMEM((EXPOS, CHUNK, FC), f32),
            pltpu.VMEM((CHUNK, FC), f32),
            pltpu.SemaphoreType.DMA((EXPOS // PIECE + 1,)),
        ],
        compiler_params=PARAMS,
        name="subtract",
    )(flux.reshape(EXPOS * SUB, LANES), model)


def shards(pixels, psf_proj, resolution, basis, sky_fibres, fibre_slot, band_shift):
    size = lax.axis_size("ccd")
    rows = pixels.reshape(LOCAL, GROUPS)
    res = resolution.transpose(1, 2, 0)
    sky = sky_fibres.reshape(1, -1)
    slot = fibre_slot.reshape(1, FC)
    shift = band_shift.reshape(1, FC)
    pairs = [[(i, i + 1) for i in range(start, size - 1, 2)] for start in (1, 0)]
    swaps = [[*pair, *((j, i) for i, j in pair)] for pair in pairs]
    send, near, far, *prepared = sky_model(res, basis, shift, sky, slot, rows)
    near = lax.ppermute(near, "ccd", swaps[0])
    far = lax.ppermute(far, "ccd", swaps[1])
    model, *tables = local_model(*prepared)
    part, vari = extract(rows, near, psf_proj)
    far, model, tables, part, vari = lax.optimization_barrier((far, model, tables, part, vari))
    sky_tiles = lax.all_to_all(send, "exp", split_axis=0, concat_axis=0, tiled=True)
    flux, parts = gram_parts(tables, far, psf_proj, part, vari, sky_tiles, size)
    parts = lax.all_to_all(parts, "ccd", split_axis=0, concat_axis=0, tiled=True)
    flux = solve(parts, flux)
    flux = lax.all_to_all(flux, "exp", split_axis=0, concat_axis=0, tiled=True)
    sky_subtracted, noise_rms = subtract(flux, model)
    return (sky_subtracted.transpose(0, 2, 1), noise_rms.transpose(1, 0))


def solution(mesh):
    in_specs = (
        P("exp", "ccd", None, None),
        P("ccd", None, None),
        P("ccd", None, "exp"),
        P(),
        P(),
        P("ccd"),
        P("ccd"),
    )
    out_specs = (P(None, "ccd", "exp"), P("ccd", "exp"))
    return jax.shard_map(shards, mesh=mesh, in_specs=in_specs, out_specs=out_specs, check_vma=False)
```
